256 devices in a mesh: seq: 128 (over y, x_lo, z, core), tp: 2 (over x_hi).
Axes of the slice: x: 4 (x_hi: 2, x_lo: 2; x = x_hi * 2 + x_lo), y: 4, z: 8, core: 2. Of those that a mesh axis runs over, the one named last changes fastest.
Arguments:
- series: bfloat16 [32768, 2048], P(('seq', 'tp')), may hold values from -4 to 4
- norm_gain: float32 [2048], replicated, may hold values from 0.1 to 1.9
- w_query: bfloat16 [2048, 1024], P(None, 'tp'), may hold values from -0.5 to 0.5
- w_key: bfloat16 [2048, 1024], P(None, 'tp'), may hold values from -0.5 to 0.5
- w_value: bfloat16 [2048, 1024], P(None, 'tp'), may hold values from -0.125 to 0.125
- w_out: bfloat16 [1024, 2048], P('tp'), may hold values from -0.1875 to 0.1875
- out_grad: bfloat16 [32768, 2048], P(('seq', 'tp')), may hold values from -6 to 6
Outputs:
- layer_out: bfloat16 [32768, 2048], P(('seq', 'tp'))
- series_grad: bfloat16 [32768, 2048], P(('seq', 'tp'))
The draws below stay inside these ranges and needn't reach their ends.
All inputs are finite; a program needn't handle non-finite values.
Results may differ from the reference program's by a relative error of at most 0.019.
Values may be sent and summed in bfloat16 or wider, within the bound.
No kernel may reach another device: no remote copies, remote signals or barrier semaphores. Data moves between devices by JAX's collectives and lax.ppermute only.
A program may use at most 128 MiB of HBM per device.

```python
import math
import jax
import jax.numpy as jnp
from jax import lax

D = 2048
HEADS = 8
HD = 128
BLOCK = 64
TOKENS = 32768


def projection_pair(key):
    base = jax.random.fold_in(key, 4101)
    first = jax.random.normal(jax.random.fold_in(base, 1), (D, HEADS * HD), jnp.float32) * D ** (-0.5)
    second = jax.random.normal(jax.random.fold_in(base, 2), (D, HEADS * HD), jnp.float32) * D ** (-0.5)
    return (first, second)


def draw_w_query(key, part):
    first, second = projection_pair(key)
    first = 1.5 * first
    return jnp.clip(first, -0.5, 0.5).astype(jnp.bfloat16)


def draw_w_key(key, part):
    first, second = projection_pair(key)
    second = 1.5 * second
    return jnp.clip(second, -0.5, 0.5).astype(jnp.bfloat16)


def draw_series(key, part):
    noise = jax.random.normal(jax.random.fold_in(key, 11), (TOKENS, D), jnp.float32)
    level = jnp.exp(jax.random.uniform(jax.random.fold_in(key, 13), (TOKENS, 1), jnp.float32, math.log(0.1), math.log(0.4)))
    return jnp.clip(noise * level, -4.0, 4.0).astype(jnp.bfloat16)


def level_of(own_key, extent, shards, smallest, high):
    factor_of = 1.0
    for axis_at, shards_of in shards:
        heights = jax.random.uniform(jax.random.fold_in(jax.random.fold_in(own_key, 6), axis_at), (shards_of,), jnp.float32, smallest / len(shards), high / len(shards))
        factor_of = factor_of * jnp.repeat(jnp.exp(heights), extent[axis_at] // shards_of).reshape((-1,) + (1,) * (len(extent) - 1 - axis_at))
    return factor_of


def normal_values(own_key, extent, deviation, limit, split=(), kind=jnp.bfloat16):
    drawn = deviation * jax.random.normal(own_key, extent, jnp.float32)
    if split:
        drawn = drawn * level_of(own_key, extent, split, -0.22, 0.18)
    return jnp.clip(drawn, -limit, limit).astype(kind)


def setup_inputs(seed: int = 0) -> dict:
    key_of = jax.random.split(jax.random.key(seed), 8)
    series = draw_series(jax.random.fold_in(key_of[7], 71), 0)
    norm_gain = jnp.clip(1.0 + 0.18 * jax.random.normal(key_of[1], (D,), jnp.float32), 0.1, 1.9)
    w_query = draw_w_query(jax.random.fold_in(key_of[7], 71), 0)
    w_key = draw_w_key(jax.random.fold_in(key_of[7], 71), 0)
    w_value = normal_values(key_of[4], (D, HEADS * HD), D ** -0.5, 0.125, ((1, 2),))
    w_out = normal_values(key_of[5], (HEADS * HD, D), (HEADS * HD) ** -0.5, 0.1875, ((0, 2),))
    out_grad = normal_values(key_of[6], (TOKENS, D), 1.0, 6.0, ((0, 256),))
    return dict(series=series, norm_gain=norm_gain, w_query=w_query, w_key=w_key, w_value=w_value, w_out=w_out, out_grad=out_grad)


NEG = -1e+30
EPS = 1e-06

def reference(series, norm_gain, w_query, w_key, w_value, w_out, out_grad):
    series_f = series.astype(jnp.float32)
    inv_rms = lax.rsqrt(lax.optimization_barrier(jnp.mean(series_f * series_f, axis=-1, keepdims=True)) + EPS)
    unit_rows = series_f * inv_rms
    gain_f = norm_gain.astype(jnp.float32)
    normed_rows = (unit_rows * gain_f).astype(jnp.bfloat16)
    query_rows = jnp.dot(normed_rows, w_query, preferred_element_type=jnp.float32).astype(jnp.bfloat16)
    key_rows = jnp.dot(normed_rows, w_key, preferred_element_type=jnp.float32).astype(jnp.bfloat16)
    value_rows = jnp.dot(normed_rows, w_value, preferred_element_type=jnp.float32).astype(jnp.bfloat16)
    block_count = TOKENS // BLOCK
    factor = HD ** (-0.5)
    distances = [2 ** section for section in range(block_count.bit_length() - 1)]
    query_blocks = query_rows.reshape(block_count, BLOCK, HEADS, HD)
    key_blocks = key_rows.reshape(block_count, BLOCK, HEADS, HD)
    value_blocks = value_rows.reshape(block_count, BLOCK, HEADS, HD)
    causal = lax.broadcasted_iota(jnp.int32, (BLOCK, BLOCK), 0) >= lax.broadcasted_iota(jnp.int32, (BLOCK, BLOCK), 1)

    def gather_earlier(table, index):
        parts = [table[index]] + [table[jnp.maximum(index - distance, 0)] for distance in distances]
        return jnp.concatenate(parts, axis=0).astype(jnp.float32)

    def earlier_mask(index):
        parts = [causal] + [jnp.broadcast_to(index - distance >= 0, (BLOCK, BLOCK)) for distance in distances]
        return jnp.concatenate(parts, axis=1)

    def block_scores(index):
        keys = gather_earlier(key_blocks, index)
        values = gather_earlier(value_blocks, index)
        scores = jnp.einsum('qhe,khe->hqk', query_blocks[index].astype(jnp.float32), keys) * factor
        scores = jnp.where(earlier_mask(index)[None], scores, NEG)
        return (keys, values, scores)

    def forward_block(index):
        keys, values, scores = block_scores(index)
        peak_score = lax.optimization_barrier(jnp.max(scores, axis=-1, keepdims=True))
        log_total = peak_score + jnp.log(lax.optimization_barrier(jnp.sum(jnp.exp(scores - peak_score), axis=-1, keepdims=True)))
        attn_prob = jnp.exp(scores - log_total)
        attn_weight = attn_prob.astype(jnp.bfloat16)
        mixed = jnp.einsum('hqk,khe->qhe', attn_weight.astype(jnp.float32), values).astype(jnp.bfloat16)
        return (mixed, log_total[..., 0])
    mixed, log_total = lax.map(forward_block, jnp.arange(block_count, dtype=jnp.int32))
    mixed_rows = mixed.reshape(TOKENS, HEADS * HD)
    attn_rows = jnp.dot(mixed_rows, w_out, preferred_element_type=jnp.float32)
    layer_out = (series_f + attn_rows).astype(jnp.bfloat16)
    grad_mixed = jnp.dot(out_grad, w_out.T, preferred_element_type=jnp.float32).astype(jnp.bfloat16)
    grad_blocks = grad_mixed.reshape(block_count, BLOCK, HEADS, HD)
    row_inner = lax.optimization_barrier(jnp.sum(grad_blocks.astype(jnp.float32) * mixed.astype(jnp.float32), axis=-1))
    row_inner = jnp.transpose(row_inner, (0, 2, 1))

    def query_grad(index):
        keys, values, scores = block_scores(index)
        attn_prob = jnp.exp(scores - log_total[index][..., None])
        grad_probs = jnp.einsum('qhe,khe->hqk', grad_blocks[index].astype(jnp.float32), values)
        grad_scores = (attn_prob * (grad_probs - row_inner[index][..., None])).astype(jnp.bfloat16)
        return (jnp.einsum('hqk,khe->qhe', grad_scores.astype(jnp.float32), keys) * factor).astype(jnp.bfloat16)

    def gather_later(table, index, axis):
        parts = [table[index]] + [table[jnp.minimum(index + distance, block_count - 1)] for distance in distances]
        return jnp.concatenate(parts, axis=axis)

    def key_grad(index):
        queries = gather_later(query_blocks, index, 0).astype(jnp.float32)
        grads = gather_later(grad_blocks, index, 0).astype(jnp.float32)
        totals = gather_later(log_total, index, 1)
        inners = gather_later(row_inner, index, 1)
        parts = [causal] + [jnp.broadcast_to(index + distance < block_count, (BLOCK, BLOCK)) for distance in distances]
        later_mask = jnp.concatenate(parts, axis=0)
        keys = key_blocks[index].astype(jnp.float32)
        values = value_blocks[index].astype(jnp.float32)
        scores = jnp.einsum('qhe,khe->hqk', queries, keys) * factor
        scores = jnp.where(later_mask[None], scores, NEG)
        attn_prob = jnp.exp(scores - totals[..., None])
        grad_probs = jnp.einsum('qhe,khe->hqk', grads, values)
        grad_scores = (attn_prob * (grad_probs - inners[..., None])).astype(jnp.bfloat16)
        grad_keys = (jnp.einsum('hqk,qhe->khe', grad_scores.astype(jnp.float32), queries) * factor).astype(jnp.bfloat16)
        attn_weight = attn_prob.astype(jnp.bfloat16).astype(jnp.float32)
        grad_values = jnp.einsum('hqk,qhe->khe', attn_weight, grads).astype(jnp.bfloat16)
        return (grad_keys, grad_values)
    all_blocks = jnp.arange(block_count, dtype=jnp.int32)
    grad_query = lax.map(query_grad, all_blocks).reshape(TOKENS, HEADS * HD)
    grad_keys, grad_values = lax.map(key_grad, all_blocks)
    grad_keys = grad_keys.reshape(TOKENS, HEADS * HD)
    grad_values = grad_values.reshape(TOKENS, HEADS * HD)
    grad_normed = jnp.dot(grad_query, w_query.T, preferred_element_type=jnp.float32)
    grad_normed = grad_normed + jnp.dot(grad_keys, w_key.T, preferred_element_type=jnp.float32)
    grad_normed = grad_normed + jnp.dot(grad_values, w_value.T, preferred_element_type=jnp.float32)
    scaled = grad_normed * gain_f
    series_grad = out_grad.astype(jnp.float32) + inv_rms * (scaled - unit_rows * lax.optimization_barrier(jnp.mean(scaled * unit_rows, axis=-1, keepdims=True)))
    return (layer_out, series_grad.astype(jnp.bfloat16))
```

```python
import functools

import jax
import jax.numpy as jnp
from jax import lax
from jax.experimental import pallas as pl
from jax.experimental.pallas import tpu as pltpu
from jax.sharding import PartitionSpec as P

HD = 128
BLOCK = 64
NEG = -1e30
EPS = 1e-06
F32 = jnp.float32
BF16 = jnp.bfloat16


def shifted(value, by):
    size = lax.axis_size("seq")
    pairs = [(i, i + by) for i in range(size) if 0 <= i + by < size]
    return lax.ppermute(value, "seq", pairs)


def swap_tp(value):
    return lax.ppermute(value, "tp", [(0, 1), (1, 0)])


def attn_kernel(n_far, groups, tp_ref, bias_ref, *refs):
    refs = list(refs)
    q_refs = [refs.pop(0) for _ in range(2)]
    g_refs = [refs.pop(0) for _ in range(2)]
    kv_refs = [refs.pop(0) for _ in range(2)]
    fetched = [[refs.pop(0) for _ in range(n)] for n in groups]
    mixed_ref, dq_ref, own_ref, near_ref = [refs.pop(0) for _ in range(4)]
    far_refs = [refs.pop(0) for _ in range(n_far)]
    ext, acc = refs
    turn = 2 * tp_ref[0]
    factor = HD ** (-0.5)

    def piece(pieces, which, slot):
        per = 4 // len(pieces)
        return pieces[slot // per][which, (slot % per) * BLOCK : (slot % per + 1) * BLOCK, :]

    blocks = [(slot + turn) % 4 for slot in range(4)]
    for slot in range(4):
        for which in range(2):
            ext[which, blocks[slot]] = piece(fetched[0], which, slot)
            ext[which, 4 + blocks[slot]] = piece(kv_refs, which, slot)
    acc[...] = jnp.zeros_like(acc)
    causal = lax.broadcasted_iota(jnp.int32, (BLOCK, BLOCK), 0) >= lax.broadcasted_iota(
        jnp.int32, (BLOCK, BLOCK), 1
    )
    causal_bias = jnp.where(causal, 0.0, NEG).astype(F32)
    nn = (((1,), (0,)), ((), ()))
    nt = (((1,), (1,)), ((), ()))
    tn = (((0,), (0,)), ((), ()))

    def dot(a, b, dims):
        return lax.dot_general(a, b, dims, preferred_element_type=F32)

    for slot in range(4):
        half, rows = slot // 2, slice((slot % 2) * BLOCK, (slot % 2 + 1) * BLOCK)
        out_rows = slice(slot * BLOCK, (slot + 1) * BLOCK)
        base = 4 + blocks[slot]
        keys, values = [
            jnp.concatenate(
                [piece(kv_refs, which, slot)]
                + [ext[which, base - d] for d in (1, 2, 4)]
                + [piece(fetched[s], which, slot) for s in range(1, n_far + 1)],
                axis=0,
            )
            for which in range(2)
        ]
        query = q_refs[half][rows, :]
        grad = g_refs[half][rows, :]
        score = dot(query, keys, nt) * factor + bias_ref[slot]
        score = jnp.concatenate([score[:, :BLOCK] + causal_bias, score[:, BLOCK:]], axis=1)
        peak = jnp.max(score, axis=-1, keepdims=True)
        weight = jnp.exp(score - peak)
        total = jnp.sum(weight, axis=-1, keepdims=True)
        prob = weight * (1.0 / total)
        prob_b = prob.astype(BF16)
        mixed = dot(prob_b, values, nn).astype(BF16)
        mixed_ref[out_rows, :] = mixed
        inner = jnp.sum(mixed.astype(F32) * grad.astype(F32), axis=-1, keepdims=True)
        grad_prob = dot(grad, values, nt)
        grad_score = (prob * (grad_prob - inner)).astype(BF16)
        dq_ref[out_rows, :] = (dot(grad_score, keys, nn) * factor).astype(BF16)
        grads = [dot(grad_score, query, tn) * factor, dot(prob_b, grad, tn)]
        for which in range(2):
            for at, d in enumerate((0, 1, 2, 4)):
                acc[which, base - d] += grads[which][at * BLOCK : (at + 1) * BLOCK]
            for s in range(n_far):
                far_refs[s][which, out_rows, :] = grads[which][
                    (4 + s) * BLOCK : (5 + s) * BLOCK
                ].astype(BF16)
    for slot in range(4):
        out_rows = slice(slot * BLOCK, (slot + 1) * BLOCK)
        for which in range(2):
            own_ref[which, out_rows, :] = acc[which, 4 + blocks[slot]]
            near_ref[which, out_rows, :] = acc[which, blocks[slot]].astype(BF16)


def attention(turn, bias, queries, grads, key_values, fetched):
    width = queries[0].shape[1]
    heads = width // HD
    n_far = len(fetched) - 1
    groups = tuple(len(f) for f in fetched)
    rows = 2 * queries[0].shape[0]
    flat = [a for f in fetched for a in f]

    def spec(a):
        if a.ndim == 2:
            return pl.BlockSpec((a.shape[0], HD), lambda h, t: (0, h))
        return pl.BlockSpec((a.shape[0], a.shape[1], HD), lambda h, t: (0, 0, h))

    row_out = jax.ShapeDtypeStruct((rows, width), BF16)
    pair_out = jax.ShapeDtypeStruct((2, rows, width), BF16)
    outs = [row_out, row_out, jax.ShapeDtypeStruct((2, rows, width), F32)] + [pair_out] * (1 + n_far)
    operands = [*queries, *grads, *key_values, *flat]
    return pl.pallas_call(
        functools.partial(attn_kernel, n_far, groups),
        out_shape=outs,
        grid_spec=pltpu.PrefetchScalarGridSpec(
            num_scalar_prefetch=1,
            grid=(heads,),
            in_specs=[pl.BlockSpec(bias.shape, lambda h, t: (0, 0, 0))] + [spec(a) for a in operands],
            out_specs=[spec(a) for a in outs],
            scratch_shapes=[
                pltpu.VMEM((2, 8, BLOCK, HD), BF16),
                pltpu.VMEM((2, 8, BLOCK, HD), F32),
            ],
        ),
        compiler_params=pltpu.CompilerParams(vmem_limit_bytes=32 * 2**20),
        cost_estimate=pl.CostEstimate(
            flops=6 * 2 * rows * bias.shape[2] * width,
            bytes_accessed=10 * 2**20,
            transcendentals=rows * bias.shape[2] * heads,
        ),
        name="attention",
    )(turn, bias, *operands)


def matmul(a, b):
    return jnp.dot(a, b, preferred_element_type=F32)


def matmul_t(a, b):
    return lax.dot_general(a, b, (((1,), (1,)), ((), ())), preferred_element_type=F32)


def per_device(series, norm_gain, w_query, w_key, w_value, w_out, out_grad):
    levels = lax.axis_size("seq").bit_length() - 1
    half = series.shape[0]
    blocks = 2 * half // BLOCK
    tp_index = lax.axis_index("tp")
    slots = jnp.arange(blocks, dtype=jnp.int32)
    global_block = lax.axis_index("seq") * blocks + (slots + 2 * tp_index) % blocks
    distances = [1, 2, 4] + [blocks * 2**s for s in range(1, levels)]
    reach = jnp.repeat(jnp.array([0] + distances, jnp.int32), BLOCK)
    bias = jnp.where(global_block[:, None] >= reach[None], 0.0, NEG).astype(F32)[:, None, :]

    series_f = series.astype(F32)
    inv_rms = lax.rsqrt(jnp.mean(series_f * series_f, axis=-1, keepdims=True) + EPS)
    unit_rows = series_f * inv_rms
    normed = (unit_rows * norm_gain).astype(BF16)
    normed_other = swap_tp(normed)
    out_grad_other = swap_tp(out_grad)

    def project(rows):
        query = matmul(rows, w_query).astype(BF16)
        pair = jnp.stack([matmul(rows, w_key).astype(BF16), matmul(rows, w_value).astype(BF16)])
        return query, pair

    query_own, kv_own = project(normed)
    early = (3, 2, 1)
    first = {s: shifted(kv_own, 2**s) for s in early}
    query_other, kv_other = project(normed_other)
    second = {s: shifted(kv_other, 2**s) for s in early}
    kv_all = jnp.concatenate([kv_own, kv_other], axis=1)
    fetched = [
        (first[s], second[s]) if s in early else (shifted(kv_all, 2**s),) for s in range(levels)
    ]
    grad_own = matmul_t(out_grad, w_out).astype(BF16)
    grad_other = matmul_t(out_grad_other, w_out).astype(BF16)
    mixed, grad_query, own_grads, *returns = attention(
        tp_index.astype(jnp.int32)[None],
        bias,
        (query_own, query_other),
        (grad_own, grad_other),
        (kv_own, kv_other),
        fetched,
    )
    returned = [shifted(returns[s], -(2**s)) for s in range(levels)]
    attn_other = swap_tp(matmul(mixed[half:], w_out).astype(BF16))
    attn_rows = matmul(mixed[:half], w_out) + attn_other.astype(F32)
    layer_out = (series_f + attn_rows).astype(BF16)

    for part in returned:
        own_grads = own_grads + part.astype(F32)
    grad_kv = own_grads.astype(BF16)

    def back(rows):
        return (
            matmul_t(grad_query[rows], w_query)
            + matmul_t(grad_kv[0, rows], w_key)
            + matmul_t(grad_kv[1, rows], w_value)
        )

    normed_grad_other = swap_tp(back(slice(half, None)).astype(BF16))
    normed_grad = back(slice(0, half)) + normed_grad_other.astype(F32)
    scaled = normed_grad * norm_gain
    series_grad = out_grad.astype(F32) + inv_rms * (
        scaled - unit_rows * jnp.mean(scaled * unit_rows, axis=-1, keepdims=True)
    )
    return (layer_out, series_grad.astype(BF16))


def solution(mesh):
    rows = P(("seq", "tp"), None)
    columns = P(None, "tp")
    in_specs = (rows, P(), columns, columns, columns, P("tp", None), rows)
    return jax.shard_map(
        per_device, mesh=mesh, in_specs=in_specs, out_specs=(rows, rows), check_vma=False
    )
```

```python
import functools

import jax
import jax.numpy as jnp
from jax import lax
from jax.experimental import pallas as pl
from jax.experimental.pallas import tpu as pltpu
from jax.sharding import PartitionSpec as P

HD = 128
BLOCK = 64
NEG = -1e30
EPS = 1e-06
F32 = jnp.float32
BF16 = jnp.bfloat16
NN = (((1,), (0,)), ((), ()))
NT = (((1,), (1,)), ((), ()))


def shifted(value, by):
    size = lax.axis_size("seq")
    pairs = [(i, i + by) for i in range(size) if 0 <= i + by < size]
    return lax.ppermute(value, "seq", pairs)


def swap_tp(value):
    return lax.ppermute(value, "tp", [(0, 1), (1, 0)])


def dot(a, b, dims):
    return lax.dot_general(a, b, dims, preferred_element_type=F32)


def piece(pieces, which, slot):
    per = 4 // len(pieces)
    at = (slot % per) * BLOCK
    return pieces[slot // per][which, at : at + BLOCK, :]


def near_slots(step, slot):
    found = []
    for turn in (0, 2):
        block = (slot + turn) % 4 + step
        found.append((0 <= block < 4, (block + turn) % 4))
    return found


def near(is_second, own, other, which, slot, step):
    options = [
        piece(own if here else other, which, at) for here, at in near_slots(step, slot)
    ]
    return jnp.where(is_second, options[1], options[0])


def causal_bias(query_axis):
    rows = lax.broadcasted_iota(jnp.int32, (BLOCK, BLOCK), query_axis)
    keys = lax.broadcasted_iota(jnp.int32, (BLOCK, BLOCK), 1 - query_axis)
    return jnp.where(rows >= keys, 0.0, NEG).astype(F32)


def query_kernel(groups, tp_ref, bias_ref, *refs):
    refs = list(refs)
    qg = [refs.pop(0) for _ in range(2)]
    kv = [refs.pop(0) for _ in range(2)]
    fetched = [[refs.pop(0) for _ in range(n)] for n in groups]
    mixed_ref, dq_ref, stat_ref = refs
    is_second = tp_ref[0] == 1
    factor = HD ** (-0.5)
    causal = causal_bias(0)
    lane = lax.broadcasted_iota(jnp.int32, (BLOCK, HD), 1)
    for slot in range(4):
        out = slice(slot * BLOCK, (slot + 1) * BLOCK)
        keys, values = [
            jnp.concatenate(
                [piece(kv, which, slot)]
                + [near(is_second, kv, fetched[0], which, slot, -d) for d in (1, 2, 4)]
                + [piece(f, which, slot) for f in fetched[1:]],
                axis=0,
            )
            for which in range(2)
        ]
        query, grad = piece(qg, 0, slot), piece(qg, 1, slot)
        score = dot(query, keys, NT) * factor + bias_ref[slot]
        score = jnp.concatenate([score[:, :BLOCK] + causal, score[:, BLOCK:]], axis=1)
        peak = jnp.max(score, axis=-1, keepdims=True)
        weight = jnp.exp(score - peak)
        total = jnp.sum(weight, axis=-1, keepdims=True)
        prob = weight * (1.0 / total)
        mixed = dot(prob.astype(BF16), values, NN).astype(BF16)
        mixed_ref[out, :] = mixed
        inner = jnp.sum(mixed.astype(F32) * grad.astype(F32), axis=-1, keepdims=True)
        grad_score = (prob * (dot(grad, values, NT) - inner)).astype(BF16)
        dq_ref[out, :] = (dot(grad_score, keys, NN) * factor).astype(BF16)
        stat = jnp.where(lane == 0, peak + jnp.log(total), inner)
        stat_ref[0, :, out] = jnp.transpose(stat)[:2]


def key_kernel(half, groups, tp_ref, *refs):
    refs = list(refs)
    kv = refs.pop(0)
    qg = [refs.pop(0) for _ in range(2)]
    stat = refs.pop(0)
    later = [[refs.pop(0) for _ in range(n)] for n in groups]
    later_stats = [refs.pop(0) for _ in groups]
    (out_ref,) = refs
    is_second = tp_ref[0] == 1
    factor = HD ** (-0.5)
    causal = causal_bias(1)

    def stat_of(ref, slot):
        return ref[0, :, slot * BLOCK : (slot + 1) * BLOCK]

    for at in range(2):
        slot = 2 * half + at
        rows = slice(at * BLOCK, (at + 1) * BLOCK)
        queries, grads = [
            jnp.concatenate(
                [piece(qg, which, slot)]
                + [near(is_second, qg, later[0], which, slot, d) for d in (1, 2, 4)]
                + [f[0][which, rows, :] for f in later[1:]],
                axis=0,
            )
            for which in range(2)
        ]
        near_stats = []
        for d in (1, 2, 4):
            options = [
                stat_of(stat if here else later_stats[0], s) for here, s in near_slots(d, slot)
            ]
            near_stats.append(jnp.where(is_second, options[1], options[0]))
        stats = jnp.concatenate(
            [stat_of(stat, slot)] + near_stats + [stat_of(f, slot) for f in later_stats[1:]], axis=1
        )
        score = dot(kv[0, rows, :], queries, NT) * factor
        score = jnp.concatenate([score[:, :BLOCK] + causal, score[:, BLOCK:]], axis=1)
        prob = jnp.exp(score - stats[0:1])
        grad_score = (prob * (dot(kv[1, rows, :], grads, NT) - stats[1:2])).astype(BF16)
        out_ref[0, rows, :] = (dot(grad_score, queries, NN) * factor).astype(BF16)
        out_ref[1, rows, :] = dot(prob.astype(BF16), grads, NN).astype(BF16)


def head_spec(a):
    if a.ndim == 2:
        return pl.BlockSpec((a.shape[0], HD), lambda h, t: (0, h))
    return pl.BlockSpec((a.shape[0], a.shape[1], HD), lambda h, t: (0, 0, h))


def stat_spec(a):
    return pl.BlockSpec((1,) + a.shape[1:], lambda h, t: (h, 0, 0))


def call(kernel, turn, operands, in_specs, outs, out_specs, heads, keys, name):
    rows = outs[0].shape[-2]
    return pl.pallas_call(
        kernel,
        out_shape=outs,
        grid_spec=pltpu.PrefetchScalarGridSpec(
            num_scalar_prefetch=1, grid=(heads,), in_specs=in_specs, out_specs=out_specs
        ),
        compiler_params=pltpu.CompilerParams(vmem_limit_bytes=12 * 2**20),
        cost_estimate=pl.CostEstimate(
            flops=4 * 2 * rows * keys * HD * heads,
            bytes_accessed=6 * 2**20,
            transcendentals=rows * keys * heads,
        ),
        name=name,
    )(turn, *operands)


def query_side(turn, bias, qg, kv, fetched):
    rows, width = 2 * qg[0].shape[1], qg[0].shape[2]
    heads = width // HD
    operands = [*qg, *kv, *[a for f in fetched for a in f]]
    row_out = jax.ShapeDtypeStruct((rows, width), BF16)
    stat_out = jax.ShapeDtypeStruct((heads, 2, rows), F32)
    return call(
        functools.partial(query_kernel, tuple(len(f) for f in fetched)),
        turn,
        [bias, *operands],
        [pl.BlockSpec(bias.shape, lambda h, t: (0, 0, 0))] + [head_spec(a) for a in operands],
        [row_out, row_out, stat_out],
        [head_spec(row_out), head_spec(row_out), stat_spec(stat_out)],
        heads,
        bias.shape[2],
        "query_side",
    )


def key_side(half, turn, kv, qg, stat, later, later_stats):
    rows, width = kv[0].shape[1], kv[0].shape[2]
    heads = width // HD

    def half_spec(f):
        if len(f) == 2:
            return f[half], head_spec(f[half])
        return f[0], pl.BlockSpec((2, rows, HD), lambda h, t: (0, half, h))

    far = [half_spec(f) for f in later[1:]]
    operands = [kv[half], *qg, stat, *later[0], *[a for a, _ in far], *later_stats]
    in_specs = (
        [head_spec(a) for a in (kv[half], *qg)]
        + [stat_spec(stat)]
        + [head_spec(a) for a in later[0]]
        + [s for _, s in far]
        + [stat_spec(a) for a in later_stats]
    )
    out = jax.ShapeDtypeStruct((2, rows, width), BF16)
    groups = (len(later[0]),) + (1,) * len(far)
    (result,) = call(
        functools.partial(key_kernel, half, groups),
        turn,
        operands,
        in_specs,
        [out],
        [head_spec(out)],
        heads,
        (4 + len(far)) * BLOCK,
        "key_side",
    )
    return result


def matmul(a, b):
    return jnp.dot(a, b, preferred_element_type=F32)


def matmul_t(a, b):
    return lax.dot_general(a, b, NT, preferred_element_type=F32)


def exchange(own, other, sign, levels):
    whole = jnp.concatenate([own, other], axis=1)
    got = {}
    for at, rows in enumerate((own, other)):
        last, reached = rows, 0
        for s in (1, 2, 3):
            last = shifted(last, sign * (2**s - reached))
            reached = 2**s
            got[s, at] = last
    return [
        (got[s, 0], got[s, 1]) if s in (1, 2, 3) else (shifted(whole, sign * 2**s),)
        for s in range(levels)
    ]


def per_device(series, norm_gain, w_query, w_key, w_value, w_out, out_grad):
    levels = lax.axis_size("seq").bit_length() - 1
    half = series.shape[0]
    blocks = 2 * half // BLOCK
    tp_index = lax.axis_index("tp").astype(jnp.int32)
    turn = tp_index[None]
    slots = jnp.arange(blocks, dtype=jnp.int32)
    global_block = lax.axis_index("seq") * blocks + (slots + 2 * tp_index) % blocks
    distances = [1, 2, 4] + [blocks * 2**s for s in range(1, levels)]
    reach = jnp.repeat(jnp.array([0] + distances, jnp.int32), BLOCK)
    bias = jnp.where(global_block[:, None] >= reach[None], 0.0, NEG).astype(F32)[:, None, :]

    series_f = series.astype(F32)
    inv_rms = lax.rsqrt(jnp.mean(series_f * series_f, axis=-1, keepdims=True) + EPS)
    unit_rows = series_f * inv_rms
    normed = (unit_rows * norm_gain).astype(BF16)
    normed_other = swap_tp(normed)
    out_grad_other = swap_tp(out_grad)

    def key_value(rows):
        return jnp.stack([matmul(rows, w_key).astype(BF16), matmul(rows, w_value).astype(BF16)])

    def query_grad(rows, grad_rows):
        return jnp.stack(
            [matmul(rows, w_query).astype(BF16), matmul_t(grad_rows, w_out).astype(BF16)]
        )

    kv = (key_value(normed), key_value(normed_other))
    qg = (query_grad(normed, out_grad), query_grad(normed_other, out_grad_other))
    fetched = exchange(*kv, 1, levels)
    later = exchange(*qg, -1, levels)
    mixed, grad_query, stat = query_side(turn, bias, qg, kv, fetched)
    stat, later = lax.optimization_barrier((stat, later))
    later_stats = [shifted(stat, -(2**s)) for s in range(levels)]
    attn_other = swap_tp(matmul(mixed[half:], w_out).astype(BF16))
    attn_rows = matmul(mixed[:half], w_out) + attn_other.astype(F32)
    layer_out = (series_f + attn_rows).astype(BF16)

    def back(at):
        grad_kv = key_side(at, turn, kv, qg, stat, later, later_stats)
        rows = slice(at * half, (at + 1) * half)
        return (
            matmul_t(grad_query[rows], w_query)
            + matmul_t(grad_kv[0], w_key)
            + matmul_t(grad_kv[1], w_value)
        )

    normed_grad_other = swap_tp(back(1).astype(BF16))
    normed_grad = back(0) + normed_grad_other.astype(F32)
    scaled = normed_grad * norm_gain
    series_grad = out_grad.astype(F32) + inv_rms * (
        scaled - unit_rows * jnp.mean(scaled * unit_rows, axis=-1, keepdims=True)
    )
    return (layer_out, series_grad.astype(BF16))


def solution(mesh):
    rows = P(("seq", "tp"), None)
    columns = P(None, "tp")
    in_specs = (rows, P(), columns, columns, columns, P("tp", None), rows)
    return jax.shard_map(
        per_device, mesh=mesh, in_specs=in_specs, out_specs=(rows, rows), check_vma=False
    )
```

```python
import functools

import jax
import jax.numpy as jnp
from jax import lax
from jax.experimental import pallas as pl
from jax.experimental.pallas import tpu as pltpu
from jax.sharding import PartitionSpec as P

HD = 128
BLOCK = 64
NEG = -1e30
EPS = 1e-06
F32 = jnp.float32
BF16 = jnp.bfloat16
NN = (((1,), (0,)), ((), ()))
NT = (((1,), (1,)), ((), ()))
TN = (((0,), (0,)), ((), ()))
NEAR = (1, 2, 4)


def shifted(value, by):
    size = lax.axis_size("seq")
    pairs = [(i, i + by) for i in range(size) if 0 <= i + by < size]
    return lax.ppermute(value, "seq", pairs)


def swap_tp(value):
    return lax.ppermute(value, "tp", [(0, 1), (1, 0)])


def dot(a, b, dims):
    return lax.dot_general(a, b, dims, preferred_element_type=F32)


def piece(pieces, which, slot):
    per = 4 // len(pieces)
    at = (slot % per) * BLOCK
    return pieces[slot // per][which, at : at + BLOCK, :]


def near_slots(step, slot):
    found = []
    for turn in (0, 2):
        block = (slot + turn) % 4 + step
        found.append((0 <= block < 4, (block + turn) % 4))
    return found


def near(is_second, own, other, which, slot, step):
    options = [
        piece(own if here else other, which, at) for here, at in near_slots(step, slot)
    ]
    return jnp.where(is_second, options[1], options[0])


def causal_bias(query_axis):
    rows = lax.broadcasted_iota(jnp.int32, (BLOCK, BLOCK), query_axis)
    keys = lax.broadcasted_iota(jnp.int32, (BLOCK, BLOCK), 1 - query_axis)
    return jnp.where(rows >= keys, 0.0, NEG).astype(F32)


def query_kernel(groups, where_ref, bias_ref, *refs):
    refs = list(refs)
    qg = [refs.pop(0) for _ in range(2)]
    kv = [refs.pop(0) for _ in range(2)]
    fetched = [[refs.pop(0) for _ in range(n)] for n in groups]
    one = refs.pop(0)
    two = [refs.pop(0) for _ in range(2)]
    mixed_ref, dq_ref, stat_ref, *back_refs = refs
    is_second = where_ref[0] == 1
    factor = HD ** (-0.5)
    causal = causal_bias(0)
    lane = lax.broadcasted_iota(jnp.int32, (BLOCK, HD), 1)
    for slot in range(4):
        out = slice(slot * BLOCK, (slot + 1) * BLOCK)
        keys, values = [
            jnp.concatenate(
                [piece(kv, which, slot)]
                + [near(is_second, kv, fetched[0], which, slot, -d) for d in NEAR]
                + [piece(f, which, slot) for f in fetched[1:]]
                + [one[which, out, :]]
                + [t[0, which, out, :] for t in two],
                axis=0,
            )
            for which in range(2)
        ]
        query, grad = piece(qg, 0, slot), piece(qg, 1, slot)
        score = dot(query, keys, NT) * factor + bias_ref[slot]
        score = jnp.concatenate([score[:, :BLOCK] + causal, score[:, BLOCK:]], axis=1)
        peak = jnp.max(score, axis=-1, keepdims=True)
        weight = jnp.exp(score - peak)
        total = jnp.sum(weight, axis=-1, keepdims=True)
        prob = weight * (1.0 / total)
        prob_b = prob.astype(BF16)
        mixed = dot(prob_b, values, NN).astype(BF16)
        mixed_ref[out, :] = mixed
        inner = jnp.sum(mixed.astype(F32) * grad.astype(F32), axis=-1, keepdims=True)
        grad_score = (prob * (dot(grad, values, NT) - inner)).astype(BF16)
        dq_ref[out, :] = (dot(grad_score, keys, NN) * factor).astype(BF16)
        stat = jnp.where(lane == 0, peak + jnp.log(total), inner)
        stat_ref[0, :, out] = jnp.transpose(stat)[:2]
        first = keys.shape[0] - len(back_refs) * BLOCK
        grad_keys = (dot(grad_score[:, first:], query, TN) * factor).astype(BF16)
        grad_values = dot(prob_b[:, first:], grad, TN).astype(BF16)
        for at, ref in enumerate(back_refs):
            ref[0, out, :] = grad_keys[at * BLOCK : (at + 1) * BLOCK]
            ref[1, out, :] = grad_values[at * BLOCK : (at + 1) * BLOCK]


def key_kernel(half, groups, n_back, where_ref, *refs):
    refs = list(refs)
    kv = refs.pop(0)
    qg = [refs.pop(0) for _ in range(2)]
    stat = refs.pop(0)
    later = [[refs.pop(0) for _ in range(n)] for n in groups]
    later_stats = [refs.pop(0) for _ in groups]
    back = [refs.pop(0) for _ in range(n_back)]
    (out_ref,) = refs
    is_second = where_ref[0] == 1
    factor = HD ** (-0.5)
    causal = causal_bias(1)

    def stat_of(ref, slot):
        return ref[0, :, slot * BLOCK : (slot + 1) * BLOCK]

    for at in range(2):
        slot = 2 * half + at
        rows = slice(at * BLOCK, (at + 1) * BLOCK)
        queries, grads = [
            jnp.concatenate(
                [piece(qg, which, slot)]
                + [near(is_second, qg, later[0], which, slot, d) for d in NEAR]
                + [f[0][which, rows, :] for f in later[1:]],
                axis=0,
            )
            for which in range(2)
        ]
        near_stats = []
        for d in NEAR:
            options = [
                stat_of(stat if here else later_stats[0], s) for here, s in near_slots(d, slot)
            ]
            near_stats.append(jnp.where(is_second, options[1], options[0]))
        stats = jnp.concatenate(
            [stat_of(stat, slot)] + near_stats + [stat_of(f, slot) for f in later_stats[1:]], axis=1
        )
        score = dot(kv[0, rows, :], queries, NT) * factor
        score = jnp.concatenate([score[:, :BLOCK] + causal, score[:, BLOCK:]], axis=1)
        prob = jnp.exp(score - stats[0:1])
        grad_score = (prob * (dot(kv[1, rows, :], grads, NT) - stats[1:2])).astype(BF16)
        totals = [
            dot(grad_score, queries, NN) * factor,
            dot(prob.astype(BF16), grads, NN),
        ]
        for which in range(2):
            for ref in back:
                totals[which] += ref[which, rows, :].astype(F32)
            out_ref[which, rows, :] = totals[which].astype(BF16)


def head_spec(a):
    if a.ndim == 2:
        return pl.BlockSpec((a.shape[0], HD), lambda h, w: (0, h))
    return pl.BlockSpec((a.shape[0], a.shape[1], HD), lambda h, w: (0, 0, h))


def stat_spec(a):
    return pl.BlockSpec((1,) + a.shape[1:], lambda h, w: (h, 0, 0))


def call(kernel, where, operands, in_specs, outs, out_specs, heads, keys, name):
    rows = outs[0].shape[-2]
    return pl.pallas_call(
        kernel,
        out_shape=outs,
        grid_spec=pltpu.PrefetchScalarGridSpec(
            num_scalar_prefetch=1, grid=(heads,), in_specs=in_specs, out_specs=out_specs
        ),
        compiler_params=pltpu.CompilerParams(vmem_limit_bytes=10 * 2**20),
        cost_estimate=pl.CostEstimate(
            flops=4 * 2 * rows * keys * HD * heads,
            bytes_accessed=6 * 2**20,
            transcendentals=rows * keys * heads,
        ),
        name=name,
    )(where, *operands)


def query_side(where, bias, qg, kv, fetched, one, column):
    rows, width = 2 * qg[0].shape[1], qg[0].shape[2]
    heads = width // HD
    far = [a for f in fetched for a in f] + [one, column]
    far = [pltpu.with_memory_space_constraint(a, pltpu.HBM) for a in far]
    column = far.pop()
    operands = [*qg, *kv, *far]
    row_out = jax.ShapeDtypeStruct((rows, width), BF16)
    stat_out = jax.ShapeDtypeStruct((heads, 2, rows), F32)
    back_out = jax.ShapeDtypeStruct((2, rows, width), BF16)

    def column_spec(back):
        return pl.BlockSpec(
            (1, 2, rows, HD), lambda h, w: (jnp.maximum(w[1] - back, 0), 0, 0, h)
        )

    return call(
        functools.partial(query_kernel, tuple(len(f) for f in fetched)),
        where,
        [bias, *operands, column, column],
        [pl.BlockSpec(bias.shape, lambda h, w: (0, 0, 0))]
        + [head_spec(a) for a in operands]
        + [column_spec(1), column_spec(2)],
        [row_out, row_out, stat_out] + [back_out] * 3,
        [head_spec(row_out), head_spec(row_out), stat_spec(stat_out)] + [head_spec(back_out)] * 3,
        heads,
        bias.shape[2],
        "query_side",
    )


def key_side(half, where, kv, qg, stat, later, later_stats, returned):
    rows, width = kv[0].shape[1], kv[0].shape[2]
    heads = width // HD
    half_of_whole = pl.BlockSpec((2, rows, HD), lambda h, w: (0, half, h))
    far = [f[half] for f in later[1:]]
    operands = [kv[half], *qg, stat, *later[0], *far, *later_stats, *returned]
    in_specs = (
        [head_spec(a) for a in (kv[half], *qg)]
        + [stat_spec(stat)]
        + [head_spec(a) for a in (*later[0], *far)]
        + [stat_spec(a) for a in later_stats]
        + [half_of_whole] * len(returned)
    )
    out = jax.ShapeDtypeStruct((2, rows, width), BF16)
    groups = (len(later[0]),) + (1,) * len(far)
    (result,) = call(
        functools.partial(key_kernel, half, groups, len(returned)),
        where,
        operands,
        in_specs,
        [out],
        [head_spec(out)],
        heads,
        (4 + len(far)) * BLOCK,
        "key_side",
    )
    return result


def matmul(a, b):
    return jnp.dot(a, b, preferred_element_type=F32)


def matmul_t(a, b):
    return lax.dot_general(a, b, NT, preferred_element_type=F32)


def relay(two, sign):
    four = shifted(two, sign * 2)
    return two, four, shifted(four, sign * 4)


def per_device(series, norm_gain, w_query, w_key, w_value, w_out, out_grad):
    levels = lax.axis_size("seq").bit_length() - 1
    half = series.shape[0]
    blocks = 2 * half // BLOCK
    tp_index = lax.axis_index("tp").astype(jnp.int32)
    seq_index = lax.axis_index("seq").astype(jnp.int32)
    seq_size = lax.axis_size("seq")
    run = seq_size // 4
    where = jnp.stack([tp_index, seq_index // run])
    slots = jnp.arange(blocks, dtype=jnp.int32)
    global_block = seq_index * blocks + (slots + 2 * tp_index) % blocks
    distances = [1, 2, 4] + [blocks * 2**s for s in range(1, levels)]
    reach = jnp.repeat(jnp.array([0] + distances, jnp.int32), BLOCK)
    bias = jnp.where(global_block[:, None] >= reach[None], 0.0, NEG).astype(F32)[:, None, :]

    series_f = series.astype(F32)
    inv_rms = lax.rsqrt(jnp.mean(series_f * series_f, axis=-1, keepdims=True) + EPS)
    unit_rows = series_f * inv_rms
    normed = (unit_rows * norm_gain).astype(BF16)
    normed_other = swap_tp(normed)
    out_grad_other = swap_tp(out_grad)

    def key_value(rows):
        return jnp.stack([matmul(rows, w_key).astype(BF16), matmul(rows, w_value).astype(BF16)])

    def query_grad(rows, grad_rows):
        return jnp.stack(
            [matmul(rows, w_query).astype(BF16), matmul_t(grad_rows, w_out).astype(BF16)]
        )

    kv_own = key_value(normed)
    qg_own = query_grad(normed, out_grad)
    kv_two, qg_two = shifted(kv_own, 2), shifted(qg_own, -2)
    normed_other, kv_two, qg_two = lax.optimization_barrier((normed_other, kv_two, qg_two))
    kv = (kv_own, key_value(normed_other))
    qg = (qg_own, query_grad(normed_other, out_grad_other))
    kv_all = jnp.concatenate(kv, axis=1)
    column = lax.all_gather(
        kv_all,
        "seq",
        axis_index_groups=[list(range(k, seq_size, run)) for k in range(run)],
    )
    kv_far = [relay(kv_two, 1), relay(shifted(kv[1], 2), 1)]
    qg_far = [relay(qg_two, -1), relay(shifted(qg[1], -2), -1)]
    fetched = [(shifted(kv_all, 1),)] + list(zip(*kv_far))
    later = [(shifted(jnp.concatenate(qg, axis=1), -1),)] + list(zip(*qg_far))
    mixed, grad_query, stat, *backs = query_side(
        where, bias, qg, kv, fetched, shifted(kv_all, 16), column
    )
    stat, backs, later = lax.optimization_barrier((stat, backs, later))
    returned = [shifted(b, -by) for b, by in zip(backs, (16, run, 2 * run))]
    later_stats = [shifted(stat, -by) for by in (1, 2, 4, 8)]
    attn_other = swap_tp(matmul(mixed[half:], w_out).astype(BF16))
    attn_rows = matmul(mixed[:half], w_out) + attn_other.astype(F32)
    layer_out = (series_f + attn_rows).astype(BF16)

    def back(at):
        grad_kv = key_side(at, where, kv, qg, stat, later, later_stats, returned)
        rows = slice(at * half, (at + 1) * half)
        return (
            matmul_t(grad_query[rows], w_query)
            + matmul_t(grad_kv[0], w_key)
            + matmul_t(grad_kv[1], w_value)
        )

    normed_grad_other = swap_tp(back(1).astype(BF16))
    normed_grad = back(0) + normed_grad_other.astype(F32)
    scaled = normed_grad * norm_gain
    series_grad = out_grad.astype(F32) + inv_rms * (
        scaled - unit_rows * jnp.mean(scaled * unit_rows, axis=-1, keepdims=True)
    )
    return (layer_out, series_grad.astype(BF16))


def solution(mesh):
    rows = P(("seq", "tp"), None)
    columns = P(None, "tp")
    in_specs = (rows, P(), columns, columns, columns, P("tp", None), rows)
    return jax.shard_map(
        per_device, mesh=mesh, in_specs=in_specs, out_specs=(rows, rows), check_vma=False
    )
```

```python
import functools

import jax
import jax.numpy as jnp
from jax import lax
from jax.experimental import pallas as pl
from jax.experimental.pallas import tpu as pltpu
from jax.sharding import PartitionSpec as P

HD = 128
BLOCK = 64
NEG = -1e30
EPS = 1e-06
F32 = jnp.float32
BF16 = jnp.bfloat16
NN = (((1,), (0,)), ((), ()))
NT = (((1,), (1,)), ((), ()))
TN = (((0,), (0,)), ((), ()))
NEAR = (1, 2, 4)


def shifted(value, by):
    size = lax.axis_size("seq")
    pairs = [(i, i + by) for i in range(size) if 0 <= i + by < size]
    return lax.ppermute(value, "seq", pairs)


def swap_tp(value):
    return lax.ppermute(value, "tp", [(0, 1), (1, 0)])


def dot(a, b, dims):
    return lax.dot_general(a, b, dims, preferred_element_type=F32)


def piece(pieces, which, slot):
    per = 4 // len(pieces)
    at = (slot % per) * BLOCK
    return pieces[slot // per][which, at : at + BLOCK, :]


def near_slots(step, slot):
    found = []
    for turn in (0, 2):
        block = (slot + turn) % 4 + step
        found.append((0 <= block < 4, (block + turn) % 4))
    return found


def near(is_second, own, other, which, slot, step):
    options = [
        piece(own if here else other, which, at) for here, at in near_slots(step, slot)
    ]
    return jnp.where(is_second, options[1], options[0])


def causal_bias(query_axis):
    rows = lax.broadcasted_iota(jnp.int32, (BLOCK, BLOCK), query_axis)
    keys = lax.broadcasted_iota(jnp.int32, (BLOCK, BLOCK), 1 - query_axis)
    return jnp.where(rows >= keys, 0.0, NEG).astype(F32)


def query_kernel(groups, n_back, where_ref, bias_ref, *refs):
    refs = list(refs)
    qg = [refs.pop(0) for _ in range(2)]
    kv = [refs.pop(0) for _ in range(2)]
    fetched = [[refs.pop(0) for _ in range(n)] for n in groups]
    mixed_ref, dq_ref, stat_ref, *back_refs = refs
    is_second = where_ref[0] == 1
    factor = HD ** (-0.5)
    causal = causal_bias(0)
    lane = lax.broadcasted_iota(jnp.int32, (BLOCK, HD), 1)
    slots = range(4)

    def gather(which, slot):
        return jnp.concatenate(
            [piece(kv, which, slot)]
            + [near(is_second, kv, fetched[0], which, slot, -d) for d in NEAR]
            + [piece(f, which, slot) for f in fetched[1:]],
            axis=0,
        )

    def rows(slot):
        return slice(slot * BLOCK, (slot + 1) * BLOCK)

    query = [piece(qg, 0, slot) for slot in slots]
    grad = [piece(qg, 1, slot) for slot in slots]
    keys = [gather(0, slot) for slot in slots]
    values = [gather(1, slot) for slot in slots]
    score = []
    for slot in slots:
        s = dot(query[slot], keys[slot], NT) * factor + bias_ref[slot]
        score.append(jnp.concatenate([s[:, :BLOCK] + causal, s[:, BLOCK:]], axis=1))
    grad_prob = [dot(grad[slot], values[slot], NT) for slot in slots]
    peak = [jnp.max(s, axis=-1, keepdims=True) for s in score]
    weight = [jnp.exp(score[slot] - peak[slot]) for slot in slots]
    total = [jnp.sum(w, axis=-1, keepdims=True) for w in weight]
    prob = [weight[slot] * (1.0 / total[slot]) for slot in slots]
    prob_b = [p.astype(BF16) for p in prob]
    mixed = [dot(prob_b[slot], values[slot], NN).astype(BF16) for slot in slots]
    inner = [
        jnp.sum(mixed[slot].astype(F32) * grad[slot].astype(F32), axis=-1, keepdims=True)
        for slot in slots
    ]
    grad_score = [
        (prob[slot] * (grad_prob[slot] - inner[slot])).astype(BF16) for slot in slots
    ]
    first = keys[0].shape[0] - n_back * BLOCK
    for slot in slots:
        out = rows(slot)
        mixed_ref[out, :] = mixed[slot]
        dq_ref[out, :] = (dot(grad_score[slot], keys[slot], NN) * factor).astype(BF16)
        stat = jnp.where(lane == 0, peak[slot] + jnp.log(total[slot]), inner[slot])
        stat_ref[0, :, out] = jnp.transpose(stat)[:2]
        if n_back:
            grad_keys = (dot(grad_score[slot][:, first:], query[slot], TN) * factor).astype(BF16)
            grad_values = dot(prob_b[slot][:, first:], grad[slot], TN).astype(BF16)
            for at, ref in enumerate(back_refs):
                ref[0, out, :] = grad_keys[at * BLOCK : (at + 1) * BLOCK]
                ref[1, out, :] = grad_values[at * BLOCK : (at + 1) * BLOCK]


def key_kernel(half, groups, n_back, where_ref, *refs):
    refs = list(refs)
    kv = refs.pop(0)
    qg = [refs.pop(0) for _ in range(2)]
    stat = refs.pop(0)
    later = [[refs.pop(0) for _ in range(n)] for n in groups]
    later_stats = [refs.pop(0) for _ in groups]
    back = [refs.pop(0) for _ in range(n_back)]
    (out_ref,) = refs
    is_second = where_ref[0] == 1
    factor = HD ** (-0.5)
    causal = causal_bias(1)

    def stat_of(ref, slot):
        return ref[0, :, slot * BLOCK : (slot + 1) * BLOCK]

    for at in range(2):
        slot = 2 * half + at
        rows = slice(at * BLOCK, (at + 1) * BLOCK)
        queries, grads = [
            jnp.concatenate(
                [piece(qg, which, slot)]
                + [near(is_second, qg, later[0], which, slot, d) for d in NEAR]
                + [f[0][which, rows, :] for f in later[1:]],
                axis=0,
            )
            for which in range(2)
        ]
        near_stats = []
        for d in NEAR:
            options = [
                stat_of(stat if here else later_stats[0], s) for here, s in near_slots(d, slot)
            ]
            near_stats.append(jnp.where(is_second, options[1], options[0]))
        stats = jnp.concatenate(
            [stat_of(stat, slot)] + near_stats + [stat_of(f, slot) for f in later_stats[1:]], axis=1
        )
        score = dot(kv[0, rows, :], queries, NT) * factor
        score = jnp.concatenate([score[:, :BLOCK] + causal, score[:, BLOCK:]], axis=1)
        prob = jnp.exp(score - stats[0:1])
        grad_score = (prob * (dot(kv[1, rows, :], grads, NT) - stats[1:2])).astype(BF16)
        totals = [
            dot(grad_score, queries, NN) * factor,
            dot(prob.astype(BF16), grads, NN),
        ]
        for which in range(2):
            for ref in back:
                totals[which] += ref[which, rows, :].astype(F32)
            out_ref[which, rows, :] = totals[which].astype(BF16)


def head_spec(a):
    if a.ndim == 2:
        return pl.BlockSpec((a.shape[0], HD), lambda h, w: (0, h))
    return pl.BlockSpec((a.shape[0], a.shape[1], HD), lambda h, w: (0, 0, h))


def stat_spec(a):
    return pl.BlockSpec((1,) + a.shape[1:], lambda h, w: (h, 0, 0))


def call(kernel, where, operands, in_specs, outs, out_specs, heads, keys, name):
    rows = outs[0].shape[-2]
    return pl.pallas_call(
        kernel,
        out_shape=outs,
        grid_spec=pltpu.PrefetchScalarGridSpec(
            num_scalar_prefetch=1, grid=(heads,), in_specs=in_specs, out_specs=out_specs
        ),
        compiler_params=pltpu.CompilerParams(vmem_limit_bytes=10 * 2**20),
        cost_estimate=pl.CostEstimate(
            flops=4 * 2 * rows * keys * HD * heads,
            bytes_accessed=6 * 2**20,
            transcendentals=rows * keys * heads,
        ),
        name=name,
    )(where, *operands)


def query_side(where, bias, qg, kv, fetched, n_back):
    rows, width = 2 * qg[0].shape[1], qg[0].shape[2]
    heads = width // HD
    far = [pltpu.with_memory_space_constraint(a, pltpu.HBM) for f in fetched for a in f]
    operands = [*qg, *kv, *far]
    row_out = jax.ShapeDtypeStruct((rows, width), BF16)
    stat_out = jax.ShapeDtypeStruct((heads, 2, rows), F32)
    back_out = jax.ShapeDtypeStruct((2, rows, width), BF16)
    outs = [row_out, row_out, stat_out] + [back_out] * n_back
    return call(
        functools.partial(query_kernel, tuple(len(f) for f in fetched), n_back),
        where,
        [bias, *operands],
        [pl.BlockSpec(bias.shape, lambda h, w: (0, 0, 0))] + [head_spec(a) for a in operands],
        outs,
        [head_spec(row_out), head_spec(row_out), stat_spec(stat_out)] + [head_spec(back_out)] * n_back,
        heads,
        bias.shape[2],
        "query_side",
    )


def key_side(half, where, kv, qg, stat, later, later_stats, returned):
    rows, width = kv[0].shape[1], kv[0].shape[2]
    heads = width // HD
    half_of_whole = pl.BlockSpec((2, rows, HD), lambda h, w: (0, half, h))
    far = [f[-1] if len(f) == 1 else f[half] for f in later[1:]]
    operands = [kv[half], *qg, stat, *later[0], *far, *later_stats, *returned]
    in_specs = (
        [head_spec(a) for a in (kv[half], *qg)]
        + [stat_spec(stat)]
        + [head_spec(a) for a in later[0]]
        + [half_of_whole if len(f) == 1 else head_spec(f[half]) for f in later[1:]]
        + [stat_spec(a) for a in later_stats]
        + [half_of_whole] * len(returned)
    )
    out = jax.ShapeDtypeStruct((2, rows, width), BF16)
    groups = (len(later[0]),) + (1,) * len(far)
    (result,) = call(
        functools.partial(key_kernel, half, groups, len(returned)),
        where,
        operands,
        in_specs,
        [out],
        [head_spec(out)],
        heads,
        (4 + len(far)) * BLOCK,
        "key_side",
    )
    return result


def matmul(a, b):
    return jnp.dot(a, b, preferred_element_type=F32)


def matmul_t(a, b):
    return lax.dot_general(a, b, NT, preferred_element_type=F32)


def relay(rows, sign):
    two = shifted(rows, sign * 2)
    four = shifted(two, sign * 2)
    return [(two,), (four,), (shifted(four, sign * 4),)]


def per_device(series, norm_gain, w_query, w_key, w_value, w_out, out_grad):
    levels = lax.axis_size("seq").bit_length() - 1
    half = series.shape[0]
    blocks = 2 * half // BLOCK
    tp_index = lax.axis_index("tp").astype(jnp.int32)
    seq_index = lax.axis_index("seq").astype(jnp.int32)
    where = tp_index[None]
    slots = jnp.arange(blocks, dtype=jnp.int32)
    global_block = seq_index * blocks + (slots + 2 * tp_index) % blocks
    distances = [1, 2, 4] + [blocks * 2**s for s in range(1, levels)]
    reach = jnp.repeat(jnp.array([0] + distances, jnp.int32), BLOCK)
    bias = jnp.where(global_block[:, None] >= reach[None], 0.0, NEG).astype(F32)[:, None, :]

    series_f = series.astype(F32)
    inv_rms = lax.rsqrt(jnp.mean(series_f * series_f, axis=-1, keepdims=True) + EPS)
    unit_rows = series_f * inv_rms
    normed = (unit_rows * norm_gain).astype(BF16)
    normed_other = swap_tp(normed)
    out_grad_other = swap_tp(out_grad)

    def key_value(rows):
        return jnp.stack([matmul(rows, w_key).astype(BF16), matmul(rows, w_value).astype(BF16)])

    def query_grad(rows, grad_rows):
        return jnp.stack(
            [matmul(rows, w_query).astype(BF16), matmul_t(grad_rows, w_out).astype(BF16)]
        )

    kv = (key_value(normed), key_value(normed_other))
    qg = (query_grad(normed, out_grad), query_grad(normed_other, out_grad_other))
    kv_all = jnp.concatenate(kv, axis=1)
    qg_all = jnp.concatenate(qg, axis=1)
    fetched = [(shifted(kv_all, 1),)] + relay(kv_all, 1) + [(shifted(kv_all, by),) for by in (16, 32, 64)]
    later = [(shifted(qg_all, -1),)] + relay(qg_all, -1)
    mixed, grad_query, stat, *backs = query_side(where, bias, qg, kv, fetched, 3)
    stat, backs, later = lax.optimization_barrier((stat, backs, later))
    returned = [shifted(b, -by) for b, by in zip(backs, (16, 32, 64))]
    later_stats = [shifted(stat, -by) for by in (1, 2, 4, 8)]
    attn_other = swap_tp(matmul(mixed[half:], w_out).astype(BF16))
    attn_rows = matmul(mixed[:half], w_out) + attn_other.astype(F32)
    layer_out = (series_f + attn_rows).astype(BF16)

    def back(at):
        grad_kv = key_side(at, where, kv, qg, stat, later, later_stats, returned)
        rows = slice(at * half, (at + 1) * half)
        return (
            matmul_t(grad_query[rows], w_query)
            + matmul_t(grad_kv[0], w_key)
            + matmul_t(grad_kv[1], w_value)
        )

    normed_grad_other = swap_tp(back(1).astype(BF16))
    normed_grad = back(0) + normed_grad_other.astype(F32)
    scaled = normed_grad * norm_gain
    series_grad = out_grad.astype(F32) + inv_rms * (
        scaled - unit_rows * jnp.mean(scaled * unit_rows, axis=-1, keepdims=True)
    )
    return (layer_out, series_grad.astype(BF16))


def solution(mesh):
    rows = P(("seq", "tp"), None)
    columns = P(None, "tp")
    in_specs = (rows, P(), columns, columns, columns, P("tp", None), rows)
    return jax.shard_map(
        per_device, mesh=mesh, in_specs=in_specs, out_specs=(rows, rows), check_vma=False
    )
```

```python
import functools

import jax
import jax.numpy as jnp
from jax import lax
from jax.experimental import pallas as pl
from jax.experimental.pallas import tpu as pltpu
from jax.sharding import PartitionSpec as P

HD = 128
BLOCK = 64
NEG = -1e30
EPS = 1e-06
F32 = jnp.float32
BF16 = jnp.bfloat16
NN = (((1,), (0,)), ((), ()))
NT = (((1,), (1,)), ((), ()))
TN = (((0,), (0,)), ((), ()))
NEAR = (1, 2, 4)


def shifted(value, by):
    size = lax.axis_size("seq")
    pairs = [(i, i + by) for i in range(size) if 0 <= i + by < size]
    return lax.ppermute(value, "seq", pairs)


def swap_tp(value):
    return lax.ppermute(value, "tp", [(0, 1), (1, 0)])


def dot(a, b, dims):
    return lax.dot_general(a, b, dims, preferred_element_type=F32)


def piece(pieces, which, slot):
    per = 4 // len(pieces)
    at = (slot % per) * BLOCK
    return pieces[slot // per][which, at : at + BLOCK, :]


def near_slots(step, slot):
    found = []
    for turn in (0, 2):
        block = (slot + turn) % 4 + step
        found.append((0 <= block < 4, (block + turn) % 4))
    return found


def near(is_second, own, other, which, slot, step):
    options = [
        piece(own if here else other, which, at) for here, at in near_slots(step, slot)
    ]
    return jnp.where(is_second, options[1], options[0])


def causal_bias(query_axis):
    rows = lax.broadcasted_iota(jnp.int32, (BLOCK, BLOCK), query_axis)
    keys = lax.broadcasted_iota(jnp.int32, (BLOCK, BLOCK), 1 - query_axis)
    return jnp.where(rows >= keys, 0.0, NEG).astype(F32)


def query_kernel(groups, n_back, where_ref, bias_ref, *refs):
    refs = list(refs)
    qg = [refs.pop(0) for _ in range(2)]
    kv = [refs.pop(0) for _ in range(2)]
    fetched = [[refs.pop(0) for _ in range(n)] for n in groups]
    mixed_ref, dq_ref, stat_ref, *back_refs = refs
    is_second = where_ref[0] == 1
    factor = HD ** (-0.5)
    causal = causal_bias(0)
    lane = lax.broadcasted_iota(jnp.int32, (BLOCK, HD), 1)
    slots = range(4)

    def gather(which, slot):
        return jnp.concatenate(
            [piece(kv, which, slot)]
            + [near(is_second, kv, fetched[0], which, slot, -d) for d in NEAR]
            + [piece(f, which, slot) for f in fetched[1:]],
            axis=0,
        )

    def rows(slot):
        return slice(slot * BLOCK, (slot + 1) * BLOCK)

    query = [piece(qg, 0, slot) for slot in slots]
    grad = [piece(qg, 1, slot) for slot in slots]
    keys = [gather(0, slot) for slot in slots]
    values = [gather(1, slot) for slot in slots]
    score = []
    for slot in slots:
        s = dot(query[slot], keys[slot], NT) * factor + bias_ref[slot]
        score.append(jnp.concatenate([s[:, :BLOCK] + causal, s[:, BLOCK:]], axis=1))
    grad_prob = [dot(grad[slot], values[slot], NT) for slot in slots]
    peak = [jnp.max(s, axis=-1, keepdims=True) for s in score]
    weight = [jnp.exp(score[slot] - peak[slot]) for slot in slots]
    total = [jnp.sum(w, axis=-1, keepdims=True) for w in weight]
    prob = [weight[slot] * (1.0 / total[slot]) for slot in slots]
    prob_b = [p.astype(BF16) for p in prob]
    mixed = [dot(prob_b[slot], values[slot], NN).astype(BF16) for slot in slots]
    inner = [
        jnp.sum(mixed[slot].astype(F32) * grad[slot].astype(F32), axis=-1, keepdims=True)
        for slot in slots
    ]
    grad_score = [
        (prob[slot] * (grad_prob[slot] - inner[slot])).astype(BF16) for slot in slots
    ]
    first = keys[0].shape[0] - n_back * BLOCK
    for slot in slots:
        out = rows(slot)
        mixed_ref[out, :] = mixed[slot]
        dq_ref[out, :] = (dot(grad_score[slot], keys[slot], NN) * factor).astype(BF16)
        stat = jnp.where(lane == 0, peak[slot] + jnp.log(total[slot]), inner[slot])
        stat_ref[0, :, out] = jnp.transpose(stat)[:2]
        if n_back:
            grad_keys = (dot(grad_score[slot][:, first:], query[slot], TN) * factor).astype(BF16)
            grad_values = dot(prob_b[slot][:, first:], grad[slot], TN).astype(BF16)
            for at, ref in enumerate(back_refs):
                ref[0, out, :] = grad_keys[at * BLOCK : (at + 1) * BLOCK]
                ref[1, out, :] = grad_values[at * BLOCK : (at + 1) * BLOCK]


def key_kernel(half, groups, n_back, where_ref, *refs):
    refs = list(refs)
    kv = refs.pop(0)
    qg = [refs.pop(0) for _ in range(2)]
    stat = refs.pop(0)
    later = [[refs.pop(0) for _ in range(n)] for n in groups]
    later_stats = [refs.pop(0) for _ in groups]
    back = [refs.pop(0) for _ in range(n_back)]
    (out_ref,) = refs
    is_second = where_ref[0] == 1
    factor = HD ** (-0.5)
    causal = causal_bias(1)

    def stat_of(ref, slot):
        return ref[0, :, slot * BLOCK : (slot + 1) * BLOCK]

    for at in range(2):
        slot = 2 * half + at
        rows = slice(at * BLOCK, (at + 1) * BLOCK)
        queries, grads = [
            jnp.concatenate(
                [piece(qg, which, slot)]
                + [near(is_second, qg, later[0], which, slot, d) for d in NEAR]
                + [f[0][which, rows, :] for f in later[1:]],
                axis=0,
            )
            for which in range(2)
        ]
        near_stats = []
        for d in NEAR:
            options = [
                stat_of(stat if here else later_stats[0], s) for here, s in near_slots(d, slot)
            ]
            near_stats.append(jnp.where(is_second, options[1], options[0]))
        stats = jnp.concatenate(
            [stat_of(stat, slot)] + near_stats + [stat_of(f, slot) for f in later_stats[1:]], axis=1
        )
        score = dot(kv[0, rows, :], queries, NT) * factor
        score = jnp.concatenate([score[:, :BLOCK] + causal, score[:, BLOCK:]], axis=1)
        prob = jnp.exp(score - stats[0:1])
        grad_score = (prob * (dot(kv[1, rows, :], grads, NT) - stats[1:2])).astype(BF16)
        totals = [
            dot(grad_score, queries, NN) * factor,
            dot(prob.astype(BF16), grads, NN),
        ]
        for which in range(2):
            for ref in back:
                totals[which] += ref[which, rows, :].astype(F32)
            out_ref[which, rows, :] = totals[which].astype(BF16)


def head_spec(a):
    if a.ndim == 2:
        return pl.BlockSpec((a.shape[0], HD), lambda h, w: (0, h))
    return pl.BlockSpec((a.shape[0], a.shape[1], HD), lambda h, w: (0, 0, h))


def stat_spec(a):
    return pl.BlockSpec((1,) + a.shape[1:], lambda h, w: (h, 0, 0))


def call(kernel, where, operands, in_specs, outs, out_specs, heads, keys, name):
    rows = outs[0].shape[-2]
    return pl.pallas_call(
        kernel,
        out_shape=outs,
        grid_spec=pltpu.PrefetchScalarGridSpec(
            num_scalar_prefetch=1, grid=(heads,), in_specs=in_specs, out_specs=out_specs
        ),
        compiler_params=pltpu.CompilerParams(vmem_limit_bytes=10 * 2**20),
        cost_estimate=pl.CostEstimate(
            flops=4 * 2 * rows * keys * HD * heads,
            bytes_accessed=6 * 2**20,
            transcendentals=rows * keys * heads,
        ),
        name=name,
    )(where, *operands)


def query_side(where, bias, qg, kv, fetched, n_back):
    rows, width = 2 * qg[0].shape[1], qg[0].shape[2]
    heads = width // HD
    far = [pltpu.with_memory_space_constraint(a, pltpu.HBM) for f in fetched for a in f]
    operands = [*qg, *kv, *far]
    row_out = jax.ShapeDtypeStruct((rows, width), BF16)
    stat_out = jax.ShapeDtypeStruct((heads, 2, rows), F32)
    back_out = jax.ShapeDtypeStruct((2, rows, width), BF16)
    outs = [row_out, row_out, stat_out] + [back_out] * n_back
    return call(
        functools.partial(query_kernel, tuple(len(f) for f in fetched), n_back),
        where,
        [bias, *operands],
        [pl.BlockSpec(bias.shape, lambda h, w: (0, 0, 0))] + [head_spec(a) for a in operands],
        outs,
        [head_spec(row_out), head_spec(row_out), stat_spec(stat_out)] + [head_spec(back_out)] * n_back,
        heads,
        bias.shape[2],
        "query_side",
    )


def key_side(half, where, kv, qg, stat, later, later_stats, returned):
    rows, width = kv[0].shape[1], kv[0].shape[2]
    heads = width // HD
    half_of_whole = pl.BlockSpec((2, rows, HD), lambda h, w: (0, half, h))
    far = [f[-1] if len(f) == 1 else f[half] for f in later[1:]]
    operands = [kv[half], *qg, stat, *later[0], *far, *later_stats, *returned]
    in_specs = (
        [head_spec(a) for a in (kv[half], *qg)]
        + [stat_spec(stat)]
        + [head_spec(a) for a in later[0]]
        + [half_of_whole if len(f) == 1 else head_spec(f[half]) for f in later[1:]]
        + [stat_spec(a) for a in later_stats]
        + [half_of_whole] * len(returned)
    )
    out = jax.ShapeDtypeStruct((2, rows, width), BF16)
    groups = (len(later[0]),) + (1,) * len(far)
    (result,) = call(
        functools.partial(key_kernel, half, groups, len(returned)),
        where,
        operands,
        in_specs,
        [out],
        [head_spec(out)],
        heads,
        (4 + len(far)) * BLOCK,
        "key_side",
    )
    return result


def matmul(a, b):
    return jnp.dot(a, b, preferred_element_type=F32)


def matmul_t(a, b):
    return lax.dot_general(a, b, NT, preferred_element_type=F32)


def swapped(own, passed, bit, sign):
    size = lax.axis_size("seq")
    high = (lax.axis_index("seq") // bit) % 2 == 1
    sent = jnp.where(high, passed, own) if sign > 0 else jnp.where(high, own, passed)
    return lax.ppermute(sent, "seq", [(i, i ^ bit) for i in range(size)])


def exchange(rows, sign):
    two = shifted(rows, sign * 2)
    far = shifted(rows, sign * 32)
    four = shifted(two, sign * 2)
    one = swapped(rows, two, 1, sign)
    sixteen = swapped(rows, far, 16, sign)
    return [one, two, four, shifted(four, sign * 4), sixteen, far, shifted(far, sign * 32)]


def per_device(series, norm_gain, w_query, w_key, w_value, w_out, out_grad):
    levels = lax.axis_size("seq").bit_length() - 1
    half = series.shape[0]
    blocks = 2 * half // BLOCK
    tp_index = lax.axis_index("tp").astype(jnp.int32)
    seq_index = lax.axis_index("seq").astype(jnp.int32)
    where = tp_index[None]
    slots = jnp.arange(blocks, dtype=jnp.int32)
    global_block = seq_index * blocks + (slots + 2 * tp_index) % blocks
    distances = [1, 2, 4] + [blocks * 2**s for s in range(1, levels)]
    reach = jnp.repeat(jnp.array([0] + distances, jnp.int32), BLOCK)
    bias = jnp.where(global_block[:, None] >= reach[None], 0.0, NEG).astype(F32)[:, None, :]

    series_f = series.astype(F32)
    inv_rms = lax.rsqrt(jnp.mean(series_f * series_f, axis=-1, keepdims=True) + EPS)
    unit_rows = series_f * inv_rms
    normed = (unit_rows * norm_gain).astype(BF16)
    normed_other = swap_tp(normed)
    out_grad_later, normed_other = lax.optimization_barrier((out_grad, normed_other))
    out_grad_other = swap_tp(out_grad_later)

    def key_value(rows):
        return jnp.stack([matmul(rows, w_key).astype(BF16), matmul(rows, w_value).astype(BF16)])

    def query_grad(rows, grad_rows):
        return jnp.stack(
            [matmul(rows, w_query).astype(BF16), matmul_t(grad_rows, w_out).astype(BF16)]
        )

    kv = (key_value(normed), key_value(normed_other))
    qg = (query_grad(normed, out_grad), query_grad(normed_other, out_grad_other))
    kv_all = jnp.concatenate(kv, axis=1)
    qg_all = jnp.concatenate(qg, axis=1)
    fetched = exchange(kv_all, 1)
    later = exchange(qg_all, -1)
    mixed, grad_query, stat = query_side(where, bias, qg, kv, [(f,) for f in fetched], 0)
    last = later.pop(3)
    stat, later = lax.optimization_barrier((stat, later))
    later.insert(3, last)
    later = [(f,) for f in later]
    later_stats = [shifted(stat, -(2**s)) for s in range(levels)]
    attn_other = swap_tp(matmul(mixed[half:], w_out).astype(BF16))
    attn_rows = matmul(mixed[:half], w_out) + attn_other.astype(F32)
    layer_out = (series_f + attn_rows).astype(BF16)

    def back(at):
        grad_kv = key_side(at, where, kv, qg, stat, later, later_stats, [])
        rows = slice(at * half, (at + 1) * half)
        return (
            matmul_t(grad_query[rows], w_query)
            + matmul_t(grad_kv[0], w_key)
            + matmul_t(grad_kv[1], w_value)
        )

    normed_grad_other = swap_tp(back(1).astype(BF16))
    normed_grad = back(0) + normed_grad_other.astype(F32)
    scaled = normed_grad * norm_gain
    series_grad = out_grad.astype(F32) + inv_rms * (
        scaled - unit_rows * jnp.mean(scaled * unit_rows, axis=-1, keepdims=True)
    )
    return (layer_out, series_grad.astype(BF16))


def solution(mesh):
    rows = P(("seq", "tp"), None)
    columns = P(None, "tp")
    in_specs = (rows, P(), columns, columns, columns, P("tp", None), rows)
    return jax.shard_map(
        per_device, mesh=mesh, in_specs=in_specs, out_specs=(rows, rows), check_vma=False
    )
```

```python
import functools

import jax
import jax.numpy as jnp
from jax import lax
from jax.experimental import pallas as pl
from jax.experimental.pallas import tpu as pltpu
from jax.sharding import PartitionSpec as P

HD = 128
BLOCK = 64
NEG = -1e30
EPS = 1e-06
F32 = jnp.float32
BF16 = jnp.bfloat16
NN = (((1,), (0,)), ((), ()))
NT = (((1,), (1,)), ((), ()))
TN = (((0,), (0,)), ((), ()))
NEAR = (1, 2, 4)


def shifted(value, by):
    size = lax.axis_size("seq")
    pairs = [(i, i + by) for i in range(size) if 0 <= i + by < size]
    return lax.ppermute(value, "seq", pairs)


def swap_tp(value):
    return lax.ppermute(value, "tp", [(0, 1), (1, 0)])


def dot(a, b, dims):
    return lax.dot_general(a, b, dims, preferred_element_type=F32)


def piece(pieces, which, slot):
    per = 4 // len(pieces)
    at = (slot % per) * BLOCK
    return pieces[slot // per][which, at : at + BLOCK, :]


def near_slots(step, slot):
    found = []
    for turn in (0, 2):
        block = (slot + turn) % 4 + step
        found.append((0 <= block < 4, (block + turn) % 4))
    return found


def near(is_second, own, other, which, slot, step):
    options = [
        piece(own if here else other, which, at) for here, at in near_slots(step, slot)
    ]
    return jnp.where(is_second, options[1], options[0])


def causal_bias(query_axis):
    rows = lax.broadcasted_iota(jnp.int32, (BLOCK, BLOCK), query_axis)
    keys = lax.broadcasted_iota(jnp.int32, (BLOCK, BLOCK), 1 - query_axis)
    return jnp.where(rows >= keys, 0.0, NEG).astype(F32)


def query_kernel(groups, n_back, where_ref, bias_ref, *refs):
    refs = list(refs)
    qg = [refs.pop(0) for _ in range(2)]
    kv = [refs.pop(0) for _ in range(2)]
    fetched = [[refs.pop(0) for _ in range(n)] for n in groups]
    mixed_ref, dq_ref, stat_ref, *back_refs = refs
    is_second = where_ref[0] == 1
    factor = HD ** (-0.5)
    causal = causal_bias(0)
    lane = lax.broadcasted_iota(jnp.int32, (BLOCK, HD), 1)
    slots = range(4)

    def gather(which, slot):
        return jnp.concatenate(
            [piece(kv, which, slot)]
            + [near(is_second, kv, fetched[0], which, slot, -d) for d in NEAR]
            + [piece(f, which, slot) for f in fetched[1:]],
            axis=0,
        )

    def rows(slot):
        return slice(slot * BLOCK, (slot + 1) * BLOCK)

    query = [piece(qg, 0, slot) for slot in slots]
    grad = [piece(qg, 1, slot) for slot in slots]
    keys = [gather(0, slot) for slot in slots]
    values = [gather(1, slot) for slot in slots]
    score = []
    for slot in slots:
        s = dot(query[slot], keys[slot], NT) * factor + bias_ref[slot]
        score.append(jnp.concatenate([s[:, :BLOCK] + causal, s[:, BLOCK:]], axis=1))
    grad_prob = [dot(grad[slot], values[slot], NT) for slot in slots]
    peak = [jnp.max(s, axis=-1, keepdims=True) for s in score]
    weight = [jnp.exp(score[slot] - peak[slot]) for slot in slots]
    total = [jnp.sum(w, axis=-1, keepdims=True) for w in weight]
    prob = [weight[slot] * (1.0 / total[slot]) for slot in slots]
    prob_b = [p.astype(BF16) for p in prob]
    mixed = [dot(prob_b[slot], values[slot], NN).astype(BF16) for slot in slots]
    inner = [
        jnp.sum(mixed[slot].astype(F32) * grad[slot].astype(F32), axis=-1, keepdims=True)
        for slot in slots
    ]
    grad_score = [
        (prob[slot] * (grad_prob[slot] - inner[slot])).astype(BF16) for slot in slots
    ]
    first = keys[0].shape[0] - n_back * BLOCK
    for slot in slots:
        out = rows(slot)
        mixed_ref[out, :] = mixed[slot]
        dq_ref[out, :] = (dot(grad_score[slot], keys[slot], NN) * factor).astype(BF16)
        stat = jnp.where(lane == 0, peak[slot] + jnp.log(total[slot]), inner[slot])
        stat_ref[0, :, out] = jnp.transpose(stat)[:2]
        if n_back:
            grad_keys = (dot(grad_score[slot][:, first:], query[slot], TN) * factor).astype(BF16)
            grad_values = dot(prob_b[slot][:, first:], grad[slot], TN).astype(BF16)
            for at, ref in enumerate(back_refs):
                ref[0, out, :] = grad_keys[at * BLOCK : (at + 1) * BLOCK]
                ref[1, out, :] = grad_values[at * BLOCK : (at + 1) * BLOCK]


def key_kernel(half, groups, n_back, where_ref, *refs):
    refs = list(refs)
    kv = refs.pop(0)
    qg = [refs.pop(0) for _ in range(2)]
    stat = refs.pop(0)
    later = [[refs.pop(0) for _ in range(n)] for n in groups]
    later_stats = [refs.pop(0) for _ in groups]
    back = [refs.pop(0) for _ in range(n_back)]
    (out_ref,) = refs
    is_second = where_ref[0] == 1
    factor = HD ** (-0.5)
    causal = causal_bias(1)

    def stat_of(ref, slot):
        return ref[0, :, slot * BLOCK : (slot + 1) * BLOCK]

    for at in range(2):
        slot = 2 * half + at
        rows = slice(at * BLOCK, (at + 1) * BLOCK)
        queries, grads = [
            jnp.concatenate(
                [piece(qg, which, slot)]
                + [near(is_second, qg, later[0], which, slot, d) for d in NEAR]
                + [f[0][which, rows, :] for f in later[1:]],
                axis=0,
            )
            for which in range(2)
        ]
        near_stats = []
        for d in NEAR:
            options = [
                stat_of(stat if here else later_stats[0], s) for here, s in near_slots(d, slot)
            ]
            near_stats.append(jnp.where(is_second, options[1], options[0]))
        stats = jnp.concatenate(
            [stat_of(stat, slot)] + near_stats + [stat_of(f, slot) for f in later_stats[1:]], axis=1
        )
        score = dot(kv[0, rows, :], queries, NT) * factor
        score = jnp.concatenate([score[:, :BLOCK] + causal, score[:, BLOCK:]], axis=1)
        prob = jnp.exp(score - stats[0:1])
        grad_score = (prob * (dot(kv[1, rows, :], grads, NT) - stats[1:2])).astype(BF16)
        totals = [
            dot(grad_score, queries, NN) * factor,
            dot(prob.astype(BF16), grads, NN),
        ]
        for which in range(2):
            for ref in back:
                totals[which] += ref[which, rows, :].astype(F32)
            out_ref[which, rows, :] = totals[which].astype(BF16)


def head_spec(a):
    if a.ndim == 2:
        return pl.BlockSpec((a.shape[0], HD), lambda h, w: (0, h))
    return pl.BlockSpec((a.shape[0], a.shape[1], HD), lambda h, w: (0, 0, h))


def stat_spec(a):
    return pl.BlockSpec((1,) + a.shape[1:], lambda h, w: (h, 0, 0))


def call(kernel, where, operands, in_specs, outs, out_specs, heads, keys, name):
    rows = outs[0].shape[-2]
    return pl.pallas_call(
        kernel,
        out_shape=outs,
        grid_spec=pltpu.PrefetchScalarGridSpec(
            num_scalar_prefetch=1, grid=(heads,), in_specs=in_specs, out_specs=out_specs
        ),
        compiler_params=pltpu.CompilerParams(vmem_limit_bytes=10 * 2**20),
        cost_estimate=pl.CostEstimate(
            flops=4 * 2 * rows * keys * HD * heads,
            bytes_accessed=6 * 2**20,
            transcendentals=rows * keys * heads,
        ),
        name=name,
    )(where, *operands)


def query_side(where, bias, qg, kv, fetched, n_back):
    rows, width = 2 * qg[0].shape[1], qg[0].shape[2]
    heads = width // HD
    far = [pltpu.with_memory_space_constraint(a, pltpu.HBM) for f in fetched for a in f]
    operands = [*qg, *kv, *far]
    row_out = jax.ShapeDtypeStruct((rows, width), BF16)
    stat_out = jax.ShapeDtypeStruct((heads, 2, rows), F32)
    back_out = jax.ShapeDtypeStruct((2, rows, width), BF16)
    outs = [row_out, row_out, stat_out] + [back_out] * n_back
    return call(
        functools.partial(query_kernel, tuple(len(f) for f in fetched), n_back),
        where,
        [bias, *operands],
        [pl.BlockSpec(bias.shape, lambda h, w: (0, 0, 0))] + [head_spec(a) for a in operands],
        outs,
        [head_spec(row_out), head_spec(row_out), stat_spec(stat_out)] + [head_spec(back_out)] * n_back,
        heads,
        bias.shape[2],
        "query_side",
    )


def key_side(half, where, kv, qg, stat, later, later_stats, returned):
    rows, width = kv[0].shape[1], kv[0].shape[2]
    heads = width // HD
    half_of_whole = pl.BlockSpec((2, rows, HD), lambda h, w: (0, half, h))
    far = [f[-1] if len(f) == 1 else f[half] for f in later[1:]]
    operands = [kv[half], *qg, stat, *later[0], *far, *later_stats, *returned]
    in_specs = (
        [head_spec(a) for a in (kv[half], *qg)]
        + [stat_spec(stat)]
        + [head_spec(a) for a in later[0]]
        + [half_of_whole if len(f) == 1 else head_spec(f[half]) for f in later[1:]]
        + [stat_spec(a) for a in later_stats]
        + [half_of_whole] * len(returned)
    )
    out = jax.ShapeDtypeStruct((2, rows, width), BF16)
    groups = (len(later[0]),) + (1,) * len(far)
    (result,) = call(
        functools.partial(key_kernel, half, groups, len(returned)),
        where,
        operands,
        in_specs,
        [out],
        [head_spec(out)],
        heads,
        (4 + len(far)) * BLOCK,
        "key_side",
    )
    return result


def matmul(a, b):
    return jnp.dot(a, b, preferred_element_type=F32)


def matmul_t(a, b):
    return lax.dot_general(a, b, NT, preferred_element_type=F32)


def swapped(own, passed, bit, sign):
    size = lax.axis_size("seq")
    high = (lax.axis_index("seq") // bit) % 2 == 1
    sent = jnp.where(high, passed, own) if sign > 0 else jnp.where(high, own, passed)
    return lax.ppermute(sent, "seq", [(i, i ^ bit) for i in range(size)])


def per_device(series, norm_gain, w_query, w_key, w_value, w_out, out_grad):
    levels = lax.axis_size("seq").bit_length() - 1
    half = series.shape[0]
    blocks = 2 * half // BLOCK
    tp_index = lax.axis_index("tp").astype(jnp.int32)
    seq_index = lax.axis_index("seq").astype(jnp.int32)
    where = tp_index[None]
    slots = jnp.arange(blocks, dtype=jnp.int32)
    global_block = seq_index * blocks + (slots + 2 * tp_index) % blocks
    distances = [1, 2, 4] + [blocks * 2**s for s in range(1, levels)]
    reach = jnp.repeat(jnp.array([0] + distances, jnp.int32), BLOCK)
    bias = jnp.where(global_block[:, None] >= reach[None], 0.0, NEG).astype(F32)[:, None, :]

    series_f = series.astype(F32)
    inv_rms = lax.rsqrt(jnp.mean(series_f * series_f, axis=-1, keepdims=True) + EPS)
    unit_rows = series_f * inv_rms
    normed = (unit_rows * norm_gain).astype(BF16)
    normed_other = swap_tp(normed)

    def key_value(rows):
        return jnp.stack([matmul(rows, w_key).astype(BF16), matmul(rows, w_value).astype(BF16)])

    def query_grad(rows, grad_rows):
        return jnp.stack(
            [matmul(rows, w_query).astype(BF16), matmul_t(grad_rows, w_out).astype(BF16)]
        )

    kv_own = key_value(normed)
    early = {by: shifted(kv_own, by) for by in (32, 2, 8)}
    normed_other, early[32], early[2] = lax.optimization_barrier((normed_other, early[32], early[2]))
    out_grad_late, normed_other = lax.optimization_barrier((out_grad, normed_other))
    out_grad_other = swap_tp(out_grad_late)
    kv = (kv_own, key_value(normed_other))
    pairs = {by: (early[by], shifted(kv[1], by)) for by in (2, 32, 8)}
    two, far = [jnp.concatenate(pairs[by], axis=1) for by in (2, 32)]
    four = shifted(two, 2)
    kv_all = jnp.concatenate(kv, axis=1)
    far_kv, early[8] = lax.optimization_barrier((far, pairs[8][0]))
    two_kv, late_eight, four = lax.optimization_barrier((two, pairs[8][1], four))
    fetched = [
        (swapped(kv_all, two_kv, 1, 1),),
        pairs[2],
        (four,),
        (early[8], late_eight),
        (swapped(kv_all, far_kv, 16, 1),),
        pairs[32],
        (shifted(far, 32),),
    ]

    qg = (query_grad(normed, out_grad), query_grad(normed_other, out_grad_other))
    qg_all = jnp.concatenate(qg, axis=1)
    two = shifted(qg_all, -2)
    qg_late, _ = lax.optimization_barrier((qg_all, four))
    far = shifted(qg_late, -32)
    four = shifted(two, -2)
    later = [swapped(qg_all, two, 1, -1), two, four, swapped(qg_all, far, 16, -1), far]
    mixed, grad_query, stat = query_side(where, bias, qg, kv, fetched, 0)
    stat, later = lax.optimization_barrier((stat, later))
    later = later[:3] + [shifted(four, -4)] + later[3:] + [shifted(far, -32)]
    later = [(f,) for f in later]
    later_stats = [shifted(stat, -(2**s)) for s in range(levels)]
    attn_other = swap_tp(matmul(mixed[half:], w_out).astype(BF16))
    attn_rows = matmul(mixed[:half], w_out) + attn_other.astype(F32)
    layer_out = (series_f + attn_rows).astype(BF16)

    grad_queries = lax.optimization_barrier(matmul_t(grad_query, w_query))

    def back(at):
        grad_kv = key_side(at, where, kv, qg, stat, later, later_stats, [])
        rows = slice(at * half, (at + 1) * half)
        return (
            grad_queries[rows]
            + matmul_t(grad_kv[0], w_key)
            + matmul_t(grad_kv[1], w_value)
        )

    normed_grad_other = swap_tp(back(1).astype(BF16))
    normed_grad = back(0) + normed_grad_other.astype(F32)
    scaled = normed_grad * norm_gain
    series_grad = out_grad.astype(F32) + inv_rms * (
        scaled - unit_rows * jnp.mean(scaled * unit_rows, axis=-1, keepdims=True)
    )
    return (layer_out, series_grad.astype(BF16))


def solution(mesh):
    rows = P(("seq", "tp"), None)
    columns = P(None, "tp")
    in_specs = (rows, P(), columns, columns, columns, P("tp", None), rows)
    return jax.shard_map(
        per_device, mesh=mesh, in_specs=in_specs, out_specs=(rows, rows), check_vma=False
    )
```

```python
import functools

import jax
import jax.numpy as jnp
from jax import lax
from jax.experimental import pallas as pl
from jax.experimental.pallas import tpu as pltpu
from jax.sharding import PartitionSpec as P

HD = 128
BLOCK = 64
NEG = -1e30
EPS = 1e-06
F32 = jnp.float32
BF16 = jnp.bfloat16
NN = (((1,), (0,)), ((), ()))
NT = (((1,), (1,)), ((), ()))
TN = (((0,), (0,)), ((), ()))
NEAR = (1, 2, 4)


def shifted(value, by):
    size = lax.axis_size("seq")
    pairs = [(i, i + by) for i in range(size) if 0 <= i + by < size]
    return lax.ppermute(value, "seq", pairs)


def swap_tp(value):
    return lax.ppermute(value, "tp", [(0, 1), (1, 0)])


def dot(a, b, dims):
    return lax.dot_general(a, b, dims, preferred_element_type=F32)


def piece(pieces, which, slot):
    per = 4 // len(pieces)
    at = (slot % per) * BLOCK
    return pieces[slot // per][which, at : at + BLOCK, :]


def near_slots(step, slot):
    found = []
    for turn in (0, 2):
        block = (slot + turn) % 4 + step
        found.append((0 <= block < 4, (block + turn) % 4))
    return found


def near(is_second, own, other, which, slot, step):
    options = [
        piece(own if here else other, which, at) for here, at in near_slots(step, slot)
    ]
    return jnp.where(is_second, options[1], options[0])


def causal_bias(query_axis):
    rows = lax.broadcasted_iota(jnp.int32, (BLOCK, BLOCK), query_axis)
    keys = lax.broadcasted_iota(jnp.int32, (BLOCK, BLOCK), 1 - query_axis)
    return jnp.where(rows >= keys, 0.0, NEG).astype(F32)


def query_kernel(groups, n_back, where_ref, bias_ref, *refs):
    refs = list(refs)
    qg = [refs.pop(0) for _ in range(2)]
    kv = [refs.pop(0) for _ in range(2)]
    fetched = [[refs.pop(0) for _ in range(n)] for n in groups]
    mixed_ref, dq_ref, stat_ref, *back_refs = refs
    is_second = where_ref[0] == 1
    factor = HD ** (-0.5)
    causal = causal_bias(0)
    lane = lax.broadcasted_iota(jnp.int32, (BLOCK, HD), 1)
    slots = range(4)

    def gather(which, slot):
        return jnp.concatenate(
            [piece(kv, which, slot)]
            + [near(is_second, kv, fetched[0], which, slot, -d) for d in NEAR]
            + [piece(f, which, slot) for f in fetched[1:]],
            axis=0,
        )

    def rows(slot):
        return slice(slot * BLOCK, (slot + 1) * BLOCK)

    query = [piece(qg, 0, slot) for slot in slots]
    grad = [piece(qg, 1, slot) for slot in slots]
    keys = [gather(0, slot) for slot in slots]
    values = [gather(1, slot) for slot in slots]
    score = []
    for slot in slots:
        s = dot(query[slot], keys[slot], NT) * factor + bias_ref[slot]
        score.append(jnp.concatenate([s[:, :BLOCK] + causal, s[:, BLOCK:]], axis=1))
    grad_prob = [dot(grad[slot], values[slot], NT) for slot in slots]
    peak = [jnp.max(s, axis=-1, keepdims=True) for s in score]
    weight = [jnp.exp(score[slot] - peak[slot]) for slot in slots]
    total = [jnp.sum(w, axis=-1, keepdims=True) for w in weight]
    prob = [weight[slot] * (1.0 / total[slot]) for slot in slots]
    prob_b = [p.astype(BF16) for p in prob]
    mixed = [dot(prob_b[slot], values[slot], NN).astype(BF16) for slot in slots]
    inner = [
        jnp.sum(mixed[slot].astype(F32) * grad[slot].astype(F32), axis=-1, keepdims=True)
        for slot in slots
    ]
    grad_score = [
        (prob[slot] * (grad_prob[slot] - inner[slot])).astype(BF16) for slot in slots
    ]
    first = keys[0].shape[0] - n_back * BLOCK
    for slot in slots:
        out = rows(slot)
        mixed_ref[out, :] = mixed[slot]
        dq_ref[out, :] = (dot(grad_score[slot], keys[slot], NN) * factor).astype(BF16)
        stat = jnp.where(lane == 0, peak[slot] + jnp.log(total[slot]), inner[slot])
        stat_ref[0, :, out] = jnp.transpose(stat)[:2]
        if n_back:
            grad_keys = (dot(grad_score[slot][:, first:], query[slot], TN) * factor).astype(BF16)
            grad_values = dot(prob_b[slot][:, first:], grad[slot], TN).astype(BF16)
            for at, ref in enumerate(back_refs):
                ref[0, out, :] = grad_keys[at * BLOCK : (at + 1) * BLOCK]
                ref[1, out, :] = grad_values[at * BLOCK : (at + 1) * BLOCK]


def key_kernel(half, groups, where_ref, *refs):
    refs = list(refs)
    kv = refs.pop(0)
    qg = [refs.pop(0) for _ in range(2)]
    stat = refs.pop(0)
    later = [[refs.pop(0) for _ in range(n)] for n in groups]
    later_stats = [refs.pop(0) for _ in groups]
    (out_ref,) = refs
    is_second = where_ref[0] == 1
    factor = HD ** (-0.5)
    causal = causal_bias(1)

    def stat_of(ref, slot):
        return ref[0, :, slot * BLOCK : (slot + 1) * BLOCK]

    def gather(which, at):
        rows = slice(at * BLOCK, (at + 1) * BLOCK)
        return jnp.concatenate(
            [piece(qg, which, 2 * half + at)]
            + [near(is_second, qg, later[0], which, 2 * half + at, d) for d in NEAR]
            + [f[0][which, rows, :] for f in later[1:]],
            axis=0,
        )

    def gather_stats(slot):
        parts = [stat_of(stat, slot)]
        for d in NEAR:
            options = [
                stat_of(stat if here else later_stats[0], s) for here, s in near_slots(d, slot)
            ]
            parts.append(jnp.where(is_second, options[1], options[0]))
        return jnp.concatenate(parts + [stat_of(f, slot) for f in later_stats[1:]], axis=1)

    both = range(2)
    rows = [slice(at * BLOCK, (at + 1) * BLOCK) for at in both]
    queries = [gather(0, at) for at in both]
    grads = [gather(1, at) for at in both]
    stats = [gather_stats(2 * half + at) for at in both]
    score = [dot(kv[0, rows[at], :], queries[at], NT) * factor for at in both]
    grad_prob = [dot(kv[1, rows[at], :], grads[at], NT) for at in both]
    score = [jnp.concatenate([s[:, :BLOCK] + causal, s[:, BLOCK:]], axis=1) for s in score]
    prob = [jnp.exp(score[at] - stats[at][0:1]) for at in both]
    grad_score = [(prob[at] * (grad_prob[at] - stats[at][1:2])).astype(BF16) for at in both]
    prob_b = [p.astype(BF16) for p in prob]
    grad_keys = [dot(grad_score[at], queries[at], NN) * factor for at in both]
    grad_values = [dot(prob_b[at], grads[at], NN) for at in both]
    for at in both:
        out_ref[0, rows[at], :] = grad_keys[at].astype(BF16)
        out_ref[1, rows[at], :] = grad_values[at].astype(BF16)


def head_spec(a):
    if a.ndim == 2:
        return pl.BlockSpec((a.shape[0], HD), lambda h, w: (0, h))
    return pl.BlockSpec((a.shape[0], a.shape[1], HD), lambda h, w: (0, 0, h))


def stat_spec(a):
    return pl.BlockSpec((1,) + a.shape[1:], lambda h, w: (h, 0, 0))


def call(kernel, where, operands, in_specs, outs, out_specs, heads, keys, name):
    rows = outs[0].shape[-2]
    return pl.pallas_call(
        kernel,
        out_shape=outs,
        grid_spec=pltpu.PrefetchScalarGridSpec(
            num_scalar_prefetch=1, grid=(heads,), in_specs=in_specs, out_specs=out_specs
        ),
        compiler_params=pltpu.CompilerParams(vmem_limit_bytes=10 * 2**20),
        cost_estimate=pl.CostEstimate(
            flops=4 * 2 * rows * keys * HD * heads,
            bytes_accessed=6 * 2**20,
            transcendentals=rows * keys * heads,
        ),
        name=name,
    )(where, *operands)


def query_side(where, bias, qg, kv, fetched, n_back):
    rows, width = 2 * qg[0].shape[1], qg[0].shape[2]
    heads = width // HD
    far = [pltpu.with_memory_space_constraint(a, pltpu.HBM) for f in fetched for a in f]
    operands = [*qg, *kv, *far]
    row_out = jax.ShapeDtypeStruct((rows, width), BF16)
    stat_out = jax.ShapeDtypeStruct((heads, 2, rows), F32)
    back_out = jax.ShapeDtypeStruct((2, rows, width), BF16)
    outs = [row_out, row_out, stat_out] + [back_out] * n_back
    return call(
        functools.partial(query_kernel, tuple(len(f) for f in fetched), n_back),
        where,
        [bias, *operands],
        [pl.BlockSpec(bias.shape, lambda h, w: (0, 0, 0))] + [head_spec(a) for a in operands],
        outs,
        [head_spec(row_out), head_spec(row_out), stat_spec(stat_out)] + [head_spec(back_out)] * n_back,
        heads,
        bias.shape[2],
        "query_side",
    )


def key_side(half, where, kv, qg, stat, later, later_stats):
    rows, width = kv[0].shape[1], kv[0].shape[2]
    heads = width // HD
    half_of_whole = pl.BlockSpec((2, rows, HD), lambda h, w: (0, half, h))
    far = [f[-1] if len(f) == 1 else f[half] for f in later[1:]]
    operands = [kv[half], *qg, stat, *later[0], *far, *later_stats]
    in_specs = (
        [head_spec(a) for a in (kv[half], *qg)]
        + [stat_spec(stat)]
        + [head_spec(a) for a in later[0]]
        + [half_of_whole if len(f) == 1 else head_spec(f[half]) for f in later[1:]]
        + [stat_spec(a) for a in later_stats]
    )
    out = jax.ShapeDtypeStruct((2, rows, width), BF16)
    groups = (len(later[0]),) + (1,) * len(far)
    (result,) = call(
        functools.partial(key_kernel, half, groups),
        where,
        operands,
        in_specs,
        [out],
        [head_spec(out)],
        heads,
        (4 + len(far)) * BLOCK,
        "key_side",
    )
    return result


def matmul(a, b):
    return jnp.dot(a, b, preferred_element_type=F32)


def matmul_t(a, b):
    return lax.dot_general(a, b, NT, preferred_element_type=F32)


def swapped(own, passed, bit, sign):
    size = lax.axis_size("seq")
    high = (lax.axis_index("seq") // bit) % 2 == 1
    sent = jnp.where(high, passed, own) if sign > 0 else jnp.where(high, own, passed)
    return lax.ppermute(sent, "seq", [(i, i ^ bit) for i in range(size)])


def exchange(rows, sign):
    two = shifted(rows, sign * 2)
    far = shifted(rows, sign * 32)
    four = shifted(two, sign * 2)
    eight = shifted(four, sign * 4)
    sixteen = swapped(rows, far, 16, sign)
    two_last = two
    if sign > 0:
        two_last, eight = lax.optimization_barrier((two, eight))
    one = swapped(rows, two_last, 1, sign)
    return [one, two, four, eight, sixteen, far, shifted(far, sign * 32)]


def exchange_stats(stat):
    two, far = shifted(stat, -2), shifted(stat, -32)
    direct = [shifted(stat, -by) for by in (64, 8, 4)]
    one = swapped(stat, two, 1, -1)
    sixteen = swapped(stat, far, 16, -1)
    return [one, two, direct[2], direct[1], sixteen, far, direct[0]]


def per_device(series, norm_gain, w_query, w_key, w_value, w_out, out_grad):
    levels = lax.axis_size("seq").bit_length() - 1
    half = series.shape[0]
    blocks = 2 * half // BLOCK
    tp_index = lax.axis_index("tp").astype(jnp.int32)
    seq_index = lax.axis_index("seq").astype(jnp.int32)
    where = tp_index[None]
    slots = jnp.arange(blocks, dtype=jnp.int32)
    global_block = seq_index * blocks + (slots + 2 * tp_index) % blocks
    distances = [1, 2, 4] + [blocks * 2**s for s in range(1, levels)]
    reach = jnp.repeat(jnp.array([0] + distances, jnp.int32), BLOCK)
    bias = jnp.where(global_block[:, None] >= reach[None], 0.0, NEG).astype(F32)[:, None, :]

    series_f = series.astype(F32)
    inv_rms = lax.rsqrt(jnp.mean(series_f * series_f, axis=-1, keepdims=True) + EPS)
    unit_rows = series_f * inv_rms
    normed = (unit_rows * norm_gain).astype(BF16)
    normed_other = swap_tp(normed)
    out_grad_other = swap_tp(out_grad)

    def key_value(rows):
        return jnp.stack([matmul(rows, w_key).astype(BF16), matmul(rows, w_value).astype(BF16)])

    def query_grad(rows, grad_rows):
        return jnp.stack(
            [matmul(rows, w_query).astype(BF16), matmul_t(grad_rows, w_out).astype(BF16)]
        )

    kv = (key_value(normed), key_value(normed_other))
    qg = (query_grad(normed, out_grad), query_grad(normed_other, out_grad_other))
    kv_all = jnp.concatenate(kv, axis=1)
    qg_all = jnp.concatenate(qg, axis=1)
    fetched = exchange(kv_all, 1)
    later = exchange(qg_all, -1)
    mixed, grad_query, stat = query_side(where, bias, qg, kv, [(f,) for f in fetched], 0)
    last = later.pop(3)
    stat, later = lax.optimization_barrier((stat, later))
    later.insert(3, last)
    later = [(f,) for f in later]
    later_stats = exchange_stats(stat)
    attn_other = swap_tp(matmul(mixed[half:], w_out).astype(BF16))
    attn_rows = matmul(mixed[:half], w_out) + attn_other.astype(F32)
    layer_out = (series_f + attn_rows).astype(BF16)

    grad_queries = lax.optimization_barrier(matmul_t(grad_query, w_query))

    def back(at):
        grad_kv = key_side(at, where, kv, qg, stat, later, later_stats)
        rows = slice(at * half, (at + 1) * half)
        return (
            grad_queries[rows]
            + matmul_t(grad_kv[0], w_key)
            + matmul_t(grad_kv[1], w_value)
        )

    normed_grad_other = swap_tp(back(1).astype(BF16))
    normed_grad = back(0) + normed_grad_other.astype(F32)
    scaled = normed_grad * norm_gain
    series_grad = out_grad.astype(F32) + inv_rms * (
        scaled - unit_rows * jnp.mean(scaled * unit_rows, axis=-1, keepdims=True)
    )
    return (layer_out, series_grad.astype(BF16))


def solution(mesh):
    rows = P(("seq", "tp"), None)
    columns = P(None, "tp")
    in_specs = (rows, P(), columns, columns, columns, P("tp", None), rows)
    return jax.shard_map(
        per_device, mesh=mesh, in_specs=in_specs, out_specs=(rows, rows), check_vma=False
    )
```

```python
import functools

import jax
import jax.numpy as jnp
from jax import lax
from jax.experimental import pallas as pl
from jax.experimental.pallas import tpu as pltpu
from jax.sharding import PartitionSpec as P

HD = 128
BLOCK = 64
NEG = -1e30
EPS = 1e-06
F32 = jnp.float32
BF16 = jnp.bfloat16
NN = (((1,), (0,)), ((), ()))
NT = (((1,), (1,)), ((), ()))
TN = (((0,), (0,)), ((), ()))
NEAR = (1, 2, 4)


def shifted(value, by):
    size = lax.axis_size("seq")
    pairs = [(i, i + by) for i in range(size) if 0 <= i + by < size]
    return lax.ppermute(value, "seq", pairs)


def swap_tp(value):
    return lax.ppermute(value, "tp", [(0, 1), (1, 0)])


def dot(a, b, dims):
    return lax.dot_general(a, b, dims, preferred_element_type=F32)


def piece(pieces, which, slot):
    per = 4 // len(pieces)
    at = (slot % per) * BLOCK
    return pieces[slot // per][which, at : at + BLOCK, :]


def near_slots(step, slot):
    found = []
    for turn in (0, 2):
        block = (slot + turn) % 4 + step
        found.append((0 <= block < 4, (block + turn) % 4))
    return found


def near(is_second, own, other, which, slot, step):
    options = [
        piece(own if here else other, which, at) for here, at in near_slots(step, slot)
    ]
    return jnp.where(is_second, options[1], options[0])


def causal_bias(query_axis):
    rows = lax.broadcasted_iota(jnp.int32, (BLOCK, BLOCK), query_axis)
    keys = lax.broadcasted_iota(jnp.int32, (BLOCK, BLOCK), 1 - query_axis)
    return jnp.where(rows >= keys, 0.0, NEG).astype(F32)


def query_kernel(groups, n_back, where_ref, bias_ref, *refs):
    refs = list(refs)
    qg = [refs.pop(0) for _ in range(2)]
    kv = [refs.pop(0) for _ in range(2)]
    fetched = [[refs.pop(0) for _ in range(n)] for n in groups]
    mixed_ref, dq_ref, stat_ref, *back_refs = refs
    is_second = where_ref[0] == 1
    factor = HD ** (-0.5)
    causal = causal_bias(0)
    lane = lax.broadcasted_iota(jnp.int32, (BLOCK, HD), 1)
    slots = range(4)

    def gather(which, slot):
        return jnp.concatenate(
            [piece(kv, which, slot)]
            + [near(is_second, kv, fetched[0], which, slot, -d) for d in NEAR]
            + [piece(f, which, slot) for f in fetched[1:]],
            axis=0,
        )

    def rows(slot):
        return slice(slot * BLOCK, (slot + 1) * BLOCK)

    query = [piece(qg, 0, slot) for slot in slots]
    grad = [piece(qg, 1, slot) for slot in slots]
    keys = [gather(0, slot) for slot in slots]
    values = [gather(1, slot) for slot in slots]
    score = []
    for slot in slots:
        s = dot(query[slot], keys[slot], NT) * factor + bias_ref[slot]
        score.append(jnp.concatenate([s[:, :BLOCK] + causal, s[:, BLOCK:]], axis=1))
    grad_prob = [dot(grad[slot], values[slot], NT) for slot in slots]
    peak = [jnp.max(s, axis=-1, keepdims=True) for s in score]
    weight = [jnp.exp(score[slot] - peak[slot]) for slot in slots]
    total = [jnp.sum(w, axis=-1, keepdims=True) for w in weight]
    prob = [weight[slot] * (1.0 / total[slot]) for slot in slots]
    prob_b = [p.astype(BF16) for p in prob]
    mixed = [dot(prob_b[slot], values[slot], NN).astype(BF16) for slot in slots]
    inner = [
        jnp.sum(mixed[slot].astype(F32) * grad[slot].astype(F32), axis=-1, keepdims=True)
        for slot in slots
    ]
    grad_score = [
        (prob[slot] * (grad_prob[slot] - inner[slot])).astype(BF16) for slot in slots
    ]
    first = keys[0].shape[0] - n_back * BLOCK
    for slot in slots:
        out = rows(slot)
        mixed_ref[out, :] = mixed[slot]
        dq_ref[out, :] = (dot(grad_score[slot], keys[slot], NN) * factor).astype(BF16)
        stat = jnp.where(lane == 0, peak[slot] + jnp.log(total[slot]), inner[slot])
        stat_ref[0, :, out] = jnp.transpose(stat)[:2]
        if n_back:
            grad_keys = (dot(grad_score[slot][:, first:], query[slot], TN) * factor).astype(BF16)
            grad_values = dot(prob_b[slot][:, first:], grad[slot], TN).astype(BF16)
            for at, ref in enumerate(back_refs):
                ref[0, out, :] = grad_keys[at * BLOCK : (at + 1) * BLOCK]
                ref[1, out, :] = grad_values[at * BLOCK : (at + 1) * BLOCK]


def key_kernel(half, groups, where_ref, *refs):
    refs = list(refs)
    kv = refs.pop(0)
    qg = [refs.pop(0) for _ in range(2)]
    stat = refs.pop(0)
    later = [[refs.pop(0) for _ in range(n)] for n in groups]
    later_stats = [refs.pop(0) for _ in groups]
    (out_ref,) = refs
    is_second = where_ref[0] == 1
    factor = HD ** (-0.5)
    causal = causal_bias(1)

    def stat_of(ref, slot):
        return ref[0, :, slot * BLOCK : (slot + 1) * BLOCK]

    def gather(which, at):
        rows = slice(at * BLOCK, (at + 1) * BLOCK)
        return jnp.concatenate(
            [piece(qg, which, 2 * half + at)]
            + [near(is_second, qg, later[0], which, 2 * half + at, d) for d in NEAR]
            + [f[0][which, rows, :] for f in later[1:]],
            axis=0,
        )

    def gather_stats(slot):
        parts = [stat_of(stat, slot)]
        for d in NEAR:
            options = [
                stat_of(stat if here else later_stats[0], s) for here, s in near_slots(d, slot)
            ]
            parts.append(jnp.where(is_second, options[1], options[0]))
        return jnp.concatenate(parts + [stat_of(f, slot) for f in later_stats[1:]], axis=1)

    both = range(2)
    rows = [slice(at * BLOCK, (at + 1) * BLOCK) for at in both]
    queries = [gather(0, at) for at in both]
    grads = [gather(1, at) for at in both]
    stats = [gather_stats(2 * half + at) for at in both]
    score = [dot(kv[0, rows[at], :], queries[at], NT) * factor for at in both]
    grad_prob = [dot(kv[1, rows[at], :], grads[at], NT) for at in both]
    score = [jnp.concatenate([s[:, :BLOCK] + causal, s[:, BLOCK:]], axis=1) for s in score]
    prob = [jnp.exp(score[at] - stats[at][0:1]) for at in both]
    grad_score = [(prob[at] * (grad_prob[at] - stats[at][1:2])).astype(BF16) for at in both]
    prob_b = [p.astype(BF16) for p in prob]
    grad_keys = [dot(grad_score[at], queries[at], NN) * factor for at in both]
    grad_values = [dot(prob_b[at], grads[at], NN) for at in both]
    for at in both:
        out_ref[0, rows[at], :] = grad_keys[at].astype(BF16)
        out_ref[1, rows[at], :] = grad_values[at].astype(BF16)


def head_spec(a):
    if a.ndim == 2:
        return pl.BlockSpec((a.shape[0], HD), lambda h, w: (0, h))
    return pl.BlockSpec((a.shape[0], a.shape[1], HD), lambda h, w: (0, 0, h))


def stat_spec(a):
    return pl.BlockSpec((1,) + a.shape[1:], lambda h, w: (h, 0, 0))


def call(kernel, where, operands, in_specs, outs, out_specs, heads, keys, name):
    rows = outs[0].shape[-2]
    return pl.pallas_call(
        kernel,
        out_shape=outs,
        grid_spec=pltpu.PrefetchScalarGridSpec(
            num_scalar_prefetch=1, grid=(heads,), in_specs=in_specs, out_specs=out_specs
        ),
        compiler_params=pltpu.CompilerParams(vmem_limit_bytes=10 * 2**20),
        cost_estimate=pl.CostEstimate(
            flops=rows * keys, bytes_accessed=2**16, transcendentals=0
        ),
        name=name,
    )(where, *operands)


def query_side(where, bias, qg, kv, fetched, n_back):
    rows, width = 2 * qg[0].shape[1], qg[0].shape[2]
    heads = width // HD
    far = [pltpu.with_memory_space_constraint(a, pltpu.HBM) for f in fetched for a in f]
    operands = [*qg, *kv, *far]
    row_out = jax.ShapeDtypeStruct((rows, width), BF16)
    stat_out = jax.ShapeDtypeStruct((heads, 2, rows), F32)
    back_out = jax.ShapeDtypeStruct((2, rows, width), BF16)
    outs = [row_out, row_out, stat_out] + [back_out] * n_back
    return call(
        functools.partial(query_kernel, tuple(len(f) for f in fetched), n_back),
        where,
        [bias, *operands],
        [pl.BlockSpec(bias.shape, lambda h, w: (0, 0, 0))] + [head_spec(a) for a in operands],
        outs,
        [head_spec(row_out), head_spec(row_out), stat_spec(stat_out)] + [head_spec(back_out)] * n_back,
        heads,
        bias.shape[2],
        "query_side",
    )


def key_side(half, where, kv, qg, stat, later, later_stats):
    rows, width = kv[0].shape[1], kv[0].shape[2]
    heads = width // HD
    half_of_whole = pl.BlockSpec((2, rows, HD), lambda h, w: (0, half, h))
    far = [f[-1] if len(f) == 1 else f[half] for f in later[1:]]
    operands = [kv[half], *qg, stat, *later[0], *far, *later_stats]
    in_specs = (
        [head_spec(a) for a in (kv[half], *qg)]
        + [stat_spec(stat)]
        + [head_spec(a) for a in later[0]]
        + [half_of_whole if len(f) == 1 else head_spec(f[half]) for f in later[1:]]
        + [stat_spec(a) for a in later_stats]
    )
    out = jax.ShapeDtypeStruct((2, rows, width), BF16)
    groups = (len(later[0]),) + (1,) * len(far)
    (result,) = call(
        functools.partial(key_kernel, half, groups),
        where,
        operands,
        in_specs,
        [out],
        [head_spec(out)],
        heads,
        (4 + len(far)) * BLOCK,
        "key_side",
    )
    return result


def matmul(a, b):
    return jnp.dot(a, b, preferred_element_type=F32)


def matmul_t(a, b):
    return lax.dot_general(a, b, NT, preferred_element_type=F32)


def swapped(own, passed, bit, sign):
    size = lax.axis_size("seq")
    high = (lax.axis_index("seq") // bit) % 2 == 1
    sent = jnp.where(high, passed, own) if sign > 0 else jnp.where(high, own, passed)
    return lax.ppermute(sent, "seq", [(i, i ^ bit) for i in range(size)])


def exchange(rows, sign):
    two = shifted(rows, sign * 2)
    far = shifted(rows, sign * 32)
    four = shifted(two, sign * 2)
    eight = shifted(four, sign * 4)
    sixteen = swapped(rows, far, 16, sign)
    two_last, eight = lax.optimization_barrier((two, eight))
    one = swapped(rows, two_last, 1, sign)
    return [one, two, four, eight, sixteen, far, shifted(far, sign * 32)]


def exchange_stats(stat):
    two, far = shifted(stat, -2), shifted(stat, -32)
    direct = [shifted(stat, -by) for by in (64, 8, 4)]
    one = swapped(stat, two, 1, -1)
    sixteen = swapped(stat, far, 16, -1)
    return [one, two, direct[2], direct[1], sixteen, far, direct[0]]


def per_device(series, norm_gain, w_query, w_key, w_value, w_out, out_grad):
    levels = lax.axis_size("seq").bit_length() - 1
    half = series.shape[0]
    blocks = 2 * half // BLOCK
    tp_index = lax.axis_index("tp").astype(jnp.int32)
    seq_index = lax.axis_index("seq").astype(jnp.int32)
    where = tp_index[None]
    slots = jnp.arange(blocks, dtype=jnp.int32)
    global_block = seq_index * blocks + (slots + 2 * tp_index) % blocks
    distances = [1, 2, 4] + [blocks * 2**s for s in range(1, levels)]
    reach = jnp.repeat(jnp.array([0] + distances, jnp.int32), BLOCK)
    bias = jnp.where(global_block[:, None] >= reach[None], 0.0, NEG).astype(F32)[:, None, :]

    series_f = series.astype(F32)
    inv_rms = lax.rsqrt(jnp.mean(series_f * series_f, axis=-1, keepdims=True) + EPS)
    unit_rows = series_f * inv_rms
    normed = (unit_rows * norm_gain).astype(BF16)
    normed_other, out_grad_other = swap_tp(jnp.stack([normed, out_grad]))

    def key_value(rows):
        return jnp.stack([matmul(rows, w_key).astype(BF16), matmul(rows, w_value).astype(BF16)])

    def query_grad(rows, grad_rows):
        return jnp.stack(
            [matmul(rows, w_query).astype(BF16), matmul_t(grad_rows, w_out).astype(BF16)]
        )

    kv = (key_value(normed), key_value(normed_other))
    qg = (query_grad(normed, out_grad), query_grad(normed_other, out_grad_other))
    kv_all, qg_all = lax.optimization_barrier(
        (jnp.concatenate(kv, axis=1), jnp.concatenate(qg, axis=1))
    )
    fetched = exchange(kv_all, 1)
    later = exchange(qg_all, -1)
    mixed, grad_query, stat = query_side(where, bias, qg, kv, [(f,) for f in fetched], 0)
    stat, later = lax.optimization_barrier((stat, later))
    later = [(f,) for f in later]
    later_stats = exchange_stats(stat)
    attn_other = swap_tp(matmul(mixed[half:], w_out).astype(BF16))
    attn_rows = matmul(mixed[:half], w_out) + attn_other.astype(F32)
    layer_out = (series_f + attn_rows).astype(BF16)

    grad_queries = lax.optimization_barrier(matmul_t(grad_query, w_query))

    def back(at):
        grad_kv = key_side(at, where, kv, qg, stat, later, later_stats)
        rows = slice(at * half, (at + 1) * half)
        return (
            grad_queries[rows]
            + matmul_t(grad_kv[0], w_key)
            + matmul_t(grad_kv[1], w_value)
        )

    normed_grad_other = swap_tp(back(1).astype(BF16))
    normed_grad = back(0) + normed_grad_other.astype(F32)
    scaled = normed_grad * norm_gain
    series_grad = out_grad.astype(F32) + inv_rms * (
        scaled - unit_rows * jnp.mean(scaled * unit_rows, axis=-1, keepdims=True)
    )
    return (layer_out, series_grad.astype(BF16))


def solution(mesh):
    rows = P(("seq", "tp"), None)
    columns = P(None, "tp")
    in_specs = (rows, P(), columns, columns, columns, P("tp", None), rows)
    return jax.shard_map(
        per_device, mesh=mesh, in_specs=in_specs, out_specs=(rows, rows), check_vma=False
    )
```

```python
import functools

import jax
import jax.numpy as jnp
from jax import lax
from jax.experimental import pallas as pl
from jax.experimental.pallas import tpu as pltpu
from jax.sharding import PartitionSpec as P

HD = 128
BLOCK = 64
NEG = -1e30
EPS = 1e-06
F32 = jnp.float32
BF16 = jnp.bfloat16
NN = (((1,), (0,)), ((), ()))
NT = (((1,), (1,)), ((), ()))
TN = (((0,), (0,)), ((), ()))
NEAR = (1, 2, 4)


def shifted(value, by):
    size = lax.axis_size("seq")
    pairs = [(i, i + by) for i in range(size) if 0 <= i + by < size]
    return lax.ppermute(value, "seq", pairs)


def swap_tp(value):
    return lax.ppermute(value, "tp", [(0, 1), (1, 0)])


def dot(a, b, dims):
    return lax.dot_general(a, b, dims, preferred_element_type=F32)


def piece(pieces, which, slot):
    per = 4 // len(pieces)
    at = (slot % per) * BLOCK
    return pieces[slot // per][which, at : at + BLOCK, :]


def near_slots(step, slot):
    found = []
    for turn in (0, 2):
        block = (slot + turn) % 4 + step
        found.append((0 <= block < 4, (block + turn) % 4))
    return found


def near(is_second, own, other, which, slot, step):
    options = [
        piece(own if here else other, which, at) for here, at in near_slots(step, slot)
    ]
    return jnp.where(is_second, options[1], options[0])


def causal_bias(query_axis):
    rows = lax.broadcasted_iota(jnp.int32, (BLOCK, BLOCK), query_axis)
    keys = lax.broadcasted_iota(jnp.int32, (BLOCK, BLOCK), 1 - query_axis)
    return jnp.where(rows >= keys, 0.0, NEG).astype(F32)


def query_kernel(groups, n_back, where_ref, *refs):
    refs = list(refs)
    qg, kv = [refs.pop(0)], [refs.pop(0)]
    fetched = [[refs.pop(0) for _ in range(n)] for n in groups]
    mixed_ref, dq_ref, stat_ref, *back_refs = refs
    is_second = where_ref[0] == 1
    factor = HD ** (-0.5)
    causal = causal_bias(0)
    lane = lax.broadcasted_iota(jnp.int32, (BLOCK, HD), 1)
    slots = range(4)

    def gather(which, slot):
        return jnp.concatenate(
            [piece(kv, which, slot)]
            + [near(is_second, kv, fetched[0], which, slot, -d) for d in NEAR]
            + [piece(f, which, slot) for f in fetched[1:]],
            axis=0,
        )

    def rows(slot):
        return slice(slot * BLOCK, (slot + 1) * BLOCK)

    part = lax.broadcasted_iota(jnp.int32, (1, (4 + len(groups) - 1) * BLOCK), 1) // BLOCK
    reach = jnp.where(part == 0, 0, jnp.left_shift(1, jnp.maximum(part - 1, 0)))
    query = [piece(qg, 0, slot) for slot in slots]
    grad = [piece(qg, 1, slot) for slot in slots]
    keys = [gather(0, slot) for slot in slots]
    values = [gather(1, slot) for slot in slots]
    score = []
    for slot in slots:
        block = where_ref[1] + (slot + 2 * where_ref[0]) % 4
        s = dot(query[slot], keys[slot], NT) * factor + jnp.where(reach <= block, 0.0, NEG)
        score.append(jnp.concatenate([s[:, :BLOCK] + causal, s[:, BLOCK:]], axis=1))
    grad_prob = [dot(grad[slot], values[slot], NT) for slot in slots]
    peak = [jnp.max(s, axis=-1, keepdims=True) for s in score]
    weight = [jnp.exp(score[slot] - peak[slot]) for slot in slots]
    total = [jnp.sum(w, axis=-1, keepdims=True) for w in weight]
    prob = [weight[slot] * (1.0 / total[slot]) for slot in slots]
    prob_b = [p.astype(BF16) for p in prob]
    mixed = [dot(prob_b[slot], values[slot], NN).astype(BF16) for slot in slots]
    inner = [
        jnp.sum(mixed[slot].astype(F32) * grad[slot].astype(F32), axis=-1, keepdims=True)
        for slot in slots
    ]
    grad_score = [
        (prob[slot] * (grad_prob[slot] - inner[slot])).astype(BF16) for slot in slots
    ]
    first = keys[0].shape[0] - n_back * BLOCK
    for slot in slots:
        out = rows(slot)
        mixed_ref[out, :] = mixed[slot]
        dq_ref[out, :] = (dot(grad_score[slot], keys[slot], NN) * factor).astype(BF16)
        stat = jnp.where(lane == 0, peak[slot] + jnp.log(total[slot]), inner[slot])
        stat_ref[0, :, out] = jnp.transpose(stat)[:2]
        if n_back:
            grad_keys = (dot(grad_score[slot][:, first:], query[slot], TN) * factor).astype(BF16)
            grad_values = dot(prob_b[slot][:, first:], grad[slot], TN).astype(BF16)
            for at, ref in enumerate(back_refs):
                ref[0, out, :] = grad_keys[at * BLOCK : (at + 1) * BLOCK]
                ref[1, out, :] = grad_values[at * BLOCK : (at + 1) * BLOCK]


def key_kernel(half, groups, where_ref, *refs):
    refs = list(refs)
    kv = refs.pop(0)
    qg = [refs.pop(0)]
    stat = refs.pop(0)
    later = [[refs.pop(0) for _ in range(n)] for n in groups]
    later_stats = [refs.pop(0) for _ in groups]
    (out_ref,) = refs
    is_second = where_ref[0] == 1
    factor = HD ** (-0.5)
    causal = causal_bias(1)

    def stat_of(ref, slot):
        return ref[0, :, slot * BLOCK : (slot + 1) * BLOCK]

    def gather(which, at):
        rows = slice(at * BLOCK, (at + 1) * BLOCK)
        return jnp.concatenate(
            [piece(qg, which, 2 * half + at)]
            + [near(is_second, qg, later[0], which, 2 * half + at, d) for d in NEAR]
            + [f[0][which, rows, :] for f in later[1:]],
            axis=0,
        )

    def gather_stats(slot):
        parts = [stat_of(stat, slot)]
        for d in NEAR:
            options = [
                stat_of(stat if here else later_stats[0], s) for here, s in near_slots(d, slot)
            ]
            parts.append(jnp.where(is_second, options[1], options[0]))
        return jnp.concatenate(parts + [stat_of(f, slot) for f in later_stats[1:]], axis=1)

    both = range(2)
    rows = [slice(at * BLOCK, (at + 1) * BLOCK) for at in both]
    queries = [gather(0, at) for at in both]
    grads = [gather(1, at) for at in both]
    stats = [gather_stats(2 * half + at) for at in both]
    score = [dot(kv[0, rows[at], :], queries[at], NT) * factor for at in both]
    grad_prob = [dot(kv[1, rows[at], :], grads[at], NT) for at in both]
    score = [jnp.concatenate([s[:, :BLOCK] + causal, s[:, BLOCK:]], axis=1) for s in score]
    prob = [jnp.exp(score[at] - stats[at][0:1]) for at in both]
    grad_score = [(prob[at] * (grad_prob[at] - stats[at][1:2])).astype(BF16) for at in both]
    prob_b = [p.astype(BF16) for p in prob]
    grad_keys = [dot(grad_score[at], queries[at], NN) * factor for at in both]
    grad_values = [dot(prob_b[at], grads[at], NN) for at in both]
    for at in both:
        out_ref[0, rows[at], :] = grad_keys[at].astype(BF16)
        out_ref[1, rows[at], :] = grad_values[at].astype(BF16)


def head_spec(a):
    if a.ndim == 2:
        return pl.BlockSpec((a.shape[0], HD), lambda h, w: (0, h))
    return pl.BlockSpec((a.shape[0], a.shape[1], HD), lambda h, w: (0, 0, h))


def stat_spec(a):
    return pl.BlockSpec((1,) + a.shape[1:], lambda h, w: (h, 0, 0))


def call(kernel, where, operands, in_specs, outs, out_specs, heads, keys, name):
    rows = outs[0].shape[-2]
    return pl.pallas_call(
        kernel,
        out_shape=outs,
        grid_spec=pltpu.PrefetchScalarGridSpec(
            num_scalar_prefetch=1, grid=(heads,), in_specs=in_specs, out_specs=out_specs
        ),
        compiler_params=pltpu.CompilerParams(vmem_limit_bytes=6 * 2**20),
        cost_estimate=pl.CostEstimate(
            flops=rows * keys, bytes_accessed=2**16, transcendentals=0
        ),
        name=name,
    )(where, *operands)


def query_side(where, qg, kv, fetched, n_back):
    rows, width = qg.shape[1], qg.shape[2]
    heads = width // HD
    far = [a for f in fetched for a in f]
    operands = [qg, kv, *far]
    row_out = jax.ShapeDtypeStruct((rows, width), BF16)
    stat_out = jax.ShapeDtypeStruct((heads, 2, rows), F32)
    back_out = jax.ShapeDtypeStruct((2, rows, width), BF16)
    outs = [row_out, row_out, stat_out] + [back_out] * n_back
    return call(
        functools.partial(query_kernel, tuple(len(f) for f in fetched), n_back),
        where,
        operands,
        [head_spec(a) for a in operands],
        outs,
        [head_spec(row_out), head_spec(row_out), stat_spec(stat_out)] + [head_spec(back_out)] * n_back,
        heads,
        (3 + len(fetched)) * BLOCK,
        "query_side",
    )


def key_side(half, where, kv, qg, stat, later, later_stats):
    rows, width = kv.shape[1] // 2, kv.shape[2]
    heads = width // HD
    half_of_whole = pl.BlockSpec((2, rows, HD), lambda h, w: (0, half, h))
    far = [f[-1] if len(f) == 1 else f[half] for f in later[1:]]
    first, *far = [pltpu.with_memory_space_constraint(a, pltpu.HBM) for a in (*later[0], *far)]
    operands = [kv, qg, stat, first, *far, *later_stats]
    in_specs = (
        [half_of_whole, head_spec(qg)]
        + [stat_spec(stat)]
        + [head_spec(a) for a in later[0]]
        + [half_of_whole if len(f) == 1 else head_spec(f[half]) for f in later[1:]]
        + [stat_spec(a) for a in later_stats]
    )
    out = jax.ShapeDtypeStruct((2, rows, width), BF16)
    groups = (len(later[0]),) + (1,) * len(far)
    (result,) = call(
        functools.partial(key_kernel, half, groups),
        where,
        operands,
        in_specs,
        [out],
        [head_spec(out)],
        heads,
        (4 + len(far)) * BLOCK,
        "key_side",
    )
    return result


def norm_kernel(series_ref, gain_ref, grad_ref, sent_ref, inv_ref):
    rows = series_ref[...].astype(F32)
    inv_rms = lax.rsqrt(jnp.mean(rows * rows, axis=-1, keepdims=True) + EPS)
    inv_ref[...] = inv_rms
    sent_ref[0] = (rows * inv_rms * gain_ref[...]).astype(BF16)
    sent_ref[1] = grad_ref[...]


def normalize(series, gain, out_grad):
    rows, width = series.shape
    step = rows // 4
    row_spec = pl.BlockSpec((step, width), lambda i: (i, 0))
    return pl.pallas_call(
        norm_kernel,
        out_shape=[
            jax.ShapeDtypeStruct((2, rows, width), BF16),
            jax.ShapeDtypeStruct((rows, 1), F32),
        ],
        grid=(4,),
        in_specs=[row_spec, pl.BlockSpec((1, width), lambda i: (0, 0)), row_spec],
        out_specs=[
            pl.BlockSpec((2, step, width), lambda i: (0, i, 0)),
            pl.BlockSpec((step, 1), lambda i: (i, 0)),
        ],
        compiler_params=pltpu.CompilerParams(vmem_limit_bytes=6 * 2**20),
        name="normalize",
    )(series, gain[None], out_grad)


def matmul(a, b):
    return jnp.dot(a, b, preferred_element_type=F32)


def matmul_t(a, b):
    return lax.dot_general(a, b, NT, preferred_element_type=F32)


def swapped(own, passed, bit, sign):
    size = lax.axis_size("seq")
    high = (lax.axis_index("seq") // bit) % 2 == 1
    sent = jnp.where(high, passed, own) if sign > 0 else jnp.where(high, own, passed)
    return lax.ppermute(sent, "seq", [(i, i ^ bit) for i in range(size)])


def exchange(rows, sign):
    two = shifted(rows, sign * 2)
    far = shifted(rows, sign * 32)
    four = shifted(two, sign * 2)
    eight = shifted(four, sign * 4)
    sixteen = swapped(rows, far, 16, sign)
    rows_last, two_last, eight = lax.optimization_barrier((rows, two, eight))
    one = swapped(rows_last, two_last, 1, sign)
    return [one, two, four, eight, sixteen, far, shifted(far, sign * 32)]


def exchange_stats(stat, attn_other):
    two, far = shifted(stat, -2), shifted(stat, -32)
    direct = [shifted(stat, -by) for by in (64, 8, 4)]
    sixteen = swapped(stat, far, 16, -1)
    two_last, attn_other = lax.optimization_barrier((two, attn_other))
    one = swapped(stat, two_last, 1, -1)
    return attn_other, [one, two, direct[2], direct[1], sixteen, far, direct[0]]


def per_device(series, norm_gain, w_query, w_key, w_value, w_out, out_grad):
    levels = lax.axis_size("seq").bit_length() - 1
    half = series.shape[0]
    blocks = 2 * half // BLOCK
    tp_index = lax.axis_index("tp").astype(jnp.int32)
    seq_index = lax.axis_index("seq").astype(jnp.int32)
    where = jnp.stack([tp_index, seq_index * blocks])
    series_f = series.astype(F32)
    sent, inv_rms = normalize(series, norm_gain, out_grad)
    normed = sent[0]
    unit_rows = series_f * inv_rms
    normed_other, out_grad_other = swap_tp(sent)

    def key_value(rows):
        return jnp.stack([matmul(rows, w_key).astype(BF16), matmul(rows, w_value).astype(BF16)])

    def query_grad(rows, grad_rows):
        return jnp.stack(
            [matmul(rows, w_query).astype(BF16), matmul_t(grad_rows, w_out).astype(BF16)]
        )

    kv = (key_value(normed), key_value(normed_other))
    qg = (query_grad(normed, out_grad), query_grad(normed_other, out_grad_other))
    kv_all, qg_all = lax.optimization_barrier(
        (jnp.concatenate(kv, axis=1), jnp.concatenate(qg, axis=1))
    )
    fetched = exchange(kv_all, 1)
    later = exchange(qg_all, -1)
    mixed, grad_query, stat = query_side(where, qg_all, kv_all, [(f,) for f in fetched], 0)
    stat, later = lax.optimization_barrier((stat, later))
    later = [(f,) for f in later]
    attn_other = swap_tp(matmul(mixed[half:], w_out).astype(BF16))
    attn_other, later_stats = exchange_stats(stat, attn_other)
    attn_rows = matmul(mixed[:half], w_out) + attn_other.astype(F32)
    layer_out = (series_f + attn_rows).astype(BF16)

    grad_queries = lax.optimization_barrier(matmul_t(grad_query, w_query))

    def back(at):
        grad_kv = key_side(at, where, kv_all, qg_all, stat, later, later_stats)
        rows = slice(at * half, (at + 1) * half)
        return (
            grad_queries[rows]
            + matmul_t(grad_kv[0], w_key)
            + matmul_t(grad_kv[1], w_value)
        )

    normed_grad_other = swap_tp(back(1).astype(BF16))
    normed_grad = back(0) + normed_grad_other.astype(F32)
    scaled = normed_grad * norm_gain
    series_grad = out_grad.astype(F32) + inv_rms * (
        scaled - unit_rows * jnp.mean(scaled * unit_rows, axis=-1, keepdims=True)
    )
    return (layer_out, series_grad.astype(BF16))


def solution(mesh):
    rows = P(("seq", "tp"), None)
    columns = P(None, "tp")
    in_specs = (rows, P(), columns, columns, columns, P("tp", None), rows)
    return jax.shard_map(
        per_device, mesh=mesh, in_specs=in_specs, out_specs=(rows, rows), check_vma=False
    )
```

```python
import functools

import jax
import jax.numpy as jnp
from jax import lax
from jax.experimental import pallas as pl
from jax.experimental.pallas import tpu as pltpu
from jax.sharding import PartitionSpec as P

HD = 128
BLOCK = 64
NEG = -1e30
EPS = 1e-06
F32 = jnp.float32
BF16 = jnp.bfloat16
NN = (((1,), (0,)), ((), ()))
NT = (((1,), (1,)), ((), ()))
TN = (((0,), (0,)), ((), ()))
NEAR = (1, 2, 4)


def shifted(value, by):
    size = lax.axis_size("seq")
    pairs = [(i, i + by) for i in range(size) if 0 <= i + by < size]
    return lax.ppermute(value, "seq", pairs)


def swap_tp(value):
    return lax.ppermute(value, "tp", [(0, 1), (1, 0)])


def dot(a, b, dims):
    return lax.dot_general(a, b, dims, preferred_element_type=F32)


def piece(pieces, which, slot):
    per = 4 // len(pieces)
    at = (slot % per) * BLOCK
    return pieces[slot // per][which, at : at + BLOCK, :]


def near_slots(step, slot):
    found = []
    for turn in (0, 2):
        block = (slot + turn) % 4 + step
        found.append((0 <= block < 4, (block + turn) % 4))
    return found


def near(is_second, own, other, which, slot, step):
    options = [
        piece(own if here else other, which, at) for here, at in near_slots(step, slot)
    ]
    return jnp.where(is_second, options[1], options[0])


def causal_bias(query_axis):
    rows = lax.broadcasted_iota(jnp.int32, (BLOCK, BLOCK), query_axis)
    keys = lax.broadcasted_iota(jnp.int32, (BLOCK, BLOCK), 1 - query_axis)
    return jnp.where(rows >= keys, 0.0, NEG).astype(F32)


def query_kernel(groups, n_back, where_ref, *refs):
    refs = list(refs)
    qg, kv = [refs.pop(0)], [refs.pop(0)]
    fetched = [[refs.pop(0) for _ in range(n)] for n in groups]
    mixed_ref, dq_ref, stat_ref, *back_refs = refs
    is_second = where_ref[0] == 1
    factor = HD ** (-0.5)
    causal = causal_bias(0)
    lane = lax.broadcasted_iota(jnp.int32, (BLOCK, HD), 1)
    slots = range(4)

    def gather(which, slot):
        return jnp.concatenate(
            [piece(kv, which, slot)]
            + [near(is_second, kv, fetched[0], which, slot, -d) for d in NEAR]
            + [piece(f, which, slot) for f in fetched[1:]],
            axis=0,
        )

    def rows(slot):
        return slice(slot * BLOCK, (slot + 1) * BLOCK)

    part = lax.broadcasted_iota(jnp.int32, (1, (4 + len(groups) - 1) * BLOCK), 1) // BLOCK
    reach = jnp.where(part == 0, 0, jnp.left_shift(1, jnp.maximum(part - 1, 0)))
    query = [piece(qg, 0, slot) for slot in slots]
    grad = [piece(qg, 1, slot) for slot in slots]
    keys = [gather(0, slot) for slot in slots]
    values = [gather(1, slot) for slot in slots]
    score = []
    for slot in slots:
        block = where_ref[1] + (slot + 2 * where_ref[0]) % 4
        s = dot(query[slot], keys[slot], NT) * factor + jnp.where(reach <= block, 0.0, NEG)
        score.append(jnp.concatenate([s[:, :BLOCK] + causal, s[:, BLOCK:]], axis=1))
    grad_prob = [dot(grad[slot], values[slot], NT) for slot in slots]
    peak = [jnp.max(s, axis=-1, keepdims=True) for s in score]
    weight = [jnp.exp(score[slot] - peak[slot]) for slot in slots]
    total = [jnp.sum(w, axis=-1, keepdims=True) for w in weight]
    prob = [weight[slot] * (1.0 / total[slot]) for slot in slots]
    prob_b = [p.astype(BF16) for p in prob]
    mixed = [dot(prob_b[slot], values[slot], NN).astype(BF16) for slot in slots]
    inner = [
        jnp.sum(mixed[slot].astype(F32) * grad[slot].astype(F32), axis=-1, keepdims=True)
        for slot in slots
    ]
    grad_score = [
        (prob[slot] * (grad_prob[slot] - inner[slot])).astype(BF16) for slot in slots
    ]
    first = keys[0].shape[0] - n_back * BLOCK
    for slot in slots:
        out = rows(slot)
        mixed_ref[out, :] = mixed[slot]
        dq_ref[out, :] = (dot(grad_score[slot], keys[slot], NN) * factor).astype(BF16)
        stat = jnp.where(lane == 0, peak[slot] + jnp.log(total[slot]), inner[slot])
        stat_ref[0, :, out] = jnp.transpose(stat)[:2]
        if n_back:
            grad_keys = (dot(grad_score[slot][:, first:], query[slot], TN) * factor).astype(BF16)
            grad_values = dot(prob_b[slot][:, first:], grad[slot], TN).astype(BF16)
            for at, ref in enumerate(back_refs):
                ref[0, out, :] = grad_keys[at * BLOCK : (at + 1) * BLOCK]
                ref[1, out, :] = grad_values[at * BLOCK : (at + 1) * BLOCK]


def key_kernel(half, groups, where_ref, *refs):
    refs = list(refs)
    kv = refs.pop(0)
    qg = [refs.pop(0)]
    stat = refs.pop(0)
    later = [[refs.pop(0) for _ in range(n)] for n in groups]
    later_stats = [refs.pop(0) for _ in groups]
    (out_ref,) = refs
    is_second = where_ref[0] == 1
    factor = HD ** (-0.5)
    causal = causal_bias(1)

    def stat_of(ref, slot):
        return ref[0, :, slot * BLOCK : (slot + 1) * BLOCK]

    def gather(which, at):
        rows = slice(at * BLOCK, (at + 1) * BLOCK)
        return jnp.concatenate(
            [piece(qg, which, 2 * half + at)]
            + [near(is_second, qg, later[0], which, 2 * half + at, d) for d in NEAR]
            + [f[0][which, rows, :] for f in later[1:]],
            axis=0,
        )

    def gather_stats(slot):
        parts = [stat_of(stat, slot)]
        for d in NEAR:
            options = [
                stat_of(stat if here else later_stats[0], s) for here, s in near_slots(d, slot)
            ]
            parts.append(jnp.where(is_second, options[1], options[0]))
        return jnp.concatenate(parts + [stat_of(f, slot) for f in later_stats[1:]], axis=1)

    both = range(2)
    rows = [slice(at * BLOCK, (at + 1) * BLOCK) for at in both]
    queries = [gather(0, at) for at in both]
    grads = [gather(1, at) for at in both]
    stats = [gather_stats(2 * half + at) for at in both]
    score = [dot(kv[0, rows[at], :], queries[at], NT) * factor for at in both]
    grad_prob = [dot(kv[1, rows[at], :], grads[at], NT) for at in both]
    score = [jnp.concatenate([s[:, :BLOCK] + causal, s[:, BLOCK:]], axis=1) for s in score]
    prob = [jnp.exp(score[at] - stats[at][0:1]) for at in both]
    grad_score = [(prob[at] * (grad_prob[at] - stats[at][1:2])).astype(BF16) for at in both]
    prob_b = [p.astype(BF16) for p in prob]
    grad_keys = [dot(grad_score[at], queries[at], NN) * factor for at in both]
    grad_values = [dot(prob_b[at], grads[at], NN) for at in both]
    for at in both:
        out_ref[0, rows[at], :] = grad_keys[at].astype(BF16)
        out_ref[1, rows[at], :] = grad_values[at].astype(BF16)


def head_spec(a):
    if a.ndim == 2:
        return pl.BlockSpec((a.shape[0], HD), lambda h, w: (0, h))
    return pl.BlockSpec((a.shape[0], a.shape[1], HD), lambda h, w: (0, 0, h))


def stat_spec(a):
    return pl.BlockSpec((1,) + a.shape[1:], lambda h, w: (h, 0, 0))


def call(kernel, where, operands, in_specs, outs, out_specs, heads, keys, name):
    rows = outs[0].shape[-2]
    return pl.pallas_call(
        kernel,
        out_shape=outs,
        grid_spec=pltpu.PrefetchScalarGridSpec(
            num_scalar_prefetch=1, grid=(heads,), in_specs=in_specs, out_specs=out_specs
        ),
        compiler_params=pltpu.CompilerParams(vmem_limit_bytes=6 * 2**20),
        cost_estimate=pl.CostEstimate(
            flops=rows * keys, bytes_accessed=2**16, transcendentals=0
        ),
        name=name,
    )(where, *operands)


def query_side(where, qg, kv, fetched, n_back):
    rows, width = qg.shape[1], qg.shape[2]
    heads = width // HD
    far = [a for f in fetched for a in f]
    operands = [qg, kv, *far]
    row_out = jax.ShapeDtypeStruct((rows, width), BF16)
    stat_out = jax.ShapeDtypeStruct((heads, 2, rows), F32)
    back_out = jax.ShapeDtypeStruct((2, rows, width), BF16)
    outs = [row_out, row_out, stat_out] + [back_out] * n_back
    return call(
        functools.partial(query_kernel, tuple(len(f) for f in fetched), n_back),
        where,
        operands,
        [head_spec(a) for a in operands],
        outs,
        [head_spec(row_out), head_spec(row_out), stat_spec(stat_out)] + [head_spec(back_out)] * n_back,
        heads,
        (3 + len(fetched)) * BLOCK,
        "query_side",
    )


def key_side(half, where, kv, qg, stat, later, later_stats):
    rows, width = kv.shape[1] // 2, kv.shape[2]
    heads = width // HD
    half_of_whole = pl.BlockSpec((2, rows, HD), lambda h, w: (0, half, h))
    far = [f[-1] if len(f) == 1 else f[half] for f in later[1:]]
    first, *far = [pltpu.with_memory_space_constraint(a, pltpu.HBM) for a in (*later[0], *far)]
    operands = [kv, qg, stat, first, *far, *later_stats]
    in_specs = (
        [half_of_whole, head_spec(qg)]
        + [stat_spec(stat)]
        + [head_spec(a) for a in later[0]]
        + [half_of_whole if len(f) == 1 else head_spec(f[half]) for f in later[1:]]
        + [stat_spec(a) for a in later_stats]
    )
    out = jax.ShapeDtypeStruct((2, rows, width), BF16)
    groups = (len(later[0]),) + (1,) * len(far)
    (result,) = call(
        functools.partial(key_kernel, half, groups),
        where,
        operands,
        in_specs,
        [out],
        [head_spec(out)],
        heads,
        (4 + len(far)) * BLOCK,
        "key_side",
    )
    return result


def norm_kernel(series_ref, gain_ref, grad_ref, sent_ref, inv_ref):
    rows = series_ref[...].astype(F32)
    inv_rms = lax.rsqrt(jnp.mean(rows * rows, axis=-1, keepdims=True) + EPS)
    inv_ref[...] = inv_rms
    sent_ref[0] = (rows * inv_rms * gain_ref[...]).astype(BF16)
    sent_ref[1] = grad_ref[...]


def normalize(series, gain, out_grad):
    rows, width = series.shape
    step = rows // 4
    series, out_grad = [
        pltpu.with_memory_space_constraint(a, pltpu.HBM) for a in (series, out_grad)
    ]
    row_spec = pl.BlockSpec((step, width), lambda i: (i, 0))
    return pl.pallas_call(
        norm_kernel,
        out_shape=[
            jax.ShapeDtypeStruct((2, rows, width), BF16),
            jax.ShapeDtypeStruct((rows, 1), F32),
        ],
        grid=(4,),
        in_specs=[row_spec, pl.BlockSpec((1, width), lambda i: (0, 0)), row_spec],
        out_specs=[
            pl.BlockSpec((2, step, width), lambda i: (0, i, 0)),
            pl.BlockSpec((step, 1), lambda i: (i, 0)),
        ],
        compiler_params=pltpu.CompilerParams(vmem_limit_bytes=6 * 2**20),
        name="normalize",
    )(series, gain[None], out_grad)


def matmul(a, b):
    return jnp.dot(a, b, preferred_element_type=F32)


def matmul_t(a, b):
    return lax.dot_general(a, b, NT, preferred_element_type=F32)


def swapped(own, passed, bit, sign):
    size = lax.axis_size("seq")
    high = (lax.axis_index("seq") // bit) % 2 == 1
    sent = jnp.where(high, passed, own) if sign > 0 else jnp.where(high, own, passed)
    return lax.ppermute(sent, "seq", [(i, i ^ bit) for i in range(size)])


def exchange(keys, queries):
    two, two_q = shifted(keys, 2), shifted(queries, -2)
    far, far_q = shifted(keys, 32), shifted(queries, -32)
    two, far = lax.optimization_barrier((two, far))
    two_q, far_q = lax.optimization_barrier((two_q, far_q))
    four, four_q = shifted(two, 2), shifted(two_q, -2)
    eight, eight_q = shifted(four, 4), shifted(four_q, -4)
    last, last_q = shifted(far, 32), shifted(far_q, -32)
    sixteen = swapped(keys, far, 16, 1)
    sixteen_q = swapped(queries, far_q, 16, -1)
    keys_late, two_late, eight, last_q, sixteen_q = lax.optimization_barrier(
        (keys, two, eight, last_q, sixteen_q)
    )
    one = swapped(keys_late, two_late, 1, 1)
    queries_late, two_q_late, eight_q = lax.optimization_barrier((queries, two_q, eight_q))
    one_q = swapped(queries_late, two_q_late, 1, -1)
    return (
        [one, two, four, eight, sixteen, far, last],
        [one_q, two_q, four_q, eight_q, sixteen_q, far_q, last_q],
    )


def exchange_stats(stat, attn_other):
    two, far = shifted(stat, -2), shifted(stat, -32)
    direct = [shifted(stat, -by) for by in (64, 8, 4)]
    sixteen = swapped(stat, far, 16, -1)
    two_last, attn_other = lax.optimization_barrier((two, attn_other))
    one = swapped(stat, two_last, 1, -1)
    return attn_other, [one, two, direct[2], direct[1], sixteen, far, direct[0]]


def per_device(series, norm_gain, w_query, w_key, w_value, w_out, out_grad):
    levels = lax.axis_size("seq").bit_length() - 1
    half = series.shape[0]
    blocks = 2 * half // BLOCK
    tp_index = lax.axis_index("tp").astype(jnp.int32)
    seq_index = lax.axis_index("seq").astype(jnp.int32)
    where = jnp.stack([tp_index, seq_index * blocks])
    series_f = series.astype(F32)
    sent, inv_rms = normalize(series, norm_gain, out_grad)
    normed = sent[0]
    unit_rows = series_f * inv_rms
    normed_other, out_grad_other = swap_tp(sent)

    def key_value(rows):
        return jnp.stack([matmul(rows, w_key).astype(BF16), matmul(rows, w_value).astype(BF16)])

    def query_grad(rows, grad_rows):
        return jnp.stack(
            [matmul(rows, w_query).astype(BF16), matmul_t(grad_rows, w_out).astype(BF16)]
        )

    kv = (key_value(normed), key_value(normed_other))
    qg = (query_grad(normed, out_grad), query_grad(normed_other, out_grad_other))
    kv_all, qg_all = lax.optimization_barrier(
        (jnp.concatenate(kv, axis=1), jnp.concatenate(qg, axis=1))
    )
    fetched, later = exchange(kv_all, qg_all)
    mixed, grad_query, stat = query_side(where, qg_all, kv_all, [(f,) for f in fetched], 0)
    stat, later = lax.optimization_barrier((stat, later))
    later = [(f,) for f in later]
    attn_other = swap_tp(matmul(mixed[half:], w_out).astype(BF16))
    attn_other, later_stats = exchange_stats(stat, attn_other)
    attn_rows = matmul(mixed[:half], w_out) + attn_other.astype(F32)
    layer_out = (series_f + attn_rows).astype(BF16)

    grad_queries = lax.optimization_barrier(matmul_t(grad_query, w_query))

    def back(at):
        grad_kv = key_side(at, where, kv_all, qg_all, stat, later, later_stats)
        rows = slice(at * half, (at + 1) * half)
        return (
            grad_queries[rows]
            + matmul_t(grad_kv[0], w_key)
            + matmul_t(grad_kv[1], w_value)
        )

    normed_grad_other = swap_tp(back(1).astype(BF16))
    normed_grad = back(0) + normed_grad_other.astype(F32)
    scaled = normed_grad * norm_gain
    series_grad = out_grad.astype(F32) + inv_rms * (
        scaled - unit_rows * jnp.mean(scaled * unit_rows, axis=-1, keepdims=True)
    )
    return (layer_out, series_grad.astype(BF16))


def solution(mesh):
    rows = P(("seq", "tp"), None)
    columns = P(None, "tp")
    in_specs = (rows, P(), columns, columns, columns, P("tp", None), rows)
    return jax.shard_map(
        per_device, mesh=mesh, in_specs=in_specs, out_specs=(rows, rows), check_vma=False
    )
```

```python
import functools

import jax
import jax.numpy as jnp
from jax import lax
from jax.experimental import pallas as pl
from jax.experimental.pallas import tpu as pltpu
from jax.sharding import PartitionSpec as P

HD = 128
BLOCK = 64
NEG = -1e30
EPS = 1e-06
F32 = jnp.float32
BF16 = jnp.bfloat16
NN = (((1,), (0,)), ((), ()))
NT = (((1,), (1,)), ((), ()))
TN = (((0,), (0,)), ((), ()))
NEAR = (1, 2, 4)


def shifted(value, by):
    size = lax.axis_size("seq")
    pairs = [(i, i + by) for i in range(size) if 0 <= i + by < size]
    return lax.ppermute(value, "seq", pairs)


def swap_tp(value):
    return lax.ppermute(value, "tp", [(0, 1), (1, 0)])


def dot(a, b, dims):
    return lax.dot_general(a, b, dims, preferred_element_type=F32)


def piece(pieces, which, slot):
    per = 4 // len(pieces)
    at = (slot % per) * BLOCK
    return pieces[slot // per][which, at : at + BLOCK, :]


def near_slots(step, slot):
    found = []
    for turn in (0, 2):
        block = (slot + turn) % 4 + step
        found.append((0 <= block < 4, (block + turn) % 4))
    return found


def near(is_second, own, other, which, slot, step):
    options = [
        piece(own if here else other, which, at) for here, at in near_slots(step, slot)
    ]
    return jnp.where(is_second, options[1], options[0])


def causal_bias(query_axis):
    rows = lax.broadcasted_iota(jnp.int32, (BLOCK, BLOCK), query_axis)
    keys = lax.broadcasted_iota(jnp.int32, (BLOCK, BLOCK), 1 - query_axis)
    return jnp.where(rows >= keys, 0.0, NEG).astype(F32)


def query_kernel(groups, backs, where_ref, *refs):
    refs = list(refs)
    qg, kv = [refs.pop(0)], [refs.pop(0)]
    fetched = [[refs.pop(0) for _ in range(n)] for n in groups]
    mixed_ref, dq_ref, stat_ref, *back_refs = refs
    is_second = where_ref[0] == 1
    factor = HD ** (-0.5)
    causal = causal_bias(0)
    lane = lax.broadcasted_iota(jnp.int32, (BLOCK, HD), 1)
    slots = range(4)

    def gather(which, slot):
        return jnp.concatenate(
            [piece(kv, which, slot)]
            + [near(is_second, kv, fetched[0], which, slot, -d) for d in NEAR]
            + [piece(f, which, slot) for f in fetched[1:]],
            axis=0,
        )

    def rows(slot):
        return slice(slot * BLOCK, (slot + 1) * BLOCK)

    part = lax.broadcasted_iota(jnp.int32, (1, (4 + len(groups) - 1) * BLOCK), 1) // BLOCK
    reach = jnp.where(part == 0, 0, jnp.left_shift(1, jnp.maximum(part - 1, 0)))
    query = [piece(qg, 0, slot) for slot in slots]
    grad = [piece(qg, 1, slot) for slot in slots]
    keys = [gather(0, slot) for slot in slots]
    values = [gather(1, slot) for slot in slots]
    score = []
    for slot in slots:
        block = where_ref[1] + (slot + 2 * where_ref[0]) % 4
        s = dot(query[slot], keys[slot], NT) * factor + jnp.where(reach <= block, 0.0, NEG)
        score.append(jnp.concatenate([s[:, :BLOCK] + causal, s[:, BLOCK:]], axis=1))
    grad_prob = [dot(grad[slot], values[slot], NT) for slot in slots]
    peak = [jnp.max(s, axis=-1, keepdims=True) for s in score]
    weight = [jnp.exp(score[slot] - peak[slot]) for slot in slots]
    total = [jnp.sum(w, axis=-1, keepdims=True) for w in weight]
    prob = [weight[slot] * (1.0 / total[slot]) for slot in slots]
    prob_b = [p.astype(BF16) for p in prob]
    mixed = [dot(prob_b[slot], values[slot], NN).astype(BF16) for slot in slots]
    inner = [
        jnp.sum(mixed[slot].astype(F32) * grad[slot].astype(F32), axis=-1, keepdims=True)
        for slot in slots
    ]
    grad_score = [
        (prob[slot] * (grad_prob[slot] - inner[slot])).astype(BF16) for slot in slots
    ]
    for slot in slots:
        out = rows(slot)
        mixed_ref[out, :] = mixed[slot]
        dq_ref[out, :] = (dot(grad_score[slot], keys[slot], NN) * factor).astype(BF16)
        stat = jnp.where(lane == 0, peak[slot] + jnp.log(total[slot]), inner[slot])
        stat_ref[0, :, out] = jnp.transpose(stat)[:2]
        for at, ref in zip(backs, back_refs):
            part = slice((3 + at) * BLOCK, (4 + at) * BLOCK)
            ref[0, out, :] = (dot(grad_score[slot][:, part], query[slot], TN) * factor).astype(BF16)
            ref[1, out, :] = dot(prob_b[slot][:, part], grad[slot], TN).astype(BF16)


def key_kernel(half, groups, n_back, where_ref, *refs):
    refs = list(refs)
    kv = refs.pop(0)
    qg = [refs.pop(0)]
    stat = refs.pop(0)
    later = [[refs.pop(0) for _ in range(n)] for n in groups]
    later_stats = [refs.pop(0) for _ in groups]
    back = [refs.pop(0) for _ in range(n_back)]
    (out_ref,) = refs
    is_second = where_ref[0] == 1
    factor = HD ** (-0.5)
    causal = causal_bias(1)

    def stat_of(ref, slot):
        return ref[0, :, slot * BLOCK : (slot + 1) * BLOCK]

    def gather(which, at):
        rows = slice(at * BLOCK, (at + 1) * BLOCK)
        return jnp.concatenate(
            [piece(qg, which, 2 * half + at)]
            + [near(is_second, qg, later[0], which, 2 * half + at, d) for d in NEAR]
            + [f[0][which, rows, :] for f in later[1:]],
            axis=0,
        )

    def gather_stats(slot):
        parts = [stat_of(stat, slot)]
        for d in NEAR:
            options = [
                stat_of(stat if here else later_stats[0], s) for here, s in near_slots(d, slot)
            ]
            parts.append(jnp.where(is_second, options[1], options[0]))
        return jnp.concatenate(parts + [stat_of(f, slot) for f in later_stats[1:]], axis=1)

    both = range(2)
    rows = [slice(at * BLOCK, (at + 1) * BLOCK) for at in both]
    queries = [gather(0, at) for at in both]
    grads = [gather(1, at) for at in both]
    stats = [gather_stats(2 * half + at) for at in both]
    score = [dot(kv[0, rows[at], :], queries[at], NT) * factor for at in both]
    grad_prob = [dot(kv[1, rows[at], :], grads[at], NT) for at in both]
    score = [jnp.concatenate([s[:, :BLOCK] + causal, s[:, BLOCK:]], axis=1) for s in score]
    prob = [jnp.exp(score[at] - stats[at][0:1]) for at in both]
    grad_score = [(prob[at] * (grad_prob[at] - stats[at][1:2])).astype(BF16) for at in both]
    prob_b = [p.astype(BF16) for p in prob]
    grad_keys = [dot(grad_score[at], queries[at], NN) * factor for at in both]
    grad_values = [dot(prob_b[at], grads[at], NN) for at in both]
    for which, totals in enumerate((grad_keys, grad_values)):
        for at in both:
            total = totals[at]
            for ref in back:
                total += ref[which, rows[at], :].astype(F32)
            out_ref[which, rows[at], :] = total.astype(BF16)


def head_spec(a):
    if a.ndim == 2:
        return pl.BlockSpec((a.shape[0], HD), lambda h, w: (0, h))
    return pl.BlockSpec((a.shape[0], a.shape[1], HD), lambda h, w: (0, 0, h))


def stat_spec(a):
    return pl.BlockSpec((1,) + a.shape[1:], lambda h, w: (h, 0, 0))


def call(kernel, where, operands, in_specs, outs, out_specs, heads, keys, name):
    rows = outs[0].shape[-2]
    return pl.pallas_call(
        kernel,
        out_shape=outs,
        grid_spec=pltpu.PrefetchScalarGridSpec(
            num_scalar_prefetch=1, grid=(heads,), in_specs=in_specs, out_specs=out_specs
        ),
        compiler_params=pltpu.CompilerParams(vmem_limit_bytes=6 * 2**20),
        cost_estimate=pl.CostEstimate(
            flops=rows * keys, bytes_accessed=2**16, transcendentals=0
        ),
        name=name,
    )(where, *operands)


def query_side(where, qg, kv, fetched, backs):
    rows, width = qg.shape[1], qg.shape[2]
    heads = width // HD
    far = [a for f in fetched for a in f]
    operands = [qg, kv, *far]
    row_out = jax.ShapeDtypeStruct((rows, width), BF16)
    stat_out = jax.ShapeDtypeStruct((heads, 2, rows), F32)
    back_out = jax.ShapeDtypeStruct((2, rows, width), BF16)
    outs = [row_out, pltpu.HBM(row_out.shape, BF16), stat_out] + [pltpu.HBM(back_out.shape, BF16)] * len(backs)
    return call(
        functools.partial(query_kernel, tuple(len(f) for f in fetched), backs),
        where,
        operands,
        [head_spec(a) for a in operands],
        outs,
        [head_spec(row_out), head_spec(row_out), stat_spec(stat_out)] + [head_spec(back_out)] * len(backs),
        heads,
        (3 + len(fetched)) * BLOCK,
        "query_side",
    )


def key_side(half, where, kv, qg, stat, later, later_stats, returned):
    rows, width = kv.shape[1] // 2, kv.shape[2]
    heads = width // HD
    half_of_whole = pl.BlockSpec((2, rows, HD), lambda h, w: (0, half, h))
    far = [f[-1] if len(f) == 1 else f[half] for f in later[1:]]
    first, *far = [pltpu.with_memory_space_constraint(a, pltpu.HBM) for a in (*later[0], *far)]
    operands = [kv, qg, stat, first, *far, *later_stats, *returned]
    in_specs = (
        [half_of_whole, head_spec(qg)]
        + [stat_spec(stat)]
        + [head_spec(a) for a in later[0]]
        + [half_of_whole if len(f) == 1 else head_spec(f[half]) for f in later[1:]]
        + [stat_spec(a) for a in later_stats]
        + [half_of_whole] * len(returned)
    )
    out = jax.ShapeDtypeStruct((2, rows, width), BF16)
    groups = (len(later[0]),) + (1,) * len(far)
    (result,) = call(
        functools.partial(key_kernel, half, groups, len(returned)),
        where,
        operands,
        in_specs,
        [out],
        [head_spec(out)],
        heads,
        (4 + len(far)) * BLOCK,
        "key_side",
    )
    return result


def norm_kernel(series_ref, gain_ref, grad_ref, sent_ref, inv_ref):
    rows = series_ref[...].astype(F32)
    inv_rms = lax.rsqrt(jnp.mean(rows * rows, axis=-1, keepdims=True) + EPS)
    inv_ref[...] = inv_rms
    sent_ref[0] = (rows * inv_rms * gain_ref[...]).astype(BF16)
    sent_ref[1] = grad_ref[...]


def normalize(series, gain, out_grad):
    rows, width = series.shape
    step = rows // 4
    series, out_grad = [
        pltpu.with_memory_space_constraint(a, pltpu.HBM) for a in (series, out_grad)
    ]
    row_spec = pl.BlockSpec((step, width), lambda i: (i, 0))
    return pl.pallas_call(
        norm_kernel,
        out_shape=[
            jax.ShapeDtypeStruct((2, rows, width), BF16),
            jax.ShapeDtypeStruct((rows, 1), F32),
        ],
        grid=(4,),
        in_specs=[row_spec, pl.BlockSpec((1, width), lambda i: (0, 0)), row_spec],
        out_specs=[
            pl.BlockSpec((2, step, width), lambda i: (0, i, 0)),
            pl.BlockSpec((step, 1), lambda i: (i, 0)),
        ],
        compiler_params=pltpu.CompilerParams(vmem_limit_bytes=6 * 2**20),
        name="normalize",
    )(series, gain[None], out_grad)


def matmul(a, b):
    return jnp.dot(a, b, preferred_element_type=F32)


def matmul_t(a, b):
    return lax.dot_general(a, b, NT, preferred_element_type=F32)


def swapped(own, passed, bit, sign):
    size = lax.axis_size("seq")
    high = (lax.axis_index("seq") // bit) % 2 == 1
    sent = jnp.where(high, passed, own) if sign > 0 else jnp.where(high, own, passed)
    return lax.ppermute(sent, "seq", [(i, i ^ bit) for i in range(size)])


def exchange(keys, queries):
    two, two_q = shifted(keys, 2), shifted(queries, -2)
    far = shifted(keys, 32)
    two, far, two_q = lax.optimization_barrier((two, far, two_q))
    four, four_q = shifted(two, 2), shifted(two_q, -2)
    eight = shifted(four, 4)
    far_q = shifted(queries, -32)
    sixteen, sixteen_q = swapped(keys, far, 16, 1), swapped(queries, far_q, 16, -1)
    keys_late, two_late, eight, four_q = lax.optimization_barrier((keys, two, eight, four_q))
    one, one_q = swapped(keys_late, two_late, 1, 1), swapped(queries, two_q, 1, -1)
    return (
        [one, two, four, eight, sixteen, far, shifted(far, 32)],
        [one_q, two_q, four_q, sixteen_q, far_q],
    )


def exchange_stats(stat, attn_other):
    two, far = shifted(stat, -2), shifted(stat, -32)
    stat_late, far = lax.optimization_barrier((stat, far))
    four = shifted(stat_late, -4)
    sixteen = swapped(stat, far, 16, -1)
    two_last, attn_other = lax.optimization_barrier((two, attn_other))
    return attn_other, [swapped(stat, two_last, 1, -1), two, four, sixteen, far]


def per_device(series, norm_gain, w_query, w_key, w_value, w_out, out_grad):
    levels = lax.axis_size("seq").bit_length() - 1
    half = series.shape[0]
    blocks = 2 * half // BLOCK
    tp_index = lax.axis_index("tp").astype(jnp.int32)
    seq_index = lax.axis_index("seq").astype(jnp.int32)
    where = jnp.stack([tp_index, seq_index * blocks])
    series_f = series.astype(F32)
    sent, inv_rms = normalize(series, norm_gain, out_grad)
    normed = sent[0]
    unit_rows = series_f * inv_rms
    normed_other, out_grad_other = swap_tp(sent)

    def key_value(rows):
        return jnp.stack([matmul(rows, w_key).astype(BF16), matmul(rows, w_value).astype(BF16)])

    def query_grad(rows, grad_rows):
        return jnp.stack(
            [matmul(rows, w_query).astype(BF16), matmul_t(grad_rows, w_out).astype(BF16)]
        )

    kv = (key_value(normed), key_value(normed_other))
    qg = (query_grad(normed, out_grad), query_grad(normed_other, out_grad_other))
    kv_all, qg_all = lax.optimization_barrier(
        (jnp.concatenate(kv, axis=1), jnp.concatenate(qg, axis=1))
    )
    fetched, later = exchange(kv_all, qg_all)
    mixed, grad_query, stat, *backs = query_side(
        where, qg_all, kv_all, [(f,) for f in fetched], (3, 6)
    )
    stat, backs, later = lax.optimization_barrier((stat, backs, later))
    returned = [shifted(b, -by) for b, by in zip(backs, (8, 64))]
    later = [(f,) for f in later]
    attn_other = swap_tp(matmul(mixed[half:], w_out).astype(BF16))
    attn_other, later_stats = exchange_stats(stat, attn_other)
    attn_rows = matmul(mixed[:half], w_out) + attn_other.astype(F32)
    layer_out = (series_f + attn_rows).astype(BF16)

    grad_queries = lax.optimization_barrier(matmul_t(grad_query, w_query))

    def back(at):
        grad_kv = key_side(at, where, kv_all, qg_all, stat, later, later_stats, returned)
        rows = slice(at * half, (at + 1) * half)
        return (
            grad_queries[rows]
            + matmul_t(grad_kv[0], w_key)
            + matmul_t(grad_kv[1], w_value)
        )

    normed_grad_other = swap_tp(back(1).astype(BF16))
    normed_grad = back(0) + normed_grad_other.astype(F32)
    scaled = normed_grad * norm_gain
    series_grad = out_grad.astype(F32) + inv_rms * (
        scaled - unit_rows * jnp.mean(scaled * unit_rows, axis=-1, keepdims=True)
    )
    return (layer_out, series_grad.astype(BF16))


def solution(mesh):
    rows = P(("seq", "tp"), None)
    columns = P(None, "tp")
    in_specs = (rows, P(), columns, columns, columns, P("tp", None), rows)
    return jax.shard_map(
        per_device, mesh=mesh, in_specs=in_specs, out_specs=(rows, rows), check_vma=False
    )
```

```python
import functools

import jax
import jax.numpy as jnp
from jax import lax
from jax.experimental import pallas as pl
from jax.experimental.pallas import tpu as pltpu
from jax.sharding import PartitionSpec as P

HD = 128
BLOCK = 64
NEG = -1e30
EPS = 1e-06
F32 = jnp.float32
BF16 = jnp.bfloat16
NN = (((1,), (0,)), ((), ()))
NT = (((1,), (1,)), ((), ()))
TN = (((0,), (0,)), ((), ()))
NEAR = (1, 2, 4)


def shifted(value, by):
    size = lax.axis_size("seq")
    pairs = [(i, i + by) for i in range(size) if 0 <= i + by < size]
    return lax.ppermute(value, "seq", pairs)


def swap_tp(value):
    return lax.ppermute(value, "tp", [(0, 1), (1, 0)])


def dot(a, b, dims):
    return lax.dot_general(a, b, dims, preferred_element_type=F32)


def piece(pieces, which, slot):
    per = 4 // len(pieces)
    at = (slot % per) * BLOCK
    return pieces[slot // per][which, at : at + BLOCK, :]


def near_slots(step, slot):
    found = []
    for turn in (0, 2):
        block = (slot + turn) % 4 + step
        found.append((0 <= block < 4, (block + turn) % 4))
    return found


def near(is_second, own, other, which, slot, step):
    options = [
        piece(own if here else other, which, at) for here, at in near_slots(step, slot)
    ]
    return jnp.where(is_second, options[1], options[0])


def causal_bias(query_axis):
    rows = lax.broadcasted_iota(jnp.int32, (BLOCK, BLOCK), query_axis)
    keys = lax.broadcasted_iota(jnp.int32, (BLOCK, BLOCK), 1 - query_axis)
    return jnp.where(rows >= keys, 0.0, NEG).astype(F32)


def query_kernel(groups, n_back, where_ref, *refs):
    refs = list(refs)
    qg, kv = [refs.pop(0)], [refs.pop(0)]
    fetched = [[refs.pop(0) for _ in range(n)] for n in groups]
    mixed_ref, dq_ref, stat_ref, *back_refs = refs
    is_second = where_ref[0] == 1
    factor = HD ** (-0.5)
    causal = causal_bias(0)
    lane = lax.broadcasted_iota(jnp.int32, (BLOCK, HD), 1)
    slots = range(4)

    def gather(which, slot):
        return jnp.concatenate(
            [piece(kv, which, slot)]
            + [near(is_second, kv, fetched[0], which, slot, -d) for d in NEAR]
            + [piece(f, which, slot) for f in fetched[1:]],
            axis=0,
        )

    def rows(slot):
        return slice(slot * BLOCK, (slot + 1) * BLOCK)

    part = lax.broadcasted_iota(jnp.int32, (1, (4 + len(groups) - 1) * BLOCK), 1) // BLOCK
    reach = jnp.where(part == 0, 0, jnp.left_shift(1, jnp.maximum(part - 1, 0)))
    query = [piece(qg, 0, slot) for slot in slots]
    grad = [piece(qg, 1, slot) for slot in slots]
    keys = [gather(0, slot) for slot in slots]
    values = [gather(1, slot) for slot in slots]
    score = []
    for slot in slots:
        block = where_ref[1] + (slot + 2 * where_ref[0]) % 4
        s = dot(query[slot], keys[slot], NT) * factor + jnp.where(reach <= block, 0.0, NEG)
        score.append(jnp.concatenate([s[:, :BLOCK] + causal, s[:, BLOCK:]], axis=1))
    grad_prob = [dot(grad[slot], values[slot], NT) for slot in slots]
    peak = [jnp.max(s, axis=-1, keepdims=True) for s in score]
    weight = [jnp.exp(score[slot] - peak[slot]) for slot in slots]
    total = [jnp.sum(w, axis=-1, keepdims=True) for w in weight]
    prob = [weight[slot] * (1.0 / total[slot]) for slot in slots]
    prob_b = [p.astype(BF16) for p in prob]
    mixed = [dot(prob_b[slot], values[slot], NN).astype(BF16) for slot in slots]
    inner = [
        jnp.sum(mixed[slot].astype(F32) * grad[slot].astype(F32), axis=-1, keepdims=True)
        for slot in slots
    ]
    grad_score = [
        (prob[slot] * (grad_prob[slot] - inner[slot])).astype(BF16) for slot in slots
    ]
    first = keys[0].shape[0] - n_back * BLOCK
    for slot in slots:
        out = rows(slot)
        mixed_ref[out, :] = mixed[slot]
        dq_ref[out, :] = (dot(grad_score[slot], keys[slot], NN) * factor).astype(BF16)
        stat = jnp.where(lane == 0, peak[slot] + jnp.log(total[slot]), inner[slot])
        stat_ref[0, :, out] = jnp.transpose(stat)[:2]
        if n_back:
            grad_keys = (dot(grad_score[slot][:, first:], query[slot], TN) * factor).astype(BF16)
            grad_values = dot(prob_b[slot][:, first:], grad[slot], TN).astype(BF16)
            for at, ref in enumerate(back_refs):
                ref[0, out, :] = grad_keys[at * BLOCK : (at + 1) * BLOCK]
                ref[1, out, :] = grad_values[at * BLOCK : (at + 1) * BLOCK]


def key_kernel(half, groups, where_ref, *refs):
    refs = list(refs)
    kv = refs.pop(0)
    qg = [refs.pop(0)]
    stat = refs.pop(0)
    later = [[refs.pop(0) for _ in range(n)] for n in groups]
    later_stats = [refs.pop(0) for _ in groups]
    (out_ref,) = refs
    is_second = where_ref[0] == 1
    factor = HD ** (-0.5)
    causal = causal_bias(1)

    def stat_of(ref, slot):
        return ref[0, :, slot * BLOCK : (slot + 1) * BLOCK]

    def gather(which, at):
        rows = slice(at * BLOCK, (at + 1) * BLOCK)
        return jnp.concatenate(
            [piece(qg, which, 2 * half + at)]
            + [near(is_second, qg, later[0], which, 2 * half + at, d) for d in NEAR]
            + [f[0][which, rows, :] for f in later[1:]],
            axis=0,
        )

    def gather_stats(slot):
        parts = [stat_of(stat, slot)]
        for d in NEAR:
            options = [
                stat_of(stat if here else later_stats[0], s) for here, s in near_slots(d, slot)
            ]
            parts.append(jnp.where(is_second, options[1], options[0]))
        return jnp.concatenate(parts + [stat_of(f, slot) for f in later_stats[1:]], axis=1)

    both = range(2)
    rows = [slice(at * BLOCK, (at + 1) * BLOCK) for at in both]
    queries = [gather(0, at) for at in both]
    grads = [gather(1, at) for at in both]
    stats = [gather_stats(2 * half + at) for at in both]
    score = [dot(kv[0, rows[at], :], queries[at], NT) * factor for at in both]
    grad_prob = [dot(kv[1, rows[at], :], grads[at], NT) for at in both]
    score = [jnp.concatenate([s[:, :BLOCK] + causal, s[:, BLOCK:]], axis=1) for s in score]
    prob = [jnp.exp(score[at] - stats[at][0:1]) for at in both]
    grad_score = [(prob[at] * (grad_prob[at] - stats[at][1:2])).astype(BF16) for at in both]
    prob_b = [p.astype(BF16) for p in prob]
    grad_keys = [dot(grad_score[at], queries[at], NN) * factor for at in both]
    grad_values = [dot(prob_b[at], grads[at], NN) for at in both]
    for at in both:
        out_ref[0, rows[at], :] = grad_keys[at].astype(BF16)
        out_ref[1, rows[at], :] = grad_values[at].astype(BF16)


def head_spec(a):
    if a.ndim == 2:
        return pl.BlockSpec((a.shape[0], HD), lambda h, w: (0, h))
    return pl.BlockSpec((a.shape[0], a.shape[1], HD), lambda h, w: (0, 0, h))


def stat_spec(a):
    return pl.BlockSpec((1,) + a.shape[1:], lambda h, w: (h, 0, 0))


def call(kernel, where, operands, in_specs, outs, out_specs, heads, keys, name):
    rows = outs[0].shape[-2]
    return pl.pallas_call(
        kernel,
        out_shape=outs,
        grid_spec=pltpu.PrefetchScalarGridSpec(
            num_scalar_prefetch=1, grid=(heads,), in_specs=in_specs, out_specs=out_specs
        ),
        compiler_params=pltpu.CompilerParams(vmem_limit_bytes=6 * 2**20),
        cost_estimate=pl.CostEstimate(
            flops=rows * keys, bytes_accessed=2**16, transcendentals=0
        ),
        name=name,
    )(where, *operands)


def query_side(where, qg, kv, fetched, n_back):
    rows, width = qg.shape[1], qg.shape[2]
    heads = width // HD
    far = [a for f in fetched for a in f]
    operands = [qg, kv, *far]
    row_out = jax.ShapeDtypeStruct((rows, width), BF16)
    stat_out = jax.ShapeDtypeStruct((heads, 2, rows), F32)
    back_out = jax.ShapeDtypeStruct((2, rows, width), BF16)
    outs = [row_out, pltpu.HBM(row_out.shape, BF16), stat_out] + [back_out] * n_back
    return call(
        functools.partial(query_kernel, tuple(len(f) for f in fetched), n_back),
        where,
        operands,
        [head_spec(a) for a in operands],
        outs,
        [head_spec(row_out), head_spec(row_out), stat_spec(stat_out)] + [head_spec(back_out)] * n_back,
        heads,
        (3 + len(fetched)) * BLOCK,
        "query_side",
    )


def key_side(half, where, kv, qg, stat, later, later_stats):
    rows, width = kv.shape[1] // 2, kv.shape[2]
    heads = width // HD
    half_of_whole = pl.BlockSpec((2, rows, HD), lambda h, w: (0, half, h))
    far = [f[-1] if len(f) == 1 else f[half] for f in later[1:]]
    first, *far = [pltpu.with_memory_space_constraint(a, pltpu.HBM) for a in (*later[0], *far)]
    operands = [kv, qg, stat, first, *far, *later_stats]
    in_specs = (
        [half_of_whole, head_spec(qg)]
        + [stat_spec(stat)]
        + [head_spec(a) for a in later[0]]
        + [half_of_whole if len(f) == 1 else head_spec(f[half]) for f in later[1:]]
        + [stat_spec(a) for a in later_stats]
    )
    out = jax.ShapeDtypeStruct((2, rows, width), BF16)
    groups = (len(later[0]),) + (1,) * len(far)
    (result,) = call(
        functools.partial(key_kernel, half, groups),
        where,
        operands,
        in_specs,
        [out],
        [head_spec(out)],
        heads,
        (4 + len(far)) * BLOCK,
        "key_side",
    )
    return result


def norm_kernel(series_ref, gain_ref, grad_ref, sent_ref, inv_ref):
    rows = series_ref[...].astype(F32)
    inv_rms = lax.rsqrt(jnp.mean(rows * rows, axis=-1, keepdims=True) + EPS)
    inv_ref[...] = inv_rms
    sent_ref[0] = (rows * inv_rms * gain_ref[...]).astype(BF16)
    sent_ref[1] = grad_ref[...]


def normalize(series, gain, out_grad):
    rows, width = series.shape
    step = rows // 4
    series, out_grad = [
        pltpu.with_memory_space_constraint(a, pltpu.HBM) for a in (series, out_grad)
    ]
    row_spec = pl.BlockSpec((step, width), lambda i: (i, 0))
    return pl.pallas_call(
        norm_kernel,
        out_shape=[
            jax.ShapeDtypeStruct((2, rows, width), BF16),
            jax.ShapeDtypeStruct((rows, 1), F32),
        ],
        grid=(4,),
        in_specs=[row_spec, pl.BlockSpec((1, width), lambda i: (0, 0)), row_spec],
        out_specs=[
            pl.BlockSpec((2, step, width), lambda i: (0, i, 0)),
            pl.BlockSpec((step, 1), lambda i: (i, 0)),
        ],
        compiler_params=pltpu.CompilerParams(vmem_limit_bytes=6 * 2**20),
        name="normalize",
    )(series, gain[None], out_grad)


def matmul(a, b):
    return jnp.dot(a, b, preferred_element_type=F32)


def matmul_t(a, b):
    return lax.dot_general(a, b, NT, preferred_element_type=F32)


def swapped(own, passed, bit, sign):
    size = lax.axis_size("seq")
    high = (lax.axis_index("seq") // bit) % 2 == 1
    sent = jnp.where(high, passed, own) if sign > 0 else jnp.where(high, own, passed)
    return lax.ppermute(sent, "seq", [(i, i ^ bit) for i in range(size)])


def exchange(keys, queries):
    two, two_q = shifted(keys, 2), shifted(queries, -2)
    far, far_q = shifted(keys, 32), shifted(queries, -32)
    two, far = lax.optimization_barrier((two, far))
    two_q, far_q = lax.optimization_barrier((two_q, far_q))
    four, four_q = shifted(two, 2), shifted(two_q, -2)
    one, sixteen = swapped(keys, two, 1, 1), swapped(keys, far, 16, 1)
    one_q, sixteen_q = swapped(queries, two_q, 1, -1), swapped(queries, far_q, 16, -1)
    four, one, sixteen = lax.optimization_barrier((four, one, sixteen))
    four_q, one_q, sixteen_q = lax.optimization_barrier((four_q, one_q, sixteen_q))
    eight, eight_q = shifted(four, 4), shifted(four_q, -4)
    return (
        [one, two, four, eight, sixteen, far, shifted(far, 32)],
        [one_q, two_q, four_q, eight_q, sixteen_q, far_q, shifted(far_q, -32)],
    )


def exchange_stats(stat, attn_other):
    two, far = shifted(stat, -2), shifted(stat, -32)
    direct = [shifted(stat, -by) for by in (64, 8, 4)]
    sixteen = swapped(stat, far, 16, -1)
    two_last, attn_other = lax.optimization_barrier((two, attn_other))
    one = swapped(stat, two_last, 1, -1)
    return attn_other, [one, two, direct[2], direct[1], sixteen, far, direct[0]]


def per_device(series, norm_gain, w_query, w_key, w_value, w_out, out_grad):
    levels = lax.axis_size("seq").bit_length() - 1
    half = series.shape[0]
    blocks = 2 * half // BLOCK
    tp_index = lax.axis_index("tp").astype(jnp.int32)
    seq_index = lax.axis_index("seq").astype(jnp.int32)
    where = jnp.stack([tp_index, seq_index * blocks])
    series_f = series.astype(F32)
    sent, inv_rms = normalize(series, norm_gain, out_grad)
    normed = sent[0]
    unit_rows = series_f * inv_rms
    normed_other, out_grad_other = swap_tp(sent)

    def key_value(rows):
        return jnp.stack([matmul(rows, w_key).astype(BF16), matmul(rows, w_value).astype(BF16)])

    def query_grad(rows, grad_rows):
        return jnp.stack(
            [matmul(rows, w_query).astype(BF16), matmul_t(grad_rows, w_out).astype(BF16)]
        )

    kv = (key_value(normed), key_value(normed_other))
    qg = (query_grad(normed, out_grad), query_grad(normed_other, out_grad_other))
    kv_all, qg_all = lax.optimization_barrier(
        (jnp.concatenate(kv, axis=1), jnp.concatenate(qg, axis=1))
    )
    fetched, later = exchange(kv_all, qg_all)
    mixed, grad_query, stat = query_side(where, qg_all, kv_all, [(f,) for f in fetched], 0)
    stat, later = lax.optimization_barrier((stat, later))
    later = [(f,) for f in later]
    attn_other = swap_tp(matmul(mixed[half:], w_out).astype(BF16))
    attn_other, later_stats = exchange_stats(stat, attn_other)
    attn_rows = matmul(mixed[:half], w_out) + attn_other.astype(F32)
    layer_out = (series_f + attn_rows).astype(BF16)

    grad_queries = lax.optimization_barrier(matmul_t(grad_query, w_query))

    def back(at):
        grad_kv = key_side(at, where, kv_all, qg_all, stat, later, later_stats)
        rows = slice(at * half, (at + 1) * half)
        return (
            grad_queries[rows]
            + matmul_t(grad_kv[0], w_key)
            + matmul_t(grad_kv[1], w_value)
        )

    normed_grad_other = swap_tp(back(1).astype(BF16))
    normed_grad = back(0) + normed_grad_other.astype(F32)
    scaled = normed_grad * norm_gain
    series_grad = out_grad.astype(F32) + inv_rms * (
        scaled - unit_rows * jnp.mean(scaled * unit_rows, axis=-1, keepdims=True)
    )
    return (layer_out, series_grad.astype(BF16))


def solution(mesh):
    rows = P(("seq", "tp"), None)
    columns = P(None, "tp")
    in_specs = (rows, P(), columns, columns, columns, P("tp", None), rows)
    return jax.shard_map(
        per_device, mesh=mesh, in_specs=in_specs, out_specs=(rows, rows), check_vma=False
    )
```

```python
import functools

import jax
import jax.numpy as jnp
from jax import lax
from jax.experimental import pallas as pl
from jax.experimental.pallas import tpu as pltpu
from jax.sharding import PartitionSpec as P

HD = 128
BLOCK = 64
NEG = -1e30
EPS = 1e-06
F32 = jnp.float32
BF16 = jnp.bfloat16
NN = (((1,), (0,)), ((), ()))
NT = (((1,), (1,)), ((), ()))
TN = (((0,), (0,)), ((), ()))
NEAR = (1, 2, 4)
GROUP = 2


def shifted(value, by):
    size = lax.axis_size("seq")
    pairs = [(i, i + by) for i in range(size) if 0 <= i + by < size]
    return lax.ppermute(value, "seq", pairs)


def swap_tp(value):
    return lax.ppermute(value, "tp", [(0, 1), (1, 0)])


def dot(a, b, dims):
    return lax.dot_general(a, b, dims, preferred_element_type=F32)


def piece(pieces, which, slot):
    per = 4 // len(pieces)
    at = (slot % per) * BLOCK
    return pieces[slot // per][which, at : at + BLOCK, :]


def near_slots(step, slot):
    found = []
    for turn in (0, 2):
        block = (slot + turn) % 4 + step
        found.append((0 <= block < 4, (block + turn) % 4))
    return found


def near(is_second, own, other, which, slot, step):
    options = [
        piece(own if here else other, which, at) for here, at in near_slots(step, slot)
    ]
    return jnp.where(is_second, options[1], options[0])


def causal_bias(query_axis):
    rows = lax.broadcasted_iota(jnp.int32, (BLOCK, BLOCK), query_axis)
    keys = lax.broadcasted_iota(jnp.int32, (BLOCK, BLOCK), 1 - query_axis)
    return jnp.where(rows >= keys, 0.0, NEG).astype(F32)


def query_kernel(groups, n_back, where_ref, *refs):
    refs = list(refs)
    qg, kv = [refs.pop(0)], [refs.pop(0)]
    fetched = [[refs.pop(0) for _ in range(n)] for n in groups]
    mixed_ref, dq_ref, stat_ref, *back_refs = refs
    is_second = where_ref[0] == 1
    factor = HD ** (-0.5)
    causal = causal_bias(0)
    lane = lax.broadcasted_iota(jnp.int32, (BLOCK, HD), 1)
    slots = range(4)

    def gather(which, slot):
        return jnp.concatenate(
            [piece(kv, which, slot)]
            + [near(is_second, kv, fetched[0], which, slot, -d) for d in NEAR]
            + [piece(f, which, slot) for f in fetched[1:]],
            axis=0,
        )

    def rows(slot):
        return slice(slot * BLOCK, (slot + 1) * BLOCK)

    part = lax.broadcasted_iota(jnp.int32, (1, (4 + len(groups) - 1) * BLOCK), 1) // BLOCK
    reach = jnp.where(part == 0, 0, jnp.left_shift(1, jnp.maximum(part - 1, 0)))
    query = [piece(qg, 0, slot) for slot in slots]
    grad = [piece(qg, 1, slot) for slot in slots]
    keys = [gather(0, slot) for slot in slots]
    values = [gather(1, slot) for slot in slots]
    score = []
    for slot in slots:
        block = where_ref[1] + (slot + 2 * where_ref[0]) % 4
        s = dot(query[slot], keys[slot], NT) * factor + jnp.where(reach <= block, 0.0, NEG)
        score.append(jnp.concatenate([s[:, :BLOCK] + causal, s[:, BLOCK:]], axis=1))
    grad_prob = [dot(grad[slot], values[slot], NT) for slot in slots]
    peak = [jnp.max(s, axis=-1, keepdims=True) for s in score]
    weight = [jnp.exp(score[slot] - peak[slot]) for slot in slots]
    total = [jnp.sum(w, axis=-1, keepdims=True) for w in weight]
    prob = [weight[slot] * (1.0 / total[slot]) for slot in slots]
    prob_b = [p.astype(BF16) for p in prob]
    mixed = [dot(prob_b[slot], values[slot], NN).astype(BF16) for slot in slots]
    inner = [
        jnp.sum(mixed[slot].astype(F32) * grad[slot].astype(F32), axis=-1, keepdims=True)
        for slot in slots
    ]
    grad_score = [
        (prob[slot] * (grad_prob[slot] - inner[slot])).astype(BF16) for slot in slots
    ]
    first = keys[0].shape[0] - n_back * BLOCK
    for slot in slots:
        out = rows(slot)
        mixed_ref[out, :] = mixed[slot]
        dq_ref[out, :] = (dot(grad_score[slot], keys[slot], NN) * factor).astype(BF16)
        stat = jnp.where(lane == 0, peak[slot] + jnp.log(total[slot]), inner[slot])
        stat_ref[0, :, out] = jnp.transpose(stat)[:2]
        if n_back:
            grad_keys = (dot(grad_score[slot][:, first:], query[slot], TN) * factor).astype(BF16)
            grad_values = dot(prob_b[slot][:, first:], grad[slot], TN).astype(BF16)
            for at, ref in enumerate(back_refs):
                ref[0, out, :] = grad_keys[at * BLOCK : (at + 1) * BLOCK]
                ref[1, out, :] = grad_values[at * BLOCK : (at + 1) * BLOCK]


def key_kernel(half, groups, where_ref, *refs):
    refs = list(refs)
    kv = refs.pop(0)
    qg = [refs.pop(0)]
    stat = refs.pop(0)
    later = [[refs.pop(0) for _ in range(n)] for n in groups]
    later_stats = [refs.pop(0) for _ in groups]
    (out_ref,) = refs
    is_second = where_ref[0] == 1
    factor = HD ** (-0.5)
    causal = causal_bias(1)

    def stat_of(ref, slot):
        return ref[0, :, slot * BLOCK : (slot + 1) * BLOCK]

    def gather(which, at):
        rows = slice(at * BLOCK, (at + 1) * BLOCK)
        return jnp.concatenate(
            [piece(qg, which, 2 * half + at)]
            + [near(is_second, qg, later[0], which, 2 * half + at, d) for d in NEAR]
            + [f[0][which, rows, :] for f in later[1:]],
            axis=0,
        )

    def gather_stats(slot):
        parts = [stat_of(stat, slot)]
        for d in NEAR:
            options = [
                stat_of(stat if here else later_stats[0], s) for here, s in near_slots(d, slot)
            ]
            parts.append(jnp.where(is_second, options[1], options[0]))
        return jnp.concatenate(parts + [stat_of(f, slot) for f in later_stats[1:]], axis=1)

    both = range(2)
    rows = [slice(at * BLOCK, (at + 1) * BLOCK) for at in both]
    queries = [gather(0, at) for at in both]
    grads = [gather(1, at) for at in both]
    stats = [gather_stats(2 * half + at) for at in both]
    score = [dot(kv[0, rows[at], :], queries[at], NT) * factor for at in both]
    grad_prob = [dot(kv[1, rows[at], :], grads[at], NT) for at in both]
    score = [jnp.concatenate([s[:, :BLOCK] + causal, s[:, BLOCK:]], axis=1) for s in score]
    prob = [jnp.exp(score[at] - stats[at][0:1]) for at in both]
    grad_score = [(prob[at] * (grad_prob[at] - stats[at][1:2])).astype(BF16) for at in both]
    prob_b = [p.astype(BF16) for p in prob]
    grad_keys = [dot(grad_score[at], queries[at], NN) * factor for at in both]
    grad_values = [dot(prob_b[at], grads[at], NN) for at in both]
    for at in both:
        out_ref[0, rows[at], :] = grad_keys[at].astype(BF16)
        out_ref[1, rows[at], :] = grad_values[at].astype(BF16)


def head_spec(a):
    if len(a.shape) == 2:
        return pl.BlockSpec((a.shape[0], GROUP * HD), lambda h, w: (0, h))
    return pl.BlockSpec((a.shape[0], a.shape[1], GROUP * HD), lambda h, w: (0, 0, h))


def stat_spec(a):
    return pl.BlockSpec((GROUP,) + a.shape[1:], lambda h, w: (h, 0, 0))


def each_head(kernel):
    def run(where_ref, *refs):
        for head in range(GROUP):
            columns = slice(head * HD, (head + 1) * HD)
            kernel(
                where_ref,
                *[
                    r.at[head : head + 1] if r.dtype == F32
                    else r.at[..., columns]
                    for r in refs
                ],
            )

    return run


def call(kernel, where, operands, in_specs, outs, out_specs, heads, keys, name):
    rows = outs[0].shape[-2]
    return pl.pallas_call(
        each_head(kernel),
        out_shape=outs,
        grid_spec=pltpu.PrefetchScalarGridSpec(
            num_scalar_prefetch=1, grid=(heads // GROUP,), in_specs=in_specs, out_specs=out_specs
        ),
        compiler_params=pltpu.CompilerParams(vmem_limit_bytes=14 * 2**20),
        cost_estimate=pl.CostEstimate(
            flops=rows * keys, bytes_accessed=2**16, transcendentals=0
        ),
        name=name,
    )(where, *operands)


def query_side(where, qg, kv, fetched, n_back):
    rows, width = qg.shape[1], qg.shape[2]
    heads = width // HD
    far = [a for f in fetched for a in f]
    operands = [qg, kv, *far]
    row_out = jax.ShapeDtypeStruct((rows, width), BF16)
    stat_out = jax.ShapeDtypeStruct((heads, 2, rows), F32)
    back_out = jax.ShapeDtypeStruct((2, rows, width), BF16)
    outs = [row_out, pltpu.HBM(row_out.shape, BF16), stat_out] + [back_out] * n_back
    return call(
        functools.partial(query_kernel, tuple(len(f) for f in fetched), n_back),
        where,
        operands,
        [head_spec(a) for a in operands],
        outs,
        [head_spec(row_out), head_spec(row_out), stat_spec(stat_out)] + [head_spec(back_out)] * n_back,
        heads,
        (3 + len(fetched)) * BLOCK,
        "query_side",
    )


def key_side(half, where, kv, qg, stat, later, later_stats):
    rows, width = kv.shape[1] // 2, kv.shape[2]
    heads = width // HD
    half_of_whole = pl.BlockSpec((2, rows, GROUP * HD), lambda h, w: (0, half, h))
    far = [f[-1] if len(f) == 1 else f[half] for f in later[1:]]
    first, *far = [pltpu.with_memory_space_constraint(a, pltpu.HBM) for a in (*later[0], *far)]
    operands = [kv, qg, stat, first, *far, *later_stats]
    in_specs = (
        [half_of_whole, head_spec(qg)]
        + [stat_spec(stat)]
        + [head_spec(a) for a in later[0]]
        + [half_of_whole if len(f) == 1 else head_spec(f[half]) for f in later[1:]]
        + [stat_spec(a) for a in later_stats]
    )
    out = jax.ShapeDtypeStruct((2, rows, width), BF16)
    groups = (len(later[0]),) + (1,) * len(far)
    (result,) = call(
        functools.partial(key_kernel, half, groups),
        where,
        operands,
        in_specs,
        [out],
        [head_spec(out)],
        heads,
        (4 + len(far)) * BLOCK,
        "key_side",
    )
    return result


def norm_kernel(series_ref, gain_ref, normed_ref, inv_ref):
    rows = series_ref[...].astype(F32)
    inv_rms = lax.rsqrt(jnp.mean(rows * rows, axis=-1, keepdims=True) + EPS)
    inv_ref[...] = inv_rms
    normed_ref[...] = (rows * inv_rms * gain_ref[...]).astype(BF16)


def normalize(series, gain):
    rows, width = series.shape
    step = rows // 2
    row_spec = pl.BlockSpec((step, width), lambda i: (i, 0))
    return pl.pallas_call(
        norm_kernel,
        out_shape=[
            jax.ShapeDtypeStruct((rows, width), BF16),
            jax.ShapeDtypeStruct((rows, 1), F32),
        ],
        grid=(2,),
        in_specs=[row_spec, pl.BlockSpec((1, width), lambda i: (0, 0))],
        out_specs=[row_spec, pl.BlockSpec((step, 1), lambda i: (i, 0))],
        compiler_params=pltpu.CompilerParams(vmem_limit_bytes=10 * 2**20),
        name="normalize",
    )(pltpu.with_memory_space_constraint(series, pltpu.HBM), gain[None])


def matmul(a, b):
    return jnp.dot(a, b, preferred_element_type=F32)


def matmul_t(a, b):
    return lax.dot_general(a, b, NT, preferred_element_type=F32)


def swapped(own, passed, bit, sign):
    size = lax.axis_size("seq")
    high = (lax.axis_index("seq") // bit) % 2 == 1
    sent = jnp.where(high, passed, own) if sign > 0 else jnp.where(high, own, passed)
    return lax.ppermute(sent, "seq", [(i, i ^ bit) for i in range(size)])


def exchange(rows, sign):
    two = shifted(rows, sign * 2)
    far = shifted(rows, sign * 32)
    four = shifted(two, sign * 2)
    eight = shifted(four, sign * 4)
    sixteen = swapped(rows, far, 16, sign)
    rows_last, two_last, eight = lax.optimization_barrier((rows, two, eight))
    one = swapped(rows_last, two_last, 1, sign)
    return [one, two, four, eight, sixteen, far, shifted(far, sign * 32)]


def exchange_stats(stat, attn_other):
    two, far = shifted(stat, -2), shifted(stat, -32)
    direct = [shifted(stat, -by) for by in (64, 8, 4)]
    sixteen = swapped(stat, far, 16, -1)
    two_last, attn_other = lax.optimization_barrier((two, attn_other))
    one = swapped(stat, two_last, 1, -1)
    return attn_other, [one, two, direct[2], direct[1], sixteen, far, direct[0]]


def per_device(series, norm_gain, w_query, w_key, w_value, w_out, out_grad):
    levels = lax.axis_size("seq").bit_length() - 1
    half = series.shape[0]
    blocks = 2 * half // BLOCK
    tp_index = lax.axis_index("tp").astype(jnp.int32)
    seq_index = lax.axis_index("seq").astype(jnp.int32)
    where = jnp.stack([tp_index, seq_index * blocks])
    series_f = series.astype(F32)
    normed, inv_rms = normalize(series, norm_gain)
    unit_rows = series_f * inv_rms
    normed_other, out_grad_other = lax.optimization_barrier((swap_tp(normed), swap_tp(out_grad)))

    def key_value(rows):
        return jnp.stack([matmul(rows, w_key).astype(BF16), matmul(rows, w_value).astype(BF16)])

    def query_grad(rows, grad_rows):
        return jnp.stack(
            [matmul(rows, w_query).astype(BF16), matmul_t(grad_rows, w_out).astype(BF16)]
        )

    kv = (key_value(normed), key_value(normed_other))
    qg = (query_grad(normed, out_grad), query_grad(normed_other, out_grad_other))
    kv_all, qg_all = lax.optimization_barrier(
        (jnp.concatenate(kv, axis=1), jnp.concatenate(qg, axis=1))
    )
    fetched = exchange(kv_all, 1)
    later = exchange(qg_all, -1)
    mixed, grad_query, stat = query_side(where, qg_all, kv_all, [(f,) for f in fetched], 0)
    stat, later = lax.optimization_barrier((stat, later))
    later = [(f,) for f in later]
    attn_other = swap_tp(matmul(mixed[half:], w_out).astype(BF16))
    attn_other, later_stats = exchange_stats(stat, attn_other)
    attn_rows = matmul(mixed[:half], w_out) + attn_other.astype(F32)
    layer_out = (series_f + attn_rows).astype(BF16)

    def back(at):
        grad_kv = key_side(at, where, kv_all, qg_all, stat, later, later_stats)
        rows = slice(at * half, (at + 1) * half)
        return (
            matmul_t(grad_query[rows], w_query)
            + matmul_t(grad_kv[0], w_key)
            + matmul_t(grad_kv[1], w_value)
        )

    normed_grad_other = swap_tp(back(1).astype(BF16))
    normed_grad = back(0) + normed_grad_other.astype(F32)
    scaled = normed_grad * norm_gain
    series_grad = out_grad.astype(F32) + inv_rms * (
        scaled - unit_rows * jnp.mean(scaled * unit_rows, axis=-1, keepdims=True)
    )
    return (layer_out, series_grad.astype(BF16))


def solution(mesh):
    rows = P(("seq", "tp"), None)
    columns = P(None, "tp")
    in_specs = (rows, P(), columns, columns, columns, P("tp", None), rows)
    return jax.shard_map(
        per_device, mesh=mesh, in_specs=in_specs, out_specs=(rows, rows), check_vma=False
    )
```

```python
import functools

import jax
import jax.numpy as jnp
from jax import lax
from jax.experimental import pallas as pl
from jax.experimental.pallas import tpu as pltpu
from jax.sharding import PartitionSpec as P

HD = 128
BLOCK = 64
NEG = -1e30
EPS = 1e-06
F32 = jnp.float32
BF16 = jnp.bfloat16
NN = (((1,), (0,)), ((), ()))
NT = (((1,), (1,)), ((), ()))
TN = (((0,), (0,)), ((), ()))
NEAR = (1, 2, 4)
GROUP = 2


def shifted(value, by):
    size = lax.axis_size("seq")
    pairs = [(i, i + by) for i in range(size) if 0 <= i + by < size]
    return lax.ppermute(value, "seq", pairs)


def swap_tp(value):
    return lax.ppermute(value, "tp", [(0, 1), (1, 0)])


def dot(a, b, dims):
    return lax.dot_general(a, b, dims, preferred_element_type=F32)


def piece(pieces, which, slot):
    per = 4 // len(pieces)
    at = (slot % per) * BLOCK
    return pieces[slot // per][which, at : at + BLOCK, :]


def near_slots(step, slot):
    found = []
    for turn in (0, 2):
        block = (slot + turn) % 4 + step
        found.append((0 <= block < 4, (block + turn) % 4))
    return found


def near(is_second, own, other, which, slot, step):
    options = [
        piece(own if here else other, which, at) for here, at in near_slots(step, slot)
    ]
    return jnp.where(is_second, options[1], options[0])


def causal_bias(query_axis):
    rows = lax.broadcasted_iota(jnp.int32, (BLOCK, BLOCK), query_axis)
    keys = lax.broadcasted_iota(jnp.int32, (BLOCK, BLOCK), 1 - query_axis)
    return jnp.where(rows >= keys, 0.0, NEG).astype(F32)


def query_kernel(groups, n_back, where_ref, *refs):
    refs = list(refs)
    qg, kv = [refs.pop(0)], [refs.pop(0)]
    fetched = [[refs.pop(0) for _ in range(n)] for n in groups]
    mixed_ref, dq_ref, stat_ref, *back_refs = refs
    is_second = where_ref[0] == 1
    factor = HD ** (-0.5)
    causal = causal_bias(0)
    lane = lax.broadcasted_iota(jnp.int32, (BLOCK, HD), 1)
    slots = range(4)

    def gather(which, slot):
        return jnp.concatenate(
            [piece(kv, which, slot)]
            + [near(is_second, kv, fetched[0], which, slot, -d) for d in NEAR]
            + [piece(f, which, slot) for f in fetched[1:]],
            axis=0,
        )

    def rows(slot):
        return slice(slot * BLOCK, (slot + 1) * BLOCK)

    part = lax.broadcasted_iota(jnp.int32, (1, (4 + len(groups) - 1) * BLOCK), 1) // BLOCK
    reach = jnp.where(part == 0, 0, jnp.left_shift(1, jnp.maximum(part - 1, 0)))
    query = [piece(qg, 0, slot) for slot in slots]
    grad = [piece(qg, 1, slot) for slot in slots]
    keys = [gather(0, slot) for slot in slots]
    values = [gather(1, slot) for slot in slots]
    score = []
    for slot in slots:
        block = where_ref[1] + (slot + 2 * where_ref[0]) % 4
        s = dot(query[slot], keys[slot], NT) * factor + jnp.where(reach <= block, 0.0, NEG)
        score.append(jnp.concatenate([s[:, :BLOCK] + causal, s[:, BLOCK:]], axis=1))
    grad_prob = [dot(grad[slot], values[slot], NT) for slot in slots]
    peak = [jnp.max(s, axis=-1, keepdims=True) for s in score]
    weight = [jnp.exp(score[slot] - peak[slot]) for slot in slots]
    total = [jnp.sum(w, axis=-1, keepdims=True) for w in weight]
    prob = [weight[slot] * (1.0 / total[slot]) for slot in slots]
    prob_b = [p.astype(BF16) for p in prob]
    mixed = [dot(prob_b[slot], values[slot], NN).astype(BF16) for slot in slots]
    inner = [
        jnp.sum(mixed[slot].astype(F32) * grad[slot].astype(F32), axis=-1, keepdims=True)
        for slot in slots
    ]
    grad_score = [
        (prob[slot] * (grad_prob[slot] - inner[slot])).astype(BF16) for slot in slots
    ]
    first = keys[0].shape[0] - n_back * BLOCK
    for slot in slots:
        out = rows(slot)
        mixed_ref[out, :] = mixed[slot]
        dq_ref[out, :] = (dot(grad_score[slot], keys[slot], NN) * factor).astype(BF16)
        stat = jnp.where(lane == 0, peak[slot] + jnp.log(total[slot]), inner[slot])
        stat_ref[0, :, out] = jnp.transpose(stat)[:2]
        if n_back:
            grad_keys = (dot(grad_score[slot][:, first:], query[slot], TN) * factor).astype(BF16)
            grad_values = dot(prob_b[slot][:, first:], grad[slot], TN).astype(BF16)
            for at, ref in enumerate(back_refs):
                ref[0, out, :] = grad_keys[at * BLOCK : (at + 1) * BLOCK]
                ref[1, out, :] = grad_values[at * BLOCK : (at + 1) * BLOCK]


def key_kernel(half, groups, where_ref, *refs):
    refs = list(refs)
    kv = refs.pop(0)
    qg = [refs.pop(0)]
    stat = refs.pop(0)
    later = [[refs.pop(0) for _ in range(n)] for n in groups]
    later_stats = [refs.pop(0) for _ in groups]
    (out_ref,) = refs
    is_second = where_ref[0] == 1
    factor = HD ** (-0.5)
    causal = causal_bias(1)

    def stat_of(ref, slot):
        return ref[0, :, slot * BLOCK : (slot + 1) * BLOCK]

    def gather(which, at):
        rows = slice(at * BLOCK, (at + 1) * BLOCK)
        return jnp.concatenate(
            [piece(qg, which, 2 * half + at)]
            + [near(is_second, qg, later[0], which, 2 * half + at, d) for d in NEAR]
            + [f[0][which, rows, :] for f in later[1:]],
            axis=0,
        )

    def gather_stats(slot):
        parts = [stat_of(stat, slot)]
        for d in NEAR:
            options = [
                stat_of(stat if here else later_stats[0], s) for here, s in near_slots(d, slot)
            ]
            parts.append(jnp.where(is_second, options[1], options[0]))
        return jnp.concatenate(parts + [stat_of(f, slot) for f in later_stats[1:]], axis=1)

    both = range(2)
    rows = [slice(at * BLOCK, (at + 1) * BLOCK) for at in both]
    queries = [gather(0, at) for at in both]
    grads = [gather(1, at) for at in both]
    stats = [gather_stats(2 * half + at) for at in both]
    score = [dot(kv[0, rows[at], :], queries[at], NT) * factor for at in both]
    grad_prob = [dot(kv[1, rows[at], :], grads[at], NT) for at in both]
    score = [jnp.concatenate([s[:, :BLOCK] + causal, s[:, BLOCK:]], axis=1) for s in score]
    prob = [jnp.exp(score[at] - stats[at][0:1]) for at in both]
    grad_score = [(prob[at] * (grad_prob[at] - stats[at][1:2])).astype(BF16) for at in both]
    prob_b = [p.astype(BF16) for p in prob]
    grad_keys = [dot(grad_score[at], queries[at], NN) * factor for at in both]
    grad_values = [dot(prob_b[at], grads[at], NN) for at in both]
    for at in both:
        out_ref[0, rows[at], :] = grad_keys[at].astype(BF16)
        out_ref[1, rows[at], :] = grad_values[at].astype(BF16)


def head_spec(a):
    if len(a.shape) == 2:
        return pl.BlockSpec((a.shape[0], GROUP * HD), lambda h, w: (0, h))
    return pl.BlockSpec((a.shape[0], a.shape[1], GROUP * HD), lambda h, w: (0, 0, h))


def stat_spec(a):
    return pl.BlockSpec((GROUP,) + a.shape[1:], lambda h, w: (h, 0, 0))


def each_head(kernel):
    def run(where_ref, *refs):
        for head in range(GROUP):
            columns = slice(head * HD, (head + 1) * HD)
            kernel(
                where_ref,
                *[
                    r.at[head : head + 1] if r.dtype == F32
                    else r.at[..., columns]
                    for r in refs
                ],
            )

    return run


def call(kernel, where, operands, in_specs, outs, out_specs, heads, keys, name):
    rows = outs[0].shape[-2]
    return pl.pallas_call(
        each_head(kernel),
        out_shape=outs,
        grid_spec=pltpu.PrefetchScalarGridSpec(
            num_scalar_prefetch=1, grid=(heads // GROUP,), in_specs=in_specs, out_specs=out_specs
        ),
        compiler_params=pltpu.CompilerParams(vmem_limit_bytes=14 * 2**20),
        cost_estimate=pl.CostEstimate(
            flops=rows * keys, bytes_accessed=2**16, transcendentals=0
        ),
        name=name,
    )(where, *operands)


def query_side(where, qg, kv, fetched, n_back):
    rows, width = qg.shape[1], qg.shape[2]
    heads = width // HD
    far = [a for f in fetched for a in f]
    operands = [qg, kv, *far]
    row_out = jax.ShapeDtypeStruct((rows, width), BF16)
    stat_out = jax.ShapeDtypeStruct((heads, 2, rows), F32)
    back_out = jax.ShapeDtypeStruct((2, rows, width), BF16)
    outs = [row_out, pltpu.HBM(row_out.shape, BF16), stat_out] + [back_out] * n_back
    return call(
        functools.partial(query_kernel, tuple(len(f) for f in fetched), n_back),
        where,
        operands,
        [head_spec(a) for a in operands],
        outs,
        [head_spec(row_out), head_spec(row_out), stat_spec(stat_out)] + [head_spec(back_out)] * n_back,
        heads,
        (3 + len(fetched)) * BLOCK,
        "query_side",
    )


def key_side(half, where, kv, qg, stat, later, later_stats):
    rows, width = kv.shape[1] // 2, kv.shape[2]
    heads = width // HD
    half_of_whole = pl.BlockSpec((2, rows, GROUP * HD), lambda h, w: (0, half, h))
    far = [f[-1] if len(f) == 1 else f[half] for f in later[1:]]
    first, *far = [pltpu.with_memory_space_constraint(a, pltpu.HBM) for a in (*later[0], *far)]
    operands = [kv, qg, stat, first, *far, *later_stats]
    in_specs = (
        [half_of_whole, head_spec(qg)]
        + [stat_spec(stat)]
        + [head_spec(a) for a in later[0]]
        + [half_of_whole if len(f) == 1 else head_spec(f[half]) for f in later[1:]]
        + [stat_spec(a) for a in later_stats]
    )
    out = jax.ShapeDtypeStruct((2, rows, width), BF16)
    groups = (len(later[0]),) + (1,) * len(far)
    (result,) = call(
        functools.partial(key_kernel, half, groups),
        where,
        operands,
        in_specs,
        [out],
        [head_spec(out)],
        heads,
        (4 + len(far)) * BLOCK,
        "key_side",
    )
    return result


def norm_kernel(series_ref, gain_ref, normed_ref, inv_ref):
    rows = series_ref[...].astype(F32)
    inv_rms = lax.rsqrt(jnp.mean(rows * rows, axis=-1, keepdims=True) + EPS)
    inv_ref[...] = inv_rms
    normed_ref[...] = (rows * inv_rms * gain_ref[...]).astype(BF16)


def normalize(series, gain):
    rows, width = series.shape
    step = rows // 2
    row_spec = pl.BlockSpec((step, width), lambda i: (i, 0))
    return pl.pallas_call(
        norm_kernel,
        out_shape=[
            jax.ShapeDtypeStruct((rows, width), BF16),
            jax.ShapeDtypeStruct((rows, 1), F32),
        ],
        grid=(2,),
        in_specs=[row_spec, pl.BlockSpec((1, width), lambda i: (0, 0))],
        out_specs=[row_spec, pl.BlockSpec((step, 1), lambda i: (i, 0))],
        compiler_params=pltpu.CompilerParams(vmem_limit_bytes=10 * 2**20),
        name="normalize",
    )(pltpu.with_memory_space_constraint(series, pltpu.HBM), gain[None])


def matmul(a, b):
    return jnp.dot(a, b, preferred_element_type=F32)


def matmul_t(a, b):
    return lax.dot_general(a, b, NT, preferred_element_type=F32)


def swapped(own, passed, bit, sign):
    size = lax.axis_size("seq")
    high = (lax.axis_index("seq") // bit) % 2 == 1
    sent = jnp.where(high, passed, own) if sign > 0 else jnp.where(high, own, passed)
    return lax.ppermute(sent, "seq", [(i, i ^ bit) for i in range(size)])


def exchange(keys, queries):
    two, two_q = shifted(keys, 2), shifted(queries, -2)
    far, far_q = shifted(keys, 32), shifted(queries, -32)
    two, far = lax.optimization_barrier((two, far))
    two_q, far_q = lax.optimization_barrier((two_q, far_q))
    four, four_q = shifted(two, 2), shifted(two_q, -2)
    one, sixteen = swapped(keys, two, 1, 1), swapped(keys, far, 16, 1)
    one_q, sixteen_q = swapped(queries, two_q, 1, -1), swapped(queries, far_q, 16, -1)
    last = shifted(far, 32)
    four, one = lax.optimization_barrier((four, one))
    four_q, one_q, last = lax.optimization_barrier((four_q, one_q, last))
    eight, eight_q = shifted(four, 4), shifted(four_q, -4)
    return (
        [one, two, four, eight, sixteen, far, last],
        [one_q, two_q, four_q, eight_q, sixteen_q, far_q, shifted(far_q, -32)],
    )


def exchange_stats(stat, attn_other):
    two, far = shifted(stat, -2), shifted(stat, -32)
    direct = [shifted(stat, -by) for by in (64, 8, 4)]
    sixteen = swapped(stat, far, 16, -1)
    two_last, attn_other = lax.optimization_barrier((two, attn_other))
    one = swapped(stat, two_last, 1, -1)
    return attn_other, [one, two, direct[2], direct[1], sixteen, far, direct[0]]


def per_device(series, norm_gain, w_query, w_key, w_value, w_out, out_grad):
    levels = lax.axis_size("seq").bit_length() - 1
    half = series.shape[0]
    blocks = 2 * half // BLOCK
    tp_index = lax.axis_index("tp").astype(jnp.int32)
    seq_index = lax.axis_index("seq").astype(jnp.int32)
    where = jnp.stack([tp_index, seq_index * blocks])
    series_f = series.astype(F32)
    normed, inv_rms = normalize(series, norm_gain)
    unit_rows = series_f * inv_rms
    normed_other, out_grad_other = lax.optimization_barrier((swap_tp(normed), swap_tp(out_grad)))

    def key_value(rows):
        return jnp.stack([matmul(rows, w_key).astype(BF16), matmul(rows, w_value).astype(BF16)])

    def query_grad(rows, grad_rows):
        return jnp.stack(
            [matmul(rows, w_query).astype(BF16), matmul_t(grad_rows, w_out).astype(BF16)]
        )

    kv = (key_value(normed), key_value(normed_other))
    qg = (query_grad(normed, out_grad), query_grad(normed_other, out_grad_other))
    kv_all, qg_all = lax.optimization_barrier(
        (jnp.concatenate(kv, axis=1), jnp.concatenate(qg, axis=1))
    )
    fetched, later = exchange(kv_all, qg_all)
    mixed, grad_query, stat = query_side(where, qg_all, kv_all, [(f,) for f in fetched], 0)
    stat, later = lax.optimization_barrier((stat, later))
    later = [(f,) for f in later]
    attn_other = swap_tp(matmul(mixed[half:], w_out).astype(BF16))
    attn_other, later_stats = exchange_stats(stat, attn_other)
    def back(at):
        grad_kv = key_side(at, where, kv_all, qg_all, stat, later, later_stats)
        rows = slice(at * half, (at + 1) * half)
        return (
            matmul_t(grad_query[rows], w_query)
            + matmul_t(grad_kv[0], w_key)
            + matmul_t(grad_kv[1], w_value)
        )

    partial, attn_other = lax.optimization_barrier((back(1).astype(BF16), attn_other))
    normed_grad_other = swap_tp(partial)
    attn_rows = matmul(mixed[:half], w_out) + attn_other.astype(F32)
    layer_out = (series_f + attn_rows).astype(BF16)
    normed_grad = back(0) + normed_grad_other.astype(F32)
    scaled = normed_grad * norm_gain
    series_grad = out_grad.astype(F32) + inv_rms * (
        scaled - unit_rows * jnp.mean(scaled * unit_rows, axis=-1, keepdims=True)
    )
    return (layer_out, series_grad.astype(BF16))


def solution(mesh):
    rows = P(("seq", "tp"), None)
    columns = P(None, "tp")
    in_specs = (rows, P(), columns, columns, columns, P("tp", None), rows)
    return jax.shard_map(
        per_device, mesh=mesh, in_specs=in_specs, out_specs=(rows, rows), check_vma=False
    )
```

```python
import functools

import jax
import jax.numpy as jnp
from jax import lax
from jax.experimental import pallas as pl
from jax.experimental.pallas import tpu as pltpu
from jax.sharding import PartitionSpec as P

HD = 128
BLOCK = 64
NEG = -1e30
EPS = 1e-06
F32 = jnp.float32
BF16 = jnp.bfloat16
NN = (((1,), (0,)), ((), ()))
NT = (((1,), (1,)), ((), ()))
TN = (((0,), (0,)), ((), ()))
NEAR = (1, 2, 4)
GROUP = 2


def shifted(value, by):
    size = lax.axis_size("seq")
    pairs = [(i, i + by) for i in range(size) if 0 <= i + by < size]
    return lax.ppermute(value, "seq", pairs)


def swap_tp(value):
    return lax.ppermute(value, "tp", [(0, 1), (1, 0)])


def dot(a, b, dims):
    return lax.dot_general(a, b, dims, preferred_element_type=F32)


def piece(pieces, which, slot):
    per = 4 // len(pieces)
    at = (slot % per) * BLOCK
    return pieces[slot // per][which, at : at + BLOCK, :]


def near_slots(step, slot):
    found = []
    for turn in (0, 2):
        block = (slot + turn) % 4 + step
        found.append((0 <= block < 4, (block + turn) % 4))
    return found


def near(is_second, own, other, which, slot, step):
    options = [
        piece(own if here else other, which, at) for here, at in near_slots(step, slot)
    ]
    return jnp.where(is_second, options[1], options[0])


def causal_bias(query_axis):
    rows = lax.broadcasted_iota(jnp.int32, (BLOCK, BLOCK), query_axis)
    keys = lax.broadcasted_iota(jnp.int32, (BLOCK, BLOCK), 1 - query_axis)
    return jnp.where(rows >= keys, 0.0, NEG).astype(F32)


def query_kernel(groups, n_back, where_ref, *refs):
    refs = list(refs)
    qg, kv = [refs.pop(0)], [refs.pop(0)]
    fetched = [[refs.pop(0) for _ in range(n)] for n in groups]
    mixed_ref, dq_ref, stat_ref, *back_refs = refs
    is_second = where_ref[0] == 1
    factor = HD ** (-0.5)
    causal = causal_bias(0)
    lane = lax.broadcasted_iota(jnp.int32, (BLOCK, HD), 1)
    slots = range(4)

    def gather(which, slot):
        return jnp.concatenate(
            [piece(kv, which, slot)]
            + [near(is_second, kv, fetched[0], which, slot, -d) for d in NEAR]
            + [piece(f, which, slot) for f in fetched[1:]],
            axis=0,
        )

    def rows(slot):
        return slice(slot * BLOCK, (slot + 1) * BLOCK)

    part = lax.broadcasted_iota(jnp.int32, (1, (4 + len(groups) - 1) * BLOCK), 1) // BLOCK
    reach = jnp.where(part == 0, 0, jnp.left_shift(1, jnp.maximum(part - 1, 0)))
    query = [piece(qg, 0, slot) for slot in slots]
    grad = [piece(qg, 1, slot) for slot in slots]
    keys = [gather(0, slot) for slot in slots]
    values = [gather(1, slot) for slot in slots]
    score = []
    for slot in slots:
        block = where_ref[1] + (slot + 2 * where_ref[0]) % 4
        s = dot(query[slot], keys[slot], NT) * factor + jnp.where(reach <= block, 0.0, NEG)
        score.append(jnp.concatenate([s[:, :BLOCK] + causal, s[:, BLOCK:]], axis=1))
    grad_prob = [dot(grad[slot], values[slot], NT) for slot in slots]
    peak = [jnp.max(s, axis=-1, keepdims=True) for s in score]
    weight = [jnp.exp(score[slot] - peak[slot]) for slot in slots]
    total = [jnp.sum(w, axis=-1, keepdims=True) for w in weight]
    prob = [weight[slot] * (1.0 / total[slot]) for slot in slots]
    prob_b = [p.astype(BF16) for p in prob]
    mixed = [dot(prob_b[slot], values[slot], NN).astype(BF16) for slot in slots]
    inner = [
        jnp.sum(mixed[slot].astype(F32) * grad[slot].astype(F32), axis=-1, keepdims=True)
        for slot in slots
    ]
    grad_score = [
        (prob[slot] * (grad_prob[slot] - inner[slot])).astype(BF16) for slot in slots
    ]
    first = keys[0].shape[0] - n_back * BLOCK
    for slot in slots:
        out = rows(slot)
        mixed_ref[out, :] = mixed[slot]
        dq_ref[out, :] = (dot(grad_score[slot], keys[slot], NN) * factor).astype(BF16)
        stat = jnp.where(lane == 0, peak[slot] + jnp.log(total[slot]), inner[slot])
        stat_ref[0, :, out] = jnp.transpose(stat)[:2]
        if n_back:
            grad_keys = (dot(grad_score[slot][:, first:], query[slot], TN) * factor).astype(BF16)
            grad_values = dot(prob_b[slot][:, first:], grad[slot], TN).astype(BF16)
            for at, ref in enumerate(back_refs):
                ref[0, out, :] = grad_keys[at * BLOCK : (at + 1) * BLOCK]
                ref[1, out, :] = grad_values[at * BLOCK : (at + 1) * BLOCK]


def key_kernel(half, groups, where_ref, *refs):
    refs = list(refs)
    kv = refs.pop(0)
    qg = [refs.pop(0)]
    stat = refs.pop(0)
    later = [[refs.pop(0) for _ in range(n)] for n in groups]
    later_stats = [refs.pop(0) for _ in groups]
    (out_ref,) = refs
    is_second = where_ref[0] == 1
    factor = HD ** (-0.5)
    causal = causal_bias(1)

    def stat_of(ref, slot):
        return ref[0, :, slot * BLOCK : (slot + 1) * BLOCK]

    def gather(which, at):
        rows = slice(at * BLOCK, (at + 1) * BLOCK)
        return jnp.concatenate(
            [piece(qg, which, 2 * half + at)]
            + [near(is_second, qg, later[0], which, 2 * half + at, d) for d in NEAR]
            + [f[0][which, rows, :] for f in later[1:]],
            axis=0,
        )

    def gather_stats(slot):
        parts = [stat_of(stat, slot)]
        for d in NEAR:
            options = [
                stat_of(stat if here else later_stats[0], s) for here, s in near_slots(d, slot)
            ]
            parts.append(jnp.where(is_second, options[1], options[0]))
        return jnp.concatenate(parts + [stat_of(f, slot) for f in later_stats[1:]], axis=1)

    both = range(2)
    rows = [slice(at * BLOCK, (at + 1) * BLOCK) for at in both]
    queries = [gather(0, at) for at in both]
    grads = [gather(1, at) for at in both]
    stats = [gather_stats(2 * half + at) for at in both]
    score = [dot(kv[0, rows[at], :], queries[at], NT) * factor for at in both]
    grad_prob = [dot(kv[1, rows[at], :], grads[at], NT) for at in both]
    score = [jnp.concatenate([s[:, :BLOCK] + causal, s[:, BLOCK:]], axis=1) for s in score]
    prob = [jnp.exp(score[at] - stats[at][0:1]) for at in both]
    grad_score = [(prob[at] * (grad_prob[at] - stats[at][1:2])).astype(BF16) for at in both]
    prob_b = [p.astype(BF16) for p in prob]
    grad_keys = [dot(grad_score[at], queries[at], NN) * factor for at in both]
    grad_values = [dot(prob_b[at], grads[at], NN) for at in both]
    for at in both:
        out_ref[0, rows[at], :] = grad_keys[at].astype(BF16)
        out_ref[1, rows[at], :] = grad_values[at].astype(BF16)


def head_spec(a):
    if len(a.shape) == 2:
        return pl.BlockSpec((a.shape[0], GROUP * HD), lambda h, w: (0, h))
    return pl.BlockSpec((a.shape[0], a.shape[1], GROUP * HD), lambda h, w: (0, 0, h))


def stat_spec(a):
    return pl.BlockSpec((GROUP,) + a.shape[1:], lambda h, w: (h, 0, 0))


def each_head(kernel):
    def run(where_ref, *refs):
        for head in range(GROUP):
            columns = slice(head * HD, (head + 1) * HD)
            kernel(
                where_ref,
                *[
                    r.at[head : head + 1] if r.dtype == F32
                    else r.at[..., columns]
                    for r in refs
                ],
            )

    return run


def call(kernel, where, operands, in_specs, outs, out_specs, heads, keys, name):
    rows = outs[0].shape[-2]
    return pl.pallas_call(
        each_head(kernel),
        out_shape=outs,
        grid_spec=pltpu.PrefetchScalarGridSpec(
            num_scalar_prefetch=1, grid=(heads // GROUP,), in_specs=in_specs, out_specs=out_specs
        ),
        compiler_params=pltpu.CompilerParams(vmem_limit_bytes=14 * 2**20),
        cost_estimate=pl.CostEstimate(
            flops=rows * keys, bytes_accessed=2**16, transcendentals=0
        ),
        name=name,
    )(where, *operands)


def query_side(where, qg, kv, fetched, n_back):
    rows, width = qg.shape[1], qg.shape[2]
    heads = width // HD
    far = [a for f in fetched for a in f]
    operands = [qg, kv, *far]
    row_out = jax.ShapeDtypeStruct((rows, width), BF16)
    stat_out = jax.ShapeDtypeStruct((heads, 2, rows), F32)
    back_out = jax.ShapeDtypeStruct((2, rows, width), BF16)
    outs = [row_out, pltpu.HBM(row_out.shape, BF16), stat_out] + [back_out] * n_back
    return call(
        functools.partial(query_kernel, tuple(len(f) for f in fetched), n_back),
        where,
        operands,
        [head_spec(a) for a in operands],
        outs,
        [head_spec(row_out), head_spec(row_out), stat_spec(stat_out)] + [head_spec(back_out)] * n_back,
        heads,
        (3 + len(fetched)) * BLOCK,
        "query_side",
    )


def key_side(half, where, kv, qg, stat, later, later_stats):
    rows, width = kv.shape[1] // 2, kv.shape[2]
    heads = width // HD
    half_of_whole = pl.BlockSpec((2, rows, GROUP * HD), lambda h, w: (0, half, h))
    far = [f[-1] if len(f) == 1 else f[half] for f in later[1:]]
    first, *far = [pltpu.with_memory_space_constraint(a, pltpu.HBM) for a in (*later[0], *far)]
    operands = [kv, qg, stat, first, *far, *later_stats]
    in_specs = (
        [half_of_whole, head_spec(qg)]
        + [stat_spec(stat)]
        + [head_spec(a) for a in later[0]]
        + [half_of_whole if len(f) == 1 else head_spec(f[half]) for f in later[1:]]
        + [stat_spec(a) for a in later_stats]
    )
    out = jax.ShapeDtypeStruct((2, rows, width), BF16)
    groups = (len(later[0]),) + (1,) * len(far)
    (result,) = call(
        functools.partial(key_kernel, half, groups),
        where,
        operands,
        in_specs,
        [out],
        [head_spec(out)],
        heads,
        (4 + len(far)) * BLOCK,
        "key_side",
    )
    return result


def norm_kernel(series_ref, gain_ref, normed_ref, inv_ref):
    rows = series_ref[...].astype(F32)
    inv_rms = lax.rsqrt(jnp.mean(rows * rows, axis=-1, keepdims=True) + EPS)
    inv_ref[...] = inv_rms
    normed_ref[...] = (rows * inv_rms * gain_ref[...]).astype(BF16)


def normalize(series, gain):
    rows, width = series.shape
    step = rows // 2
    row_spec = pl.BlockSpec((step, width), lambda i: (i, 0))
    return pl.pallas_call(
        norm_kernel,
        out_shape=[
            jax.ShapeDtypeStruct((rows, width), BF16),
            jax.ShapeDtypeStruct((rows, 1), F32),
        ],
        grid=(2,),
        in_specs=[row_spec, pl.BlockSpec((1, width), lambda i: (0, 0))],
        out_specs=[row_spec, pl.BlockSpec((step, 1), lambda i: (i, 0))],
        compiler_params=pltpu.CompilerParams(vmem_limit_bytes=10 * 2**20),
        name="normalize",
    )(pltpu.with_memory_space_constraint(series, pltpu.HBM), gain[None])


def matmul(a, b):
    return jnp.dot(a, b, preferred_element_type=F32)


def matmul_t(a, b):
    return lax.dot_general(a, b, NT, preferred_element_type=F32)


def swapped(own, passed, bit, sign):
    size = lax.axis_size("seq")
    high = (lax.axis_index("seq") // bit) % 2 == 1
    sent = jnp.where(high, passed, own) if sign > 0 else jnp.where(high, own, passed)
    return lax.ppermute(sent, "seq", [(i, i ^ bit) for i in range(size)])


def exchange(keys, keys_other, queries):
    two, two_q = shifted(keys, 2), shifted(queries, -2)
    far, far_q = shifted(keys, 32), shifted(queries, -32)
    two, far = lax.optimization_barrier((two, far))
    two_q, far_q = lax.optimization_barrier((two_q, far_q))
    four, four_q = shifted(two, 2), shifted(two_q, -2)
    eight_other = shifted(keys_other, 8)
    one, sixteen = swapped(keys, two, 1, 1), swapped(keys, far, 16, 1)
    one_q, sixteen_q = swapped(queries, two_q, 1, -1), swapped(queries, far_q, 16, -1)
    last = shifted(far, 32)
    four, one, eight_other = lax.optimization_barrier((four, one, eight_other))
    four_q, one_q, last = lax.optimization_barrier((four_q, one_q, last))
    eight_own, eight_q = shifted(four[:, : four.shape[1] // 2], 4), shifted(four_q, -4)
    whole = [(one,), (two,), (four,), (sixteen,), (far,), (last,)]
    return (
        whole[:3] + [(eight_own, eight_other)] + whole[3:],
        [one_q, two_q, four_q, eight_q, sixteen_q, far_q, shifted(far_q, -32)],
    )


def exchange_stats(stat, attn_other):
    two, far = shifted(stat, -2), shifted(stat, -32)
    direct = [shifted(stat, -by) for by in (64, 8, 4)]
    sixteen = swapped(stat, far, 16, -1)
    two_last, attn_other = lax.optimization_barrier((two, attn_other))
    one = swapped(stat, two_last, 1, -1)
    return attn_other, [one, two, direct[2], direct[1], sixteen, far, direct[0]]


def per_device(series, norm_gain, w_query, w_key, w_value, w_out, out_grad):
    levels = lax.axis_size("seq").bit_length() - 1
    half = series.shape[0]
    blocks = 2 * half // BLOCK
    tp_index = lax.axis_index("tp").astype(jnp.int32)
    seq_index = lax.axis_index("seq").astype(jnp.int32)
    where = jnp.stack([tp_index, seq_index * blocks])
    series_f = series.astype(F32)
    normed, inv_rms = normalize(series, norm_gain)
    unit_rows = series_f * inv_rms
    normed_other, out_grad_other = lax.optimization_barrier((swap_tp(normed), swap_tp(out_grad)))

    def key_value(rows):
        return jnp.stack([matmul(rows, w_key).astype(BF16), matmul(rows, w_value).astype(BF16)])

    def query_grad(rows, grad_rows):
        return jnp.stack(
            [matmul(rows, w_query).astype(BF16), matmul_t(grad_rows, w_out).astype(BF16)]
        )

    kv = (key_value(normed), key_value(normed_other))
    qg = (query_grad(normed, out_grad), query_grad(normed_other, out_grad_other))
    kv_all, qg_all = lax.optimization_barrier(
        (jnp.concatenate(kv, axis=1), jnp.concatenate(qg, axis=1))
    )
    fetched, later = exchange(kv_all, kv[1], qg_all)
    mixed, grad_query, stat = query_side(where, qg_all, kv_all, fetched, 0)
    stat, later = lax.optimization_barrier((stat, later))
    later = [(f,) for f in later]
    attn_other = swap_tp(matmul(mixed[half:], w_out).astype(BF16))
    attn_other, later_stats = exchange_stats(stat, attn_other)
    def back(at):
        grad_kv = key_side(at, where, kv_all, qg_all, stat, later, later_stats)
        rows = slice(at * half, (at + 1) * half)
        return (
            matmul_t(grad_query[rows], w_query)
            + matmul_t(grad_kv[0], w_key)
            + matmul_t(grad_kv[1], w_value)
        )

    partial, attn_other = lax.optimization_barrier((back(1).astype(BF16), attn_other))
    normed_grad_other = swap_tp(partial)
    attn_rows = matmul(mixed[:half], w_out) + attn_other.astype(F32)
    layer_out = (series_f + attn_rows).astype(BF16)
    normed_grad = back(0) + normed_grad_other.astype(F32)
    scaled = normed_grad * norm_gain
    series_grad = out_grad.astype(F32) + inv_rms * (
        scaled - unit_rows * jnp.mean(scaled * unit_rows, axis=-1, keepdims=True)
    )
    return (layer_out, series_grad.astype(BF16))


def solution(mesh):
    rows = P(("seq", "tp"), None)
    columns = P(None, "tp")
    in_specs = (rows, P(), columns, columns, columns, P("tp", None), rows)
    return jax.shard_map(
        per_device, mesh=mesh, in_specs=in_specs, out_specs=(rows, rows), check_vma=False
    )
```
